32 devices in a mesh: grp: 2 (over y), tm: 16 (over z, x, core).
Axes of the slice: x: 2, y: 2, z: 4, core: 2. Of those that a mesh axis runs over, the one named last changes fastest.
Arguments:
- frames: bfloat16 [24576, 1536], P('tm'), may hold values from -6 to 6
- ln_gain: float32 [1536], replicated, may hold values from 0.5 to 1.5
- w_value: bfloat16 [1536, 1536], P(None, 'grp'), may hold values from -0.15625 to 0.15625
- w_gate: bfloat16 [1536, 1536], P(None, 'grp'), may hold values from -0.15625 to 0.15625
- conv_taps: float32 [31, 1536], P(None, 'grp'), may hold values from -1 to 1
- bn_scale: float32 [1536], P('grp'), may hold values from 0.25 to 1.75
- bn_shift: float32 [1536], P('grp'), may hold values from -3 to 3
- w_out: bfloat16 [1536, 1536], replicated, may hold values from -0.15625 to 0.15625
- w_classes: bfloat16 [1536, 512], replicated, may hold values from -0.15625 to 0.15625
- seg_lengths: int32 [16, 128], P('tm'), may hold values from 1 to 24, 1536 in all within a row
- owners: int32 [2048, 1], P('tm'), may hold values from 0 to 15; in each aligned block of 128 rows (0 to 127, 128 to 255, ...) at most 8 rows name the same one
- silence: int32 [16, 128], P('tm'), may hold values from 0 to 1
- tags: int32 [16, 128], P('tm'), may hold values from 0 to 255
Outputs:
- block_out: bfloat16 [16, 2, 768, 1536], P('tm', 'grp')
- scores: float32 [2048, 512], P('tm', 'grp')
The draws below stay inside these ranges and needn't reach their ends.
Inputs may be any that keep to these rules, and one draw needn't show every extreme that they name: `owners`: among the segments of one shard no owner is named by more than 8. `seg_lengths`: the lengths of one shard sum to 1536.
All inputs are finite; a program needn't handle non-finite values.
Results may differ from the reference program's by a relative error of at most 0.0085.
Values may be sent and summed in bfloat16 or wider, within the bound.
No kernel may reach another device: no remote copies, remote signals or barrier semaphores. Data moves between devices by JAX's collectives and lax.ppermute only.
A program may use at most 64 MiB of HBM per device.

```python
import math
import jax
import jax.numpy as jnp
import numpy as np
from jax import lax

D = 1536
CLASSES = 512
KERNEL = 31
TAGS = 256
CAP = 8
FR_DEV = 1536
SEG_DEV = 128
MAXLEN = 24
FRAMES = 24576
SEGMENTS = 2048
SLOTS = 128
N_GRP = 2
N_TM = 16


def draw_silence(key, part):
    shard_rows = jnp.arange(N_TM, dtype=jnp.int32)[:, None]
    values = jax.random.randint(key, (N_TM, SEG_DEV), 0, 6 * N_TM)
    return (values < N_TM + 2 * shard_rows).astype(jnp.int32)


def with_ends(entries, stream_key, least, top_value):
    place = [jax.random.randint(jax.random.fold_in(stream_key, axis), (), 0, length) for axis, length in enumerate(entries.shape)]
    widest = entries.shape.index(max(entries.shape))
    next_to = place[:widest] + [(place[widest] + 1) % entries.shape[widest]] + place[widest + 1:]
    return entries.at[tuple(place)].set(least).at[tuple(next_to)].set(top_value)


def block_levels(own_key, dims, split, smallest, largest):
    loudness = 1.0
    for dim, parts in split:
        draws = jax.random.uniform(jax.random.fold_in(jax.random.fold_in(own_key, 6), dim), (parts,), jnp.float32, smallest / len(split), largest / len(split))
        loudness = loudness * jnp.repeat(jnp.exp(draws), dims[dim] // parts).reshape((-1,) + (1,) * (len(dims) - 1 - dim))
    return loudness


def length_profile(number_of, total, most, skew):
    loads = [(1 << 20) // math.isqrt(rank ** skew) + 1 for rank in range(2, number_of + 1)]
    spare, given = total - most - (number_of - 1), [1] * (number_of - 1)
    while spare > 0:
        free = [i for i in range(number_of - 1) if given[i] < most]
        whole, budget = sum([loads[i] for i in free]), spare
        for i in free:
            more = min(most - given[i], max(1, budget * loads[i] // whole), spare)
            given[i] = given[i] + more
            spare = spare - more
    return np.array([most] + given)


def ragged(rng, number_of, total, reach, slope):
    if number_of == 2:
        one = jax.random.randint(rng, (), max(1, total - reach), min(reach, total - 1) + 1)
        return jnp.stack([one, total - one])
    sizes = jnp.asarray(length_profile(number_of, total, reach, slope), jnp.int32)
    couples = (number_of - 1) // 2
    giver, taker = sizes[1:1 + 2 * couples:2], sizes[2:2 + 2 * couples:2]
    margin = jnp.minimum(giver - 1, reach - taker)
    moved = jax.random.randint(jax.random.fold_in(rng, 1), (couples,), 0, 1 << 20) % (margin + 1)
    sizes = sizes.at[1:1 + 2 * couples:2].set(giver - moved).at[2:2 + 2 * couples:2].set(taker + moved)
    return sizes[jax.random.permutation(jax.random.fold_in(rng, 2), number_of)]


def deal_out(key, own, number, rows, number_of, top, limit, lean):
    sequence = jax.random.permutation(key, number_of)
    packed, ordinary = portions_of(number_of, rows * top, limit, lean, True), portions_of(number_of, rows * top, limit, lean, False)
    places = jnp.arange(number_of)

    def named(tallies, turn):
        used = int((tallies > 0).sum())
        fixed = max(1, used // 4)
        passed = fixed + (places - fixed + turn * (used - fixed)) % max(1, number_of - fixed)
        return jnp.zeros((number_of,), jnp.int32).at[sequence[jnp.where(places < fixed, places, passed)]].set(jnp.asarray(tallies, jnp.int32))

    tallies = jnp.where(number % 4 == 0, named(packed, number // 4), named(ordinary, number - number // 4 - 1))
    mixed = jax.random.permutation(jax.random.fold_in(own, 3), number_of)
    source_of, receiver = mixed[0:number_of // 2 * 2:2], mixed[1:number_of // 2 * 2:2]
    room = jnp.minimum(tallies[source_of] - 1, limit - tallies[receiver]) // 2
    room = jnp.where((source_of == sequence[0]) | (receiver == sequence[0]) | (tallies[receiver] == 0), 0, jnp.maximum(room, 0))
    passed = jax.random.randint(jax.random.fold_in(own, 4), (number_of // 2,), 0, 1 << 20) % (room + 1)
    tallies = tallies.at[source_of].add(-passed).at[receiver].add(passed)
    members = jnp.searchsorted(jnp.cumsum(tallies), jnp.arange(rows * top), side="right").astype(jnp.int32)
    table = members.reshape(top, rows).T
    table = table[jax.random.permutation(jax.random.fold_in(own, 1), rows)]
    turn = jax.random.randint(jax.random.fold_in(own, 2), (rows, 1), 0, top)
    return jnp.take_along_axis(table, (jnp.arange(top)[None, :] + turn) % top, axis=1)


def portions_of(amount, total, limit, slope, full):
    weights = [(1 << 20) // math.isqrt(standing ** slope) + 1 for standing in range(1, amount + 1)]
    largest = limit if full else min(limit, max(-(-total // amount), total * weights[0] // sum(weights)))
    least = 1 if total - largest >= amount - 1 else 0
    given, spare = [largest] + [least] * (amount - 1), total - largest - least * (amount - 1)
    while spare > 0:
        candidates = [i for i in range(1, amount) if given[i] < largest] or [i for i in range(1, amount) if given[i] < limit]
        whole, remaining = sum([weights[i] for i in candidates]), spare
        for i in candidates:
            extra = min(limit - given[i], max(1, remaining * weights[i] // whole), spare)
            given[i] = given[i] + extra
            spare = spare - extra
    return np.array(given)


def bell_draw(rng, dims, deviation, bound, split=(), kind=jnp.bfloat16):
    level = block_levels(rng, dims, split, -0.22, 0.18) if split else 1.0
    entries = jax.random.normal(rng, dims, jnp.float32) * deviation * level
    return jnp.minimum(jnp.maximum(entries, -bound), bound).astype(kind)


def setup_inputs(seed: int = 0) -> dict:
    key_of = jax.random.split(jax.random.key(seed), 14)
    frames = bell_draw(key_of[0], (FRAMES, D), 1.0, 6.0, ((0, 16),))
    ln_gain = jnp.clip(1.0 + 0.1 * jax.random.normal(key_of[1], (D,), jnp.float32), 0.5, 1.5)
    w_value = bell_draw(key_of[2], (D, D), D ** -0.5, 0.15625, ((1, 2),))
    w_gate = bell_draw(key_of[3], (D, D), D ** -0.5, 0.15625, ((1, 2),))
    conv_taps = bell_draw(key_of[4], (KERNEL, D), KERNEL ** -0.5, 1.0, ((1, 2),), jnp.float32)
    bn_scale = jnp.clip(1.0 + 0.15 * jax.random.normal(key_of[5], (D,), jnp.float32), 0.25, 1.75)
    bn_shift = bell_draw(key_of[6], (D,), 0.5, 3.0, ((0, 2),), jnp.float32)
    w_out = bell_draw(key_of[7], (D, D), D ** -0.5, 0.15625)
    w_classes = bell_draw(key_of[8], (D, CLASSES), D ** -0.5, 0.15625)
    seg_lengths = jax.vmap(lambda own: ragged(own, SEG_DEV, FR_DEV, MAXLEN, 2))(jax.random.split(key_of[9], N_TM)).reshape((N_TM, SEG_DEV)).astype(jnp.int32)
    owners_keys = jax.random.split(jax.random.fold_in(key_of[10], 1), SEGMENTS // SEG_DEV)
    owners_turns = jax.random.permutation(jax.random.fold_in(key_of[10], 3), SEGMENTS // SEG_DEV)
    owners = jax.vmap(lambda own, number: deal_out(jax.random.fold_in(key_of[10], 2), own, number, SEG_DEV, N_TM, 1, CAP, 2))(owners_keys, owners_turns).reshape((SEGMENTS, 1))
    silence = draw_silence(jax.random.fold_in(key_of[13], 71), 0)
    tags = with_ends(jax.random.randint(key_of[12], (N_TM, SEG_DEV), 0, TAGS), jax.random.fold_in(key_of[12], 1), 0, TAGS - 1).astype(jnp.int32)
    return {"frames": frames, "ln_gain": ln_gain, "w_value": w_value, "w_gate": w_gate, "conv_taps": conv_taps, "bn_scale": bn_scale, "bn_shift": bn_shift, "w_out": w_out, "w_classes": w_classes, "seg_lengths": seg_lengths, "owners": owners, "silence": silence, "tags": tags}


def reference(frames, ln_gain, w_value, w_gate, conv_taps, bn_scale, bn_shift, w_out, w_classes, seg_lengths, owners, silence, tags):
    inputs = frames.astype(jnp.float32)
    center = lax.optimization_barrier(jnp.mean(inputs, axis=-1, keepdims=True))
    spread = lax.optimization_barrier(jnp.mean((inputs - center) ** 2, axis=-1, keepdims=True))
    normed = ((inputs - center) * lax.rsqrt(spread + 1e-05) * ln_gain).astype(jnp.bfloat16)
    values_part = jnp.dot(normed, w_value, preferred_element_type=jnp.float32)
    gates_part = jnp.dot(normed, w_gate, preferred_element_type=jnp.float32)
    glu_out = (values_part * jax.nn.sigmoid(gates_part)).astype(jnp.bfloat16)
    half_width = (KERNEL - 1) // 2
    padded = jnp.pad(glu_out.astype(jnp.float32), ((half_width, half_width), (0, 0)))
    depth_sum = jnp.zeros((FRAMES, D), jnp.float32)
    for tap_index in range(KERNEL):
        depth_sum = depth_sum + conv_taps[tap_index] * padded[tap_index:tap_index + FRAMES]
    shifted = depth_sum * bn_scale + bn_shift
    activated = (shifted * jax.nn.sigmoid(shifted)).astype(jnp.bfloat16)
    block_out = (inputs + jnp.dot(activated, w_out, preferred_element_type=jnp.float32)).astype(jnp.bfloat16)
    projected = jnp.dot(block_out, w_classes, preferred_element_type=jnp.float32)
    seg_ends = jnp.cumsum(seg_lengths, axis=1).astype(jnp.int32)
    seg_starts = (seg_ends - seg_lengths).astype(jnp.int32)
    positions = jnp.arange(FR_DEV, dtype=jnp.int32)
    inside = (positions[None, None, :] >= seg_starts[:, :, None]) & (positions[None, None, :] < seg_ends[:, :, None])
    pooling = inside.astype(jnp.float32) / seg_lengths[:, :, None].astype(jnp.float32)
    logits = jnp.einsum('tsf,tfc->tsc', pooling, projected.reshape(N_TM, FR_DEV, CLASSES), precision=lax.Precision.HIGHEST)
    owner_ids = owners[:, 0].reshape(N_TM, SEG_DEV)
    matches = owner_ids[:, :, None] == owner_ids[:, None, :]
    seg_index = jnp.arange(SEG_DEV, dtype=jnp.int32)
    earlier = seg_index[None, :] < seg_index[:, None]
    slot_index = lax.optimization_barrier(jnp.sum((matches & earlier[None]).astype(jnp.int32), axis=2)).astype(jnp.int32)
    source_ids = jnp.arange(N_TM, dtype=jnp.int32)[:, None]
    dest_rows = (owner_ids * SLOTS + source_ids * CAP + slot_index).astype(jnp.int32)
    silent = silence.astype(jnp.float32)
    tag_onehot = (tags[:, :, None] == jnp.arange(TAGS, dtype=jnp.int32)[None, None, :]).astype(jnp.float32)
    weighted = tag_onehot * silent[:, :, None]
    tag_sums = jnp.einsum('tsg,tsc->gc', weighted, logits, precision=lax.Precision.HIGHEST)
    tag_counts = lax.optimization_barrier(jnp.sum(weighted, axis=(0, 1)))
    calibration = tag_sums / (tag_counts + 1.0)[:, None]
    seg_scores = logits - jnp.einsum('tsg,gc->tsc', tag_onehot, calibration, precision=lax.Precision.HIGHEST)
    scores = jnp.zeros((N_TM * SLOTS, CLASSES), jnp.float32).at[dest_rows.reshape(-1)].set(seg_scores.reshape(-1, CLASSES))
    return (block_out.reshape(N_TM, N_GRP, FR_DEV // N_GRP, D), scores)
```

```python
import functools

import jax
import jax.numpy as jnp
from jax import lax
from jax.experimental import pallas as pl
from jax.experimental.pallas import tpu as pltpu
from jax.sharding import PartitionSpec as P

TAGS = 256
CAP = 8
HALO = 16
BLOCK = 256
LANES = 128
VMEM_LIMIT = 48 << 20
F32, BF16 = jnp.float32, jnp.bfloat16


def sigmoid(v):
    return 0.5 * jnp.tanh(0.5 * v) + 0.5


def params():
    return pltpu.CompilerParams(
        dimension_semantics=("arbitrary",), vmem_limit_bytes=VMEM_LIMIT
    )


def whole(shape):
    return pl.BlockSpec(shape, lambda i, s: (0,) * len(shape))


def segment_mask(first, count, starts, ends):
    rows = first + lax.broadcasted_iota(jnp.int32, (starts.shape[0], count), 1)
    return (rows >= starts) & (rows < ends)


def glu_kernel(s, frames, gain, w_value, w_gate, starts, ends, glu, pooled, *, own_rows):
    step = pl.program_id(0)
    block = frames.shape[0]
    own_first = s[0] * own_rows

    @pl.when(step == 0)
    def _():
        pooled[...] = jnp.zeros_like(pooled)

    first = step * block

    @pl.when((first < own_first + own_rows) & (first + block > own_first))
    def _():
        rows = first + lax.broadcasted_iota(jnp.int32, (starts.shape[0], block), 1)
        low = jnp.maximum(starts[...], own_first)
        high = jnp.minimum(ends[...], own_first + own_rows)
        mask = ((rows >= low) & (rows < high)).astype(F32).astype(BF16)
        pooled[...] += jnp.dot(mask, frames[...], preferred_element_type=F32)

    half = block // 2
    for part in range(2):
        rows = pl.ds(part * half, half)
        x = frames[rows, :].astype(F32)
        center = jnp.mean(x, axis=-1, keepdims=True)
        x = x - center
        spread = jnp.mean(x * x, axis=-1, keepdims=True)
        normed = (x * lax.rsqrt(spread + 1e-05) * gain[...]).astype(BF16)
        value = jnp.dot(normed, w_value[...], preferred_element_type=F32)
        gate = jnp.dot(normed, w_gate[...], preferred_element_type=F32)
        glu[rows, :] = (value * sigmoid(gate)).astype(BF16)


def conv_kernel(s, window, taps, scale, shift, starts, ends, act, pooled, xs, *, taps_n):
    step = pl.program_id(0)
    block, channels = act.shape
    tiles = [(c, min(LANES, channels - c)) for c in range(0, channels, LANES)]
    for t, (c, w) in enumerate(tiles):
        xs[t, :, 0:w] = window[:, c : c + w].astype(F32)

    def tile(t, c, w):
        lanes = pl.ds(c, w)
        for r in range(0, block, 64):
            total = jnp.zeros((64, w), F32)
            for k in range(taps_n):
                total = total + taps[k : k + 1, lanes] * xs[t, pl.ds(r + 1 + k, 64), 0:w]
            v = total * scale[:, lanes] + shift[:, lanes]
            act[pl.ds(r, 64), lanes] = (v * sigmoid(v)).astype(BF16)

    if channels % LANES == 0:

        @pl.loop(0, channels // LANES)
        def _(t):
            tile(t, pl.multiple_of(t * LANES, LANES), LANES)
    else:
        for t, (c, w) in enumerate(tiles):
            tile(t, c, w)

    first = s[0] + step * block
    mask = segment_mask(first, block, starts[...], ends[...]).astype(F32).astype(BF16)
    part = jnp.dot(mask, act[...], preferred_element_type=F32)

    @pl.when(step == 0)
    def _():
        pooled[...] = part

    @pl.when(step > 0)
    def _():
        pooled[...] += part


def logits_kernel(s, frames_pooled, pooled, w_out, w_classes, starts, ends, out):
    mixed = jnp.dot(pooled[...].astype(BF16), w_out[...], preferred_element_type=F32)
    inverse = 1.0 / (ends[...] - starts[...]).astype(F32)
    mean = ((frames_pooled[...] + mixed) * inverse).astype(BF16)
    out[...] = jnp.dot(mean, w_classes[...], preferred_element_type=F32)


def out_kernel(s, *refs):
    *pairs, frames, out = refs
    total = frames[...].astype(F32)
    for act, w_out in zip(pairs[0::2], pairs[1::2]):
        total = total + jnp.dot(act[...], w_out[...], preferred_element_type=F32)
    out[...] = total.astype(BF16)


def run_glu(group_index, own_rows, frames, gain, w_value, w_gate, starts, ends):
    count, width = frames.shape
    channels = w_value.shape[1]
    segs = starts.shape[0]
    return pl.pallas_call(
        functools.partial(glu_kernel, own_rows=own_rows),
        grid_spec=pltpu.PrefetchScalarGridSpec(
            num_scalar_prefetch=1,
            grid=(count // BLOCK,),
            in_specs=[
                pl.BlockSpec((BLOCK, width), lambda i, s: (i, 0)),
                whole((1, width)),
                whole((width, channels)),
                whole((width, channels)),
                whole((segs, 1)),
                whole((segs, 1)),
            ],
            out_specs=[
                pl.BlockSpec((BLOCK, channels), lambda i, s: (i, 0)),
                whole((segs, width)),
            ],
        ),
        out_shape=[
            jax.ShapeDtypeStruct((count, channels), BF16),
            jax.ShapeDtypeStruct((segs, width), F32),
        ],
        compiler_params=params(),
        name="glu",
    )(group_index, frames, gain, w_value, w_gate, starts, ends)


def run_conv(base, rows, padded, taps, scale, shift, starts, ends):
    channels = padded.shape[1]
    segs = starts.shape[0]
    tiles = pl.cdiv(channels, LANES)
    return pl.pallas_call(
        functools.partial(conv_kernel, taps_n=taps.shape[0]),
        grid_spec=pltpu.PrefetchScalarGridSpec(
            num_scalar_prefetch=1,
            grid=(rows // BLOCK,),
            in_specs=[
                pl.BlockSpec(
                    (pl.Element(BLOCK + 2 * HALO), pl.Element(channels)),
                    lambda i, s: (pl.multiple_of(s[0] + i * BLOCK, HALO), 0),
                ),
                whole(taps.shape),
                whole((1, channels)),
                whole((1, channels)),
                whole((segs, 1)),
                whole((segs, 1)),
            ],
            out_specs=[
                pl.BlockSpec((BLOCK, channels), lambda i, s: (i, 0)),
                whole((segs, channels)),
            ],
            scratch_shapes=[pltpu.VMEM((tiles, BLOCK + 2 * HALO, LANES), F32)],
        ),
        out_shape=[
            jax.ShapeDtypeStruct((rows, channels), BF16),
            jax.ShapeDtypeStruct((segs, channels), F32),
        ],
        compiler_params=params(),
        name="conv",
    )(base, padded, taps, scale, shift, starts, ends)


def run_logits(group_index, frames_pooled, pooled, w_out, w_classes, starts, ends):
    segs, channels = pooled.shape
    width, classes = w_classes.shape
    return pl.pallas_call(
        logits_kernel,
        grid_spec=pltpu.PrefetchScalarGridSpec(
            num_scalar_prefetch=1,
            grid=(1,),
            in_specs=[
                whole((segs, width)),
                whole((segs, channels)),
                pl.BlockSpec((channels, width), lambda i, s: (s[0], 0)),
                whole((width, classes)),
                whole((segs, 1)),
                whole((segs, 1)),
            ],
            out_specs=whole((segs, classes)),
        ),
        out_shape=jax.ShapeDtypeStruct((segs, classes), F32),
        compiler_params=params(),
        name="logits",
    )(group_index, frames_pooled, pooled, w_out, w_classes, starts, ends)


def run_out(scalars, sources, w_out, frames, rows):
    width = frames.shape[1]
    block = BLOCK if rows % BLOCK == 0 else rows
    steps = rows // block
    in_specs, operands = [], []
    for act, place in sources:
        in_specs.append(pl.BlockSpec((block, act.shape[1]), lambda i, s: (i, 0)))
        in_specs.append(
            pl.BlockSpec((act.shape[1], width), functools.partial(lambda p, i, s: (s[p], 0), place))
        )
        operands += [act, w_out]
    in_specs.append(pl.BlockSpec((block, width), lambda i, s: (s[0] * steps + i, 0)))
    return pl.pallas_call(
        out_kernel,
        grid_spec=pltpu.PrefetchScalarGridSpec(
            num_scalar_prefetch=1,
            grid=(steps,),
            in_specs=in_specs,
            out_specs=pl.BlockSpec((block, width), lambda i, s: (i, 0)),
        ),
        out_shape=jax.ShapeDtypeStruct((rows, width), BF16),
        compiler_params=params(),
        name="block_out",
    )(scalars, *operands, frames)


def swap(value, axis, bit):
    count = lax.axis_size(axis)
    return lax.ppermute(value, axis, [(i, i ^ bit) for i in range(count)])


def body(
    frames,
    ln_gain,
    w_value,
    w_gate,
    conv_taps,
    bn_scale,
    bn_shift,
    w_out,
    w_classes,
    seg_lengths,
    owners,
    silence,
    tags,
):
    count, width = frames.shape
    channels = w_value.shape[1]
    group_size = lax.axis_size("grp")
    time_size = lax.axis_size("tm")
    group = lax.axis_index("grp")
    time = lax.axis_index("tm")
    own_rows = count // group_size
    lengths = seg_lengths[0]
    segs = lengths.shape[0]
    order = jnp.arange(segs, dtype=jnp.int32)
    ends = jnp.sum(
        jnp.where(order[None, :] <= order[:, None], lengths[None, :], 0), axis=1, keepdims=True
    )
    starts = ends - lengths[:, None]
    group_scalar = group[None].astype(jnp.int32)

    glu, frames_pooled = run_glu(
        group_scalar, own_rows, frames, ln_gain[None, :], w_value, w_gate, starts, ends
    )
    up = [(i, i + 1) for i in range(time_size - 1)]
    down = [(j, i) for i, j in up]
    before = lax.ppermute(glu[count - HALO :], "tm", up)
    after = lax.ppermute(glu[:HALO], "tm", down)
    padded = jnp.concatenate([before, glu, after], axis=0)
    bn = (conv_taps, bn_scale[None, :], bn_shift[None, :], starts, ends)

    if group_size == 2:
        other = 1 - group_scalar
        act_other, pooled_other = run_conv(other * own_rows, own_rows, padded, *bn)
        act_got = swap(act_other, "grp", 1)
        act_own, pooled_own = run_conv(group_scalar * own_rows, own_rows, padded, *bn)
        pooled = pooled_other + pooled_own
        sources = [(act_own, 0), (act_got, 1)]
        scalars = jnp.concatenate([group_scalar, other])
    else:
        act, pooled = run_conv(jnp.zeros((1,), jnp.int32), count, padded, *bn)
        rows = lax.all_to_all(act, "grp", split_axis=0, concat_axis=1, tiled=True)
        sources = [(rows, 1)]
        scalars = jnp.concatenate([group_scalar, jnp.zeros((1,), jnp.int32)])

    logits = run_logits(group_scalar, frames_pooled, pooled, w_out, w_classes, starts, ends)

    bit = group_size // 2
    while bit:
        half = logits.shape[1] // 2
        upper = (group // bit) % 2
        kept = lax.dynamic_slice_in_dim(logits, upper * half, half, 1)
        sent = lax.dynamic_slice_in_dim(logits, (1 - upper) * half, half, 1)
        logits = kept + swap(sent.astype(BF16), "grp", bit).astype(F32)
        bit //= 2
    classes = logits.shape[1]

    owner_ids = owners[:, 0]
    earlier = order[None, :] < order[:, None]
    slot = jnp.sum(((owner_ids[:, None] == owner_ids[None, :]) & earlier).astype(jnp.int32), axis=1)
    dest = owner_ids * CAP + slot
    slots = time_size * CAP
    placing = (dest[None, :] == jnp.arange(slots, dtype=jnp.int32)[:, None]).astype(BF16)
    rounded = logits.astype(BF16)
    tag_numbers = (tags[0] + 1).astype(BF16)
    pad = jnp.zeros((segs, LANES - 1), BF16)
    labelled = jnp.concatenate([rounded, tag_numbers[:, None], pad], axis=1)
    send = jnp.dot(placing, labelled, preferred_element_type=F32).astype(BF16)
    got = lax.all_to_all(send, "tm", split_axis=0, concat_axis=0, tiled=True)

    tag_ids = jnp.arange(TAGS, dtype=jnp.int32)
    weighted = (tag_ids[:, None] == tags) & (silence > 0)
    sums = jnp.dot(weighted.astype(BF16), rounded, preferred_element_type=F32)
    counts = jnp.sum(weighted.astype(F32), axis=1, keepdims=True)
    counts = jnp.broadcast_to(counts, (TAGS, LANES))

    def exchanged(values, numbers, bit):
        high = jnp.floor(numbers * (1 / 128)) * 128
        lane = lax.broadcasted_iota(jnp.int32, numbers.shape, 1)
        coded = jnp.where(lane == 0, high, numbers - high)
        message = jnp.concatenate([values, coded], axis=1).astype(BF16)
        arrived = swap(message, "tm", bit).astype(F32)
        return arrived[:, :classes], arrived[:, classes : classes + 1] + arrived[:, classes + 1 : classes + 2]

    core = time % 2
    half = TAGS // 2
    sent_sums = lax.dynamic_slice_in_dim(sums, (1 - core) * half, half, 0)
    sent_counts = lax.dynamic_slice_in_dim(counts, (1 - core) * half, half, 0)
    sums = lax.dynamic_slice_in_dim(sums, core * half, half, 0)
    counts = lax.dynamic_slice_in_dim(counts, core * half, half, 0)
    more_sums, more_counts = exchanged(sent_sums, sent_counts, 1)
    sums, counts = sums + more_sums, counts + more_counts
    bit = 2
    while bit < time_size:
        more_sums, more_counts = exchanged(sums, counts, bit)
        sums, counts = sums + more_sums, counts + more_counts
        bit *= 2
    mine = (sums / (counts[:, :1] + 1.0)).astype(BF16)
    theirs = swap(mine, "tm", 1)
    shard_tags = got[:, classes : classes + 1].astype(jnp.int32)
    onehot_mine = (shard_tags == (tag_ids[:half] + core * half + 1)[None, :]).astype(BF16)
    onehot_theirs = (shard_tags == (tag_ids[:half] + (1 - core) * half + 1)[None, :]).astype(BF16)
    calibration = jnp.dot(onehot_mine, mine, preferred_element_type=F32) + jnp.dot(
        onehot_theirs, theirs, preferred_element_type=F32
    )
    scores = got[:, :classes].astype(F32) - calibration

    block_rows = run_out(scalars, sources, w_out, frames, own_rows)
    return (block_rows[None, None], scores)


def solution(mesh):
    in_specs = (
        P("tm", None),
        P(),
        P(None, "grp"),
        P(None, "grp"),
        P(None, "grp"),
        P("grp"),
        P("grp"),
        P(),
        P(),
        P("tm", None),
        P("tm", None),
        P("tm", None),
        P("tm", None),
    )
    out_specs = (P("tm", "grp", None, None), P("tm", "grp"))
    return jax.shard_map(body, mesh=mesh, in_specs=in_specs, out_specs=out_specs, check_vma=False)
```

```python
import functools

import jax
import jax.numpy as jnp
from jax import lax
from jax.experimental import pallas as pl
from jax.experimental.pallas import tpu as pltpu
from jax.sharding import PartitionSpec as P

TAGS = 256
CAP = 8
HALO = 16
BLOCK = 256
LANES = 128
VMEM_LIMIT = 48 << 20
F32, BF16 = jnp.float32, jnp.bfloat16


def sigmoid(v):
    return 0.5 * jnp.tanh(0.5 * v) + 0.5


def params():
    return pltpu.CompilerParams(
        dimension_semantics=("arbitrary",), vmem_limit_bytes=VMEM_LIMIT
    )


def whole(shape):
    return pl.BlockSpec(shape, lambda i, s: (0,) * len(shape))


def segment_mask(first, count, starts, ends):
    rows = first + lax.broadcasted_iota(jnp.int32, (starts.shape[0], count), 1)
    return (rows >= starts) & (rows < ends)


def glu_kernel(s, frames, gain, w_value, w_gate, starts, ends, glu, pooled, *, own_rows):
    step = pl.program_id(0)
    block = frames.shape[0]
    own_first = s[0] * own_rows

    @pl.when(step == 0)
    def _():
        pooled[...] = jnp.zeros_like(pooled)

    first = step * block

    @pl.when((first < own_first + own_rows) & (first + block > own_first))
    def _():
        rows = first + lax.broadcasted_iota(jnp.int32, (starts.shape[0], block), 1)
        low = jnp.maximum(starts[...], own_first)
        high = jnp.minimum(ends[...], own_first + own_rows)
        mask = ((rows >= low) & (rows < high)).astype(F32).astype(BF16)
        pooled[...] += jnp.dot(mask, frames[...], preferred_element_type=F32)

    half = block // 2
    for part in range(2):
        rows = pl.ds(part * half, half)
        x = frames[rows, :].astype(F32)
        center = jnp.mean(x, axis=-1, keepdims=True)
        x = x - center
        spread = jnp.mean(x * x, axis=-1, keepdims=True)
        normed = (x * lax.rsqrt(spread + 1e-05) * gain[...]).astype(BF16)
        value = jnp.dot(normed, w_value[...], preferred_element_type=F32)
        gate = jnp.dot(normed, w_gate[...], preferred_element_type=F32)
        glu[rows, :] = (value * sigmoid(gate)).astype(BF16)


def conv_kernel(s, window, taps, scale, shift, starts, ends, act, pooled, xs, *, taps_n):
    step = pl.program_id(0)
    block, channels = act.shape
    tiles = [(c, min(LANES, channels - c)) for c in range(0, channels, LANES)]
    for t, (c, w) in enumerate(tiles):
        xs[t, :, 0:w] = window[:, c : c + w].astype(F32)

    def tile(t, c, w):
        lanes = pl.ds(c, w)
        for r in range(0, block, 64):
            total = jnp.zeros((64, w), F32)
            for k in range(taps_n):
                total = total + taps[k : k + 1, lanes] * xs[t, pl.ds(r + 1 + k, 64), 0:w]
            v = total * scale[:, lanes] + shift[:, lanes]
            act[pl.ds(r, 64), lanes] = (v * sigmoid(v)).astype(BF16)

    if channels % LANES == 0:

        @pl.loop(0, channels // LANES)
        def _(t):
            tile(t, pl.multiple_of(t * LANES, LANES), LANES)
    else:
        for t, (c, w) in enumerate(tiles):
            tile(t, c, w)

    first = s[0] + step * block
    mask = segment_mask(first, block, starts[...], ends[...]).astype(F32).astype(BF16)
    part = jnp.dot(mask, act[...], preferred_element_type=F32)

    @pl.when(step == 0)
    def _():
        pooled[...] = part

    @pl.when(step > 0)
    def _():
        pooled[...] += part


def logits_kernel(s, frames_pooled, pooled, w_out, w_classes, starts, ends, out):
    mixed = jnp.dot(pooled[...].astype(BF16), w_out[...], preferred_element_type=F32)
    inverse = 1.0 / (ends[...] - starts[...]).astype(F32)
    mean = ((frames_pooled[...] + mixed) * inverse).astype(BF16)
    out[...] = jnp.dot(mean, w_classes[...], preferred_element_type=F32)


def out_kernel(s, *refs):
    *pairs, frames, out = refs
    total = frames[...].astype(F32)
    for act, w_out in zip(pairs[0::2], pairs[1::2]):
        total = total + jnp.dot(act[...], w_out[...], preferred_element_type=F32)
    out[...] = total.astype(BF16)


def run_glu(group_index, own_rows, frames, gain, w_value, w_gate, starts, ends):
    count, width = frames.shape
    channels = w_value.shape[1]
    segs = starts.shape[0]
    return pl.pallas_call(
        functools.partial(glu_kernel, own_rows=own_rows),
        grid_spec=pltpu.PrefetchScalarGridSpec(
            num_scalar_prefetch=1,
            grid=(count // BLOCK,),
            in_specs=[
                pl.BlockSpec((BLOCK, width), lambda i, s: (i, 0)),
                whole((1, width)),
                whole((width, channels)),
                whole((width, channels)),
                whole((segs, 1)),
                whole((segs, 1)),
            ],
            out_specs=[
                pl.BlockSpec((BLOCK, channels), lambda i, s: (i, 0)),
                whole((segs, width)),
            ],
        ),
        out_shape=[
            jax.ShapeDtypeStruct((count, channels), BF16),
            jax.ShapeDtypeStruct((segs, width), F32),
        ],
        compiler_params=params(),
        name="glu",
    )(group_index, frames, gain, w_value, w_gate, starts, ends)


def run_conv(base, rows, padded, taps, scale, shift, starts, ends):
    channels = padded.shape[1]
    segs = starts.shape[0]
    tiles = pl.cdiv(channels, LANES)
    return pl.pallas_call(
        functools.partial(conv_kernel, taps_n=taps.shape[0]),
        grid_spec=pltpu.PrefetchScalarGridSpec(
            num_scalar_prefetch=1,
            grid=(rows // BLOCK,),
            in_specs=[
                pl.BlockSpec(
                    (pl.Element(BLOCK + 2 * HALO), pl.Element(channels)),
                    lambda i, s: (pl.multiple_of(s[0] + i * BLOCK, HALO), 0),
                ),
                whole(taps.shape),
                whole((1, channels)),
                whole((1, channels)),
                whole((segs, 1)),
                whole((segs, 1)),
            ],
            out_specs=[
                pl.BlockSpec((BLOCK, channels), lambda i, s: (i, 0)),
                whole((segs, channels)),
            ],
            scratch_shapes=[pltpu.VMEM((tiles, BLOCK + 2 * HALO, LANES), F32)],
        ),
        out_shape=[
            jax.ShapeDtypeStruct((rows, channels), BF16),
            jax.ShapeDtypeStruct((segs, channels), F32),
        ],
        compiler_params=params(),
        name="conv",
    )(base, padded, taps, scale, shift, starts, ends)


def run_logits(group_index, frames_pooled, pooled, w_out, w_classes, starts, ends):
    segs, channels = pooled.shape
    width, classes = w_classes.shape
    return pl.pallas_call(
        logits_kernel,
        grid_spec=pltpu.PrefetchScalarGridSpec(
            num_scalar_prefetch=1,
            grid=(1,),
            in_specs=[
                whole((segs, width)),
                whole((segs, channels)),
                pl.BlockSpec((channels, width), lambda i, s: (s[0], 0)),
                whole((width, classes)),
                whole((segs, 1)),
                whole((segs, 1)),
            ],
            out_specs=whole((segs, classes)),
        ),
        out_shape=jax.ShapeDtypeStruct((segs, classes), F32),
        compiler_params=params(),
        name="logits",
    )(group_index, frames_pooled, pooled, w_out, w_classes, starts, ends)


def run_out(scalars, sources, w_out, frames, rows):
    width = frames.shape[1]
    block = BLOCK if rows % BLOCK == 0 else rows
    steps = rows // block
    in_specs, operands = [], []
    for act, place in sources:
        in_specs.append(pl.BlockSpec((block, act.shape[1]), lambda i, s: (i, 0)))
        in_specs.append(
            pl.BlockSpec((act.shape[1], width), functools.partial(lambda p, i, s: (s[p], 0), place))
        )
        operands += [act, w_out]
    in_specs.append(pl.BlockSpec((block, width), lambda i, s: (s[0] * steps + i, 0)))
    return pl.pallas_call(
        out_kernel,
        grid_spec=pltpu.PrefetchScalarGridSpec(
            num_scalar_prefetch=1,
            grid=(steps,),
            in_specs=in_specs,
            out_specs=pl.BlockSpec((block, width), lambda i, s: (i, 0)),
        ),
        out_shape=jax.ShapeDtypeStruct((rows, width), BF16),
        compiler_params=params(),
        name="block_out",
    )(scalars, *operands, frames)


def swap(value, axis, bit):
    count = lax.axis_size(axis)
    return lax.ppermute(value, axis, [(i, i ^ bit) for i in range(count)])


def general_body(
    frames,
    ln_gain,
    w_value,
    w_gate,
    conv_taps,
    bn_scale,
    bn_shift,
    w_out,
    w_classes,
    seg_lengths,
    owners,
    silence,
    tags,
):
    count, width = frames.shape
    channels = w_value.shape[1]
    group_size = lax.axis_size("grp")
    time_size = lax.axis_size("tm")
    group = lax.axis_index("grp")
    time = lax.axis_index("tm")
    own_rows = count // group_size
    lengths = seg_lengths[0]
    segs = lengths.shape[0]
    order = jnp.arange(segs, dtype=jnp.int32)
    ends = jnp.sum(
        jnp.where(order[None, :] <= order[:, None], lengths[None, :], 0), axis=1, keepdims=True
    )
    starts = ends - lengths[:, None]
    group_scalar = group[None].astype(jnp.int32)

    glu, frames_pooled = run_glu(
        group_scalar, own_rows, frames, ln_gain[None, :], w_value, w_gate, starts, ends
    )
    up = [(i, i + 1) for i in range(time_size - 1)]
    down = [(j, i) for i, j in up]
    before = lax.ppermute(glu[count - HALO :], "tm", up)
    after = lax.ppermute(glu[:HALO], "tm", down)
    padded = jnp.concatenate([before, glu, after], axis=0)
    bn = (conv_taps, bn_scale[None, :], bn_shift[None, :], starts, ends)

    if group_size == 2:
        other = 1 - group_scalar
        act_other, pooled_other = run_conv(other * own_rows, own_rows, padded, *bn)
        act_got = swap(act_other, "grp", 1)
        act_own, pooled_own = run_conv(group_scalar * own_rows, own_rows, padded, *bn)
        pooled = pooled_other + pooled_own
        sources = [(act_own, 0), (act_got, 1)]
        scalars = jnp.concatenate([group_scalar, other])
    else:
        act, pooled = run_conv(jnp.zeros((1,), jnp.int32), count, padded, *bn)
        rows = lax.all_to_all(act, "grp", split_axis=0, concat_axis=1, tiled=True)
        sources = [(rows, 1)]
        scalars = jnp.concatenate([group_scalar, jnp.zeros((1,), jnp.int32)])

    logits = run_logits(group_scalar, frames_pooled, pooled, w_out, w_classes, starts, ends)

    scores = tail(logits, owners, silence, tags)

    block_rows = run_out(scalars, sources, w_out, frames, own_rows)
    return (block_rows[None, None], scores)


def in_hbm(value):
    return pltpu.with_memory_space_constraint(value, pltpu.HBM)


def cost(flops, traffic):
    return pl.CostEstimate(flops=flops, bytes_accessed=traffic, transcendentals=0)


VMEM_SPEC = pl.BlockSpec(memory_space=pltpu.VMEM)
SMEM_SPEC = pl.BlockSpec(memory_space=pltpu.SMEM)
ANY_SPEC = pl.BlockSpec(memory_space=pltpu.HBM)
SMALL = pltpu.CompilerParams(vmem_limit_bytes=8 << 20)


def fast_glu_kernel(frames, gain, w_value, w_gate, glu, rows_in, wv, wg, normed, row_sem, col_sem):
    count, width = frames.shape
    channels = wv.shape[1]
    blocks = count // BLOCK
    columns = channels // BLOCK

    def row_copy(b):
        rows = pl.ds(b * BLOCK, BLOCK)
        return pltpu.make_async_copy(frames.at[rows, :], rows_in.at[rows, :], row_sem.at[b])

    def column_copies(c):
        cols = pl.ds(c * BLOCK, BLOCK)
        return (
            pltpu.make_async_copy(w_value.at[:, cols], wv.at[:, cols], col_sem.at[0, c]),
            pltpu.make_async_copy(w_gate.at[:, cols], wg.at[:, cols], col_sem.at[1, c]),
        )

    def normalize(b):
        rows = pl.ds(b * BLOCK, BLOCK)
        x = rows_in[rows, :].astype(F32)
        center = jnp.mean(x, axis=-1, keepdims=True)
        x = x - center
        spread = jnp.mean(x * x, axis=-1, keepdims=True)
        normed[...] = (x * (0.5 * lax.rsqrt(spread + 1e-05)) * gain[...]).astype(BF16)

    def gated(b, c):
        cols = pl.ds(c * BLOCK, BLOCK)
        value = jnp.dot(normed[...], wv[:, cols], preferred_element_type=F32)
        gate = jnp.dot(normed[...], wg[:, cols], preferred_element_type=F32)
        glu[pl.ds(b * BLOCK, BLOCK), cols] = (value * jnp.tanh(gate) + value).astype(BF16)

    row_copy(0).start()
    for c in range(columns):
        for copy in column_copies(c):
            copy.start()
        if c + 1 < blocks:
            row_copy(c + 1).start()
    for b in range(columns + 1, blocks):
        row_copy(b).start()
    row_copy(0).wait()
    normalize(0)
    for c in range(columns):
        for copy in column_copies(c):
            copy.wait()
        gated(0, c)

    @pl.loop(1, blocks)
    def _(b):
        row_copy(b).wait()
        normalize(b)
        for c in range(columns):
            gated(b, c)


def run_fast_glu(frames, gain, w_value, w_gate):
    count, width = frames.shape
    channels = w_value.shape[1]
    return pl.pallas_call(
        fast_glu_kernel,
        in_specs=[ANY_SPEC, VMEM_SPEC, ANY_SPEC, ANY_SPEC],
        out_specs=VMEM_SPEC,
        out_shape=jax.ShapeDtypeStruct((count, channels), BF16),
        scratch_shapes=[
            pltpu.VMEM((count, width), BF16),
            pltpu.VMEM((width, channels), BF16),
            pltpu.VMEM((width, channels), BF16),
            pltpu.VMEM((BLOCK, width), BF16),
            pltpu.SemaphoreType.DMA((count // BLOCK,)),
            pltpu.SemaphoreType.DMA((2, channels // BLOCK)),
        ],
        compiler_params=pltpu.CompilerParams(vmem_limit_bytes=14 << 20),
        cost_estimate=cost(4 * count * width * channels, 12 << 20),
        name="glu",
    )(in_hbm(frames), gain, in_hbm(w_value), in_hbm(w_gate))


def fast_conv_kernel(s, token, glu, before, after, taps, scale, shift, starts, ends, act, pooled, xs, *, plan, taps_n):
    count, channels = glu.shape
    tiles = channels // LANES
    outer = BLOCK + HALO

    @pl.loop(0, tiles)
    def _(t):
        lanes = pl.ds(pl.multiple_of(t * LANES, LANES), LANES)
        half_scale = 0.5 * scale[:, lanes]
        half_shift = 0.5 * shift[:, lanes]
        tap = [
            jnp.broadcast_to((taps[k : k + 1, lanes] * half_scale).astype(BF16), (16, LANES))
            for k in range(taps_n)
        ]
        for inner, source, place in plan:
            source = pl.multiple_of(s[source], BLOCK)
            place = pl.multiple_of(s[place], BLOCK)
            if inner:
                rows = pl.ds(pl.multiple_of(source - HALO, HALO), BLOCK + 2 * HALO)
                xs[...] = glu[rows, lanes].astype(F32)
            else:

                @pl.when(source == 0)
                def _():
                    xs[0:HALO, :] = before[:, lanes].astype(F32)
                    xs[HALO:, :] = glu[0:outer, lanes].astype(F32)

                @pl.when(source != 0)
                def _():
                    xs[0:outer, :] = glu[count - outer : count, lanes].astype(F32)
                    xs[outer:, :] = after[:, lanes].astype(F32)

            sums = {}

            def add(block, k, product):
                key = (block, k // 8)
                sums[key] = sums[key] + product if key in sums else product

            for m in range(BLOCK // 16 + 1):
                for r in range(16):
                    if m == BLOCK // 16 and r + 16 >= taps_n:
                        continue
                    shifted = xs[pl.ds(16 * m + r + 1, 16), :].astype(BF16)
                    if m < BLOCK // 16:
                        add(m, r, tap[r] * shifted)
                    if m > 0 and r + 16 < taps_n:
                        add(m - 1, r + 16, tap[r + 16] * shifted)
                if m > 0:
                    total = half_shift
                    for q in range(pl.cdiv(taps_n, 8)):
                        total = total + sums.pop((m - 1, q)).astype(F32)
                    rows = pl.ds(place + 16 * (m - 1), 16)
                    act[rows, lanes] = (total * jnp.tanh(total) + total).astype(BF16)

    total = None
    for inner, source, place in plan:
        mask = segment_mask(s[source], BLOCK, starts[...], ends[...]).astype(F32).astype(BF16)
        rows = pl.ds(pl.multiple_of(s[place], BLOCK), BLOCK)
        part = jnp.dot(mask, act[rows, :], preferred_element_type=F32)
        total = part if total is None else total + part
    pooled[...] = total


def run_fast_conv(
    scalars, plan, rows, glu, before, after, taps, scale, shift, starts, ends, token=None
):
    token = jnp.zeros((8, LANES), F32) if token is None else token
    channels = glu.shape[1]
    segs = starts.shape[0]
    return pl.pallas_call(
        functools.partial(fast_conv_kernel, plan=plan, taps_n=taps.shape[0]),
        in_specs=[SMEM_SPEC, pl.BlockSpec(memory_space=pl.ANY)] + [VMEM_SPEC] * 8,
        out_specs=[VMEM_SPEC, VMEM_SPEC],
        out_shape=[
            jax.ShapeDtypeStruct((rows, channels), BF16),
            jax.ShapeDtypeStruct((segs, channels), F32),
        ],
        scratch_shapes=[pltpu.VMEM((BLOCK + 2 * HALO, LANES), F32)],
        compiler_params=SMALL,
        cost_estimate=cost(rows * channels * 2000, 1 << 20),
        name="conv",
    )(scalars, token, glu, before, after, taps, scale, shift, starts, ends)


def fast_logits_kernel(s, frames, pooled_a, pooled_b, pooled_c, w_out, w_classes, starts, ends, out, buf, sem):
    own_rows = buf.shape[0]
    channels = pooled_a.shape[1]
    first = pl.multiple_of(s[0], own_rows)
    copy = pltpu.make_async_copy(frames.at[pl.ds(first, own_rows), :], buf, sem)
    copy.start()
    pooled = (pooled_a[...] + pooled_b[...] + pooled_c[...]).astype(BF16)
    mine = w_out[pl.ds(pl.multiple_of(s[1], channels), channels), :]
    total = jnp.dot(pooled, mine, preferred_element_type=F32)
    mask = segment_mask(first, own_rows, starts[...], ends[...]).astype(F32).astype(BF16)
    copy.wait()
    total = total + jnp.dot(mask, buf[...], preferred_element_type=F32)
    inverse = 1.0 / (ends[...] - starts[...]).astype(F32)
    out[...] = jnp.dot((total * inverse).astype(BF16), w_classes[...], preferred_element_type=F32)


def run_fast_logits(scalars, own_rows, frames, pooled, w_out, w_classes, starts, ends):
    segs = starts.shape[0]
    width, classes = w_classes.shape
    return pl.pallas_call(
        fast_logits_kernel,
        in_specs=[SMEM_SPEC, ANY_SPEC] + [VMEM_SPEC] * 7,
        out_specs=VMEM_SPEC,
        out_shape=jax.ShapeDtypeStruct((segs, classes), F32),
        scratch_shapes=[pltpu.VMEM((own_rows, width), BF16), pltpu.SemaphoreType.DMA(())],
        compiler_params=SMALL,
        cost_estimate=cost(1 << 30, 4 << 20),
        name="logits",
    )(scalars, in_hbm(frames), *pooled, w_out, w_classes, starts, ends)


def fast_out_kernel(s, frames, inner, outer, got, w_out, out, buf, sem, out_sem):
    rows, width = buf.shape
    channels = inner.shape[1]
    first = pl.multiple_of(s[0], BLOCK)
    mine = pl.ds(pl.multiple_of(s[3], channels), channels)
    theirs = pl.ds(pl.multiple_of(s[4], channels), channels)
    copy = pltpu.make_async_copy(frames.at[pl.ds(first, rows), :], buf, sem)
    copy.start()
    pieces = [(inner, b * BLOCK, s[1] + b * BLOCK) for b in range(inner.shape[0] // BLOCK)]
    pieces += [(outer, b * BLOCK, s[2] + b * BLOCK) for b in range(outer.shape[0] // BLOCK)]
    copies = []
    for n, (source, at, place) in enumerate(pieces):
        place = pl.ds(pl.multiple_of(place, BLOCK), BLOCK)
        total = jnp.dot(
            source[at : at + BLOCK, :], w_out[mine, :], preferred_element_type=F32
        ) + jnp.dot(got[place, :], w_out[theirs, :], preferred_element_type=F32)
        if n == 0:
            copy.wait()
        buf[place, :] = (total + buf[place, :].astype(F32)).astype(BF16)
        copies.append(pltpu.make_async_copy(buf.at[place, :], out.at[place, :], out_sem.at[n]))
        copies[-1].start()
    for copy in copies:
        copy.wait()


def run_fast_out(scalars, frames, inner, outer, got, w_out):
    rows = got.shape[0]
    width = frames.shape[1]
    return pl.pallas_call(
        fast_out_kernel,
        in_specs=[SMEM_SPEC, ANY_SPEC] + [VMEM_SPEC] * 4,
        out_specs=ANY_SPEC,
        out_shape=jax.ShapeDtypeStruct((rows, width), BF16),
        scratch_shapes=[
            pltpu.VMEM((rows, width), BF16),
            pltpu.SemaphoreType.DMA(()),
            pltpu.SemaphoreType.DMA((rows // BLOCK,)),
        ],
        compiler_params=SMALL,
        cost_estimate=cost(4 * rows * width * inner.shape[1], 4 << 20),
        name="block_out",
    )(scalars, in_hbm(frames), inner, outer, got, w_out)


def tail(logits, owners, silence, tags):
    group_size = lax.axis_size("grp")
    time_size = lax.axis_size("tm")
    group = lax.axis_index("grp")
    time = lax.axis_index("tm")
    segs = logits.shape[0]
    order = jnp.arange(segs, dtype=jnp.int32)

    bit = group_size // 2
    while bit:
        half = logits.shape[1] // 2
        upper = (group // bit) % 2
        kept = lax.dynamic_slice_in_dim(logits, upper * half, half, 1)
        sent = lax.dynamic_slice_in_dim(logits, (1 - upper) * half, half, 1)
        logits = kept + swap(sent.astype(BF16), "grp", bit).astype(F32)
        bit //= 2
    classes = logits.shape[1]

    owner_ids = owners[:, 0]
    earlier = order[None, :] < order[:, None]
    slot = jnp.sum(((owner_ids[:, None] == owner_ids[None, :]) & earlier).astype(jnp.int32), axis=1)
    dest = owner_ids * CAP + slot
    slots = time_size * CAP
    placing = (dest[None, :] == jnp.arange(slots, dtype=jnp.int32)[:, None]).astype(BF16)
    rounded = logits.astype(BF16)
    tag_numbers = (tags[0] + 1).astype(BF16)
    pad = jnp.zeros((segs, LANES - 1), BF16)
    labelled = jnp.concatenate([rounded, tag_numbers[:, None], pad], axis=1)
    send = jnp.dot(placing, labelled, preferred_element_type=F32).astype(BF16)
    got = lax.all_to_all(send, "tm", split_axis=0, concat_axis=0, tiled=True)

    tag_ids = jnp.arange(TAGS, dtype=jnp.int32)
    weighted = (tag_ids[:, None] == tags) & (silence > 0)
    sums = jnp.dot(weighted.astype(BF16), rounded, preferred_element_type=F32)
    counts = jnp.sum(weighted.astype(F32), axis=1, keepdims=True)
    counts = jnp.broadcast_to(counts, (TAGS, LANES))

    def exchanged(values, numbers, bit):
        high = jnp.floor(numbers * (1 / 128)) * 128
        lane = lax.broadcasted_iota(jnp.int32, numbers.shape, 1)
        coded = jnp.where(lane == 0, high, numbers - high)
        message = jnp.concatenate([values, coded], axis=1).astype(BF16)
        arrived = swap(message, "tm", bit).astype(F32)
        return arrived[:, :classes], arrived[:, classes : classes + 1] + arrived[:, classes + 1 : classes + 2]

    core = time % 2
    half = TAGS // 2
    sent_sums = lax.dynamic_slice_in_dim(sums, (1 - core) * half, half, 0)
    sent_counts = lax.dynamic_slice_in_dim(counts, (1 - core) * half, half, 0)
    sums = lax.dynamic_slice_in_dim(sums, core * half, half, 0)
    counts = lax.dynamic_slice_in_dim(counts, core * half, half, 0)
    more_sums, more_counts = exchanged(sent_sums, sent_counts, 1)
    sums, counts = sums + more_sums, counts + more_counts
    bit = 2
    while bit < time_size:
        more_sums, more_counts = exchanged(sums, counts, bit)
        sums, counts = sums + more_sums, counts + more_counts
        bit *= 2
    mine = (sums / (counts[:, :1] + 1.0)).astype(BF16)
    theirs = swap(mine, "tm", 1)
    shard_tags = got[:, classes : classes + 1].astype(jnp.int32)
    onehot_mine = (shard_tags == (tag_ids[:half] + core * half + 1)[None, :]).astype(BF16)
    onehot_theirs = (shard_tags == (tag_ids[:half] + (1 - core) * half + 1)[None, :]).astype(BF16)
    calibration = jnp.dot(onehot_mine, mine, preferred_element_type=F32) + jnp.dot(
        onehot_theirs, theirs, preferred_element_type=F32
    )
    scores = got[:, :classes].astype(F32) - calibration
    return scores

SUM_ROWS = TAGS // 2
AUX_ROWS = 16
MESSAGE = SUM_ROWS + AUX_ROWS + 64
SEGS = 128


def as_column(row):
    size = row.shape[1]
    eye = lax.broadcasted_iota(jnp.int32, (size, size), 0) == lax.broadcasted_iota(
        jnp.int32, (size, size), 1
    )
    return jnp.sum(jnp.where(eye, row, jnp.zeros_like(row)), axis=1, keepdims=True)


def iota(shape, dim):
    return lax.broadcasted_iota(jnp.int32, shape, dim)


def to_bf16(mask):
    return mask.astype(F32).astype(BF16)


def labels_kernel(s, after, owners, silence, tags, placing, weighted, aux):
    owner = owners[...]
    square = (SEGS, SEGS)
    same = as_column(owner) == owner
    slot_row = jnp.sum(jnp.where(same & (iota(square, 0) < iota(square, 1)), 1, 0), axis=0, keepdims=True)
    slot_column = jnp.sum(jnp.where(same & (iota(square, 1) < iota(square, 0)), 1, 0), axis=1, keepdims=True)
    placing[...] = to_bf16(iota(square, 0) == owner * CAP + slot_row)
    chosen = (iota((TAGS, SEGS), 0) == tags[...]) & (silence[...] > 0)
    weighted[...] = to_bf16(chosen)
    named = jnp.where(iota((AUX_ROWS, SEGS), 0) == owner, tags[...] + 1, 0).astype(F32).astype(BF16)
    lane = to_bf16(iota(square, 1) == slot_column + s[0] * CAP)
    aux[:, 0:SEGS] = jnp.dot(named, lane, preferred_element_type=F32)
    silent = jnp.where(silence[...] > 0, 1.0, 0.0)
    ones = jnp.broadcast_to(silent, (8, SEGS)).astype(BF16)
    columns = as_column(tags[...])
    aux[:, SEGS:] = jnp.zeros((AUX_ROWS, SEGS), F32)
    for h in range(2):
        match = to_bf16(columns == iota((SEGS, SUM_ROWS), 1) + h * SUM_ROWS)
        count = jnp.dot(ones, match, preferred_element_type=F32)
        aux[2 + h : 3 + h, SEGS:] = count[0:1, :]


def picked(have, bit):
    rows, columns = iota((64, SEGS), 0), iota((64, SEGS), 1)
    chosen = columns == (rows // 8) * 16 + bit * 8 + rows % 8
    return jnp.dot(to_bf16(chosen), have, preferred_element_type=F32).astype(BF16)


def send_parts(message, keep, aux, sums, totals, have, bit):
    counts = aux[0:2, SEGS:] + aux[2:4, SEGS:]
    high = jnp.floor(counts * (1 / 128)) * 128
    totals[...] = aux
    totals[0:2, SEGS:] = high
    totals[2:4, SEGS:] = counts - high
    message[0:SUM_ROWS, :] = sums.astype(BF16)
    message[SUM_ROWS : SUM_ROWS + AUX_ROWS, :] = totals[...].astype(BF16)
    message[SUM_ROWS + AUX_ROWS :, :] = picked(have, 1 - bit)
    keep[...] = picked(have, bit)


def first_kernel(s, logits, got, placing, weighted, aux, message, sums, totals, keep):
    core = s[0]
    classes = got.shape[1]
    mine = logits[:, pl.ds(pl.multiple_of(s[1] * classes, classes), classes)]
    rounded = (mine + got[...].astype(F32)).astype(BF16)
    have = jnp.dot(placing[...], rounded, preferred_element_type=F32).astype(BF16)
    kept = weighted[pl.ds(pl.multiple_of(core * SUM_ROWS, SUM_ROWS), SUM_ROWS), :]
    sent = weighted[pl.ds(pl.multiple_of((1 - core) * SUM_ROWS, SUM_ROWS), SUM_ROWS), :]
    sums[...] = jnp.dot(kept, rounded, preferred_element_type=F32)
    sent = jnp.dot(sent, rounded, preferred_element_type=F32)
    send_parts(message, keep, aux[...], sent, totals, have, core)


def merged(s, arrived, sums, totals, keep, have):
    bit = s[0]
    have[pl.ds(pl.multiple_of(bit * 64, 64), 64), :] = keep[...]
    have[pl.ds(pl.multiple_of((1 - bit) * 64, 64), 64), :] = arrived[SUM_ROWS + AUX_ROWS :, :]
    total = sums[...] + arrived[0:SUM_ROWS, :].astype(F32)
    aux = totals[...] + arrived[SUM_ROWS : SUM_ROWS + AUX_ROWS, :].astype(F32)
    return total, aux


def middle_kernel(s, arrived, sums, totals, keep, message, sums_out, totals_out, keep_out, have):
    total, aux = merged(s, arrived, sums, totals, keep, have)
    sums_out[...] = total
    send_parts(message, keep_out, aux, total, totals_out, have[...], s[1])


def last_kernel(s, after, arrived, sums, totals, keep, calibration, table, have):
    total, aux = merged(s, arrived, sums, totals, keep, have)
    table[...] = aux
    both = aux[0:2, SEGS:] + aux[2:4, SEGS:]
    counts = jnp.where(s[1] == 0, both[0:1, :], both[1:2, :])
    calibration[...] = (total / (as_column(counts) + 1.0)).astype(BF16)


def scores_kernel(s, mine, theirs, table, have, scores):
    named = jnp.where(iota((AUX_ROWS, SEGS), 0) == s[0], table[:, 0:SEGS], 0.0)
    row = jnp.sum(named, axis=0, keepdims=True).astype(jnp.int32)
    column = as_column(row)
    ids = iota((SEGS, SUM_ROWS), 1) + 1
    near = to_bf16(column == ids + s[1] * SUM_ROWS)
    far = to_bf16(column == ids + (1 - s[1]) * SUM_ROWS)
    scores[...] = (
        have[...].astype(F32)
        - jnp.dot(near, mine[...], preferred_element_type=F32)
        - jnp.dot(far, theirs[...], preferred_element_type=F32)
    )


def small_call(kernel, name, scalars, operands, outs, scratch=(), hbm=0):
    return pl.pallas_call(
        kernel,
        in_specs=[SMEM_SPEC] + [ANY_SPEC] * hbm + [VMEM_SPEC] * (len(operands) - hbm),
        out_specs=[VMEM_SPEC] * len(outs),
        out_shape=[jax.ShapeDtypeStruct(*o) for o in outs],
        scratch_shapes=list(scratch),
        compiler_params=SMALL,
        cost_estimate=cost(1 << 24, 1 << 20),
        name=name,
    )(jnp.stack(scalars).astype(jnp.int32), *operands)


def fast_tail(logits, owners, silence, tags, block_out):
    group = lax.axis_index("grp")
    time = lax.axis_index("tm")
    classes = logits.shape[1] // 2
    sent = lax.dynamic_slice_in_dim(logits, (1 - group) * classes, classes, 1)
    got = swap(sent.astype(BF16), "grp", 1)
    sums = ((SUM_ROWS, classes), F32)
    aux = ((AUX_ROWS, 2 * SEGS), F32)
    keep = ((64, classes), BF16)
    message = ((MESSAGE, classes), BF16)
    have = (pltpu.VMEM((SEGS, classes), BF16),)
    placing, weighted, labels = small_call(
        labels_kernel,
        "labels",
        [time],
        [in_hbm(logits), owners[:, 0][None, :], silence, tags],
        [((SEGS, SEGS), BF16), ((TAGS, SEGS), BF16), aux],
        hbm=1,
    )
    bits = [(time >> b) & 1 for b in range(4)]
    state = small_call(
        first_kernel,
        "first",
        [bits[0], group],
        [logits, got, placing, weighted, labels],
        [message, sums, aux, keep],
    )
    for b in range(3):
        arrived = swap(state[0], "tm", 1 << b)
        state = small_call(
            middle_kernel,
            "middle",
            [bits[b], bits[b + 1]],
            [arrived, *state[1:]],
            [message, sums, aux, keep],
            have,
        )
    arrived = swap(state[0], "tm", 8)
    block_rows = block_out()
    calibration, table, ready = small_call(
        last_kernel,
        "last",
        [bits[3], bits[0]],
        [in_hbm(block_rows), arrived, *state[1:]],
        [((SUM_ROWS, classes), BF16), aux, ((SEGS, classes), BF16)],
        hbm=1,
    )
    theirs = swap(calibration, "tm", 1)
    [scores] = small_call(
        scores_kernel,
        "scores",
        [time, bits[0]],
        [calibration, theirs, table, ready],
        [((SEGS, classes), F32)],
    )
    return block_rows, scores


def fast_body(
    frames,
    ln_gain,
    w_value,
    w_gate,
    conv_taps,
    bn_scale,
    bn_shift,
    w_out,
    w_classes,
    seg_lengths,
    owners,
    silence,
    tags,
):
    count, width = frames.shape
    channels = w_value.shape[1]
    group = lax.axis_index("grp").astype(jnp.int32)
    time_size = lax.axis_size("tm")
    own_rows = count // 2
    lengths = seg_lengths[0]
    segs = lengths.shape[0]
    order = jnp.arange(segs, dtype=jnp.int32)
    ends = jnp.sum(
        jnp.where(order[None, :] <= order[:, None], lengths[None, :], 0), axis=1, keepdims=True
    )
    starts = ends - lengths[:, None]

    glu = run_fast_glu(frames, ln_gain[None, :], w_value, w_gate)
    up = [(i, i + 1) for i in range(time_size - 1)]
    down = [(j, i) for i, j in up]
    before = lax.ppermute(glu[count - HALO :], "tm", up)
    after = lax.ppermute(glu[:HALO], "tm", down)
    bn = (conv_taps, bn_scale[None, :], bn_shift[None, :], starts, ends)

    last = count - BLOCK
    inner_rows = own_rows - BLOCK
    own_inner = jnp.where(group == 0, BLOCK, own_rows)
    own_outer = jnp.where(group == 0, 0, last)
    other_inner = jnp.where(group == 0, own_rows, BLOCK)
    other_outer = jnp.where(group == 0, last, 0)
    inner_at = jnp.where(group == 0, BLOCK, 0)
    outer_at = jnp.where(group == 0, 0, inner_rows)
    other_inner_at = jnp.where(group == 0, 0, BLOCK)
    other_outer_at = jnp.where(group == 0, inner_rows, 0)
    blocks = inner_rows // BLOCK
    zero = jnp.zeros((), jnp.int32)

    steps = [b * BLOCK for b in range(blocks)]
    edge = jnp.zeros((HALO, channels), BF16)
    inner_plan = [(True, b, blocks + b) for b in range(blocks)]
    scalars = jnp.stack([own_inner + b for b in steps] + [zero + b for b in steps])
    act_inner, pooled_inner = run_fast_conv(scalars, inner_plan, inner_rows, glu, edge, edge, *bn)
    plan = inner_plan + [(False, 2 * blocks, 2 * blocks + 1)]
    scalars = jnp.stack(
        [other_inner + b for b in steps]
        + [other_inner_at + b for b in steps]
        + [other_outer, other_outer_at]
    )
    act_other, pooled_other = run_fast_conv(
        scalars, plan, own_rows, glu, before, after, *bn, token=pooled_inner
    )
    act_got = swap(act_other, "grp", 1)
    scalars = jnp.stack([own_outer, zero])
    act_outer, pooled_outer = run_fast_conv(
        scalars, [(False, 0, 1)], BLOCK, glu, before, after, *bn, token=pooled_other
    )

    mine, theirs = group * channels, (1 - group) * channels
    logits = run_fast_logits(
        jnp.stack([group * own_rows, mine]),
        own_rows,
        frames,
        (pooled_inner, pooled_outer, pooled_other),
        w_out,
        w_classes,
        starts,
        ends,
    )

    def block_out():
        scalars = jnp.stack([group * own_rows, inner_at, outer_at, mine, theirs])
        return run_fast_out(scalars, frames, act_inner, act_outer, act_got, w_out)

    block_rows, scores = fast_tail(logits, owners, silence, tags, block_out)
    return (block_rows[None, None], scores)


def body(*args):
    rows = args[0].shape[0] // lax.axis_size("grp")
    channels = args[2].shape[1]
    fits = rows % BLOCK == 0 and rows > BLOCK and channels % BLOCK == 0
    fits = fits and lax.axis_size("grp") == 2 and lax.axis_size("tm") == 16
    fits = fits and args[4].shape[0] == 31 and args[8].shape[1] == 512 and args[9].shape[1] == SEGS
    return (fast_body if fits else general_body)(*args)


def solution(mesh):
    in_specs = (
        P("tm", None),
        P(),
        P(None, "grp"),
        P(None, "grp"),
        P(None, "grp"),
        P("grp"),
        P("grp"),
        P(),
        P(),
        P("tm", None),
        P("tm", None),
        P("tm", None),
        P("tm", None),
    )
    out_specs = (P("tm", "grp", None, None), P("tm", "grp"))
    return jax.shard_map(body, mesh=mesh, in_specs=in_specs, out_specs=out_specs, check_vma=False)
```

```python
import functools

import jax
import jax.numpy as jnp
from jax import lax
from jax.experimental import pallas as pl
from jax.experimental.pallas import tpu as pltpu
from jax.sharding import PartitionSpec as P

TAGS = 256
CAP = 8
HALO = 16
BLOCK = 256
LANES = 128
VMEM_LIMIT = 48 << 20
F32, BF16 = jnp.float32, jnp.bfloat16


def sigmoid(v):
    return 0.5 * jnp.tanh(0.5 * v) + 0.5


def params():
    return pltpu.CompilerParams(
        dimension_semantics=("arbitrary",), vmem_limit_bytes=VMEM_LIMIT
    )


def whole(shape):
    return pl.BlockSpec(shape, lambda i, s: (0,) * len(shape))


def segment_mask(first, count, starts, ends):
    rows = first + lax.broadcasted_iota(jnp.int32, (starts.shape[0], count), 1)
    return (rows >= starts) & (rows < ends)


def glu_kernel(s, frames, gain, w_value, w_gate, starts, ends, glu, pooled, *, own_rows):
    step = pl.program_id(0)
    block = frames.shape[0]
    own_first = s[0] * own_rows

    @pl.when(step == 0)
    def _():
        pooled[...] = jnp.zeros_like(pooled)

    first = step * block

    @pl.when((first < own_first + own_rows) & (first + block > own_first))
    def _():
        rows = first + lax.broadcasted_iota(jnp.int32, (starts.shape[0], block), 1)
        low = jnp.maximum(starts[...], own_first)
        high = jnp.minimum(ends[...], own_first + own_rows)
        mask = ((rows >= low) & (rows < high)).astype(F32).astype(BF16)
        pooled[...] += jnp.dot(mask, frames[...], preferred_element_type=F32)

    half = block // 2
    for part in range(2):
        rows = pl.ds(part * half, half)
        x = frames[rows, :].astype(F32)
        center = jnp.mean(x, axis=-1, keepdims=True)
        x = x - center
        spread = jnp.mean(x * x, axis=-1, keepdims=True)
        normed = (x * lax.rsqrt(spread + 1e-05) * gain[...]).astype(BF16)
        value = jnp.dot(normed, w_value[...], preferred_element_type=F32)
        gate = jnp.dot(normed, w_gate[...], preferred_element_type=F32)
        glu[rows, :] = (value * sigmoid(gate)).astype(BF16)


def conv_kernel(s, window, taps, scale, shift, starts, ends, act, pooled, xs, *, taps_n):
    step = pl.program_id(0)
    block, channels = act.shape
    tiles = [(c, min(LANES, channels - c)) for c in range(0, channels, LANES)]
    for t, (c, w) in enumerate(tiles):
        xs[t, :, 0:w] = window[:, c : c + w].astype(F32)

    def tile(t, c, w):
        lanes = pl.ds(c, w)
        for r in range(0, block, 64):
            total = jnp.zeros((64, w), F32)
            for k in range(taps_n):
                total = total + taps[k : k + 1, lanes] * xs[t, pl.ds(r + 1 + k, 64), 0:w]
            v = total * scale[:, lanes] + shift[:, lanes]
            act[pl.ds(r, 64), lanes] = (v * sigmoid(v)).astype(BF16)

    if channels % LANES == 0:

        @pl.loop(0, channels // LANES)
        def _(t):
            tile(t, pl.multiple_of(t * LANES, LANES), LANES)
    else:
        for t, (c, w) in enumerate(tiles):
            tile(t, c, w)

    first = s[0] + step * block
    mask = segment_mask(first, block, starts[...], ends[...]).astype(F32).astype(BF16)
    part = jnp.dot(mask, act[...], preferred_element_type=F32)

    @pl.when(step == 0)
    def _():
        pooled[...] = part

    @pl.when(step > 0)
    def _():
        pooled[...] += part


def logits_kernel(s, frames_pooled, pooled, w_out, w_classes, starts, ends, out):
    mixed = jnp.dot(pooled[...].astype(BF16), w_out[...], preferred_element_type=F32)
    inverse = 1.0 / (ends[...] - starts[...]).astype(F32)
    mean = ((frames_pooled[...] + mixed) * inverse).astype(BF16)
    out[...] = jnp.dot(mean, w_classes[...], preferred_element_type=F32)


def out_kernel(s, *refs):
    *pairs, frames, out = refs
    total = frames[...].astype(F32)
    for act, w_out in zip(pairs[0::2], pairs[1::2]):
        total = total + jnp.dot(act[...], w_out[...], preferred_element_type=F32)
    out[...] = total.astype(BF16)


def run_glu(group_index, own_rows, frames, gain, w_value, w_gate, starts, ends):
    count, width = frames.shape
    channels = w_value.shape[1]
    segs = starts.shape[0]
    return pl.pallas_call(
        functools.partial(glu_kernel, own_rows=own_rows),
        grid_spec=pltpu.PrefetchScalarGridSpec(
            num_scalar_prefetch=1,
            grid=(count // BLOCK,),
            in_specs=[
                pl.BlockSpec((BLOCK, width), lambda i, s: (i, 0)),
                whole((1, width)),
                whole((width, channels)),
                whole((width, channels)),
                whole((segs, 1)),
                whole((segs, 1)),
            ],
            out_specs=[
                pl.BlockSpec((BLOCK, channels), lambda i, s: (i, 0)),
                whole((segs, width)),
            ],
        ),
        out_shape=[
            jax.ShapeDtypeStruct((count, channels), BF16),
            jax.ShapeDtypeStruct((segs, width), F32),
        ],
        compiler_params=params(),
        name="glu",
    )(group_index, frames, gain, w_value, w_gate, starts, ends)


def run_conv(base, rows, padded, taps, scale, shift, starts, ends):
    channels = padded.shape[1]
    segs = starts.shape[0]
    tiles = pl.cdiv(channels, LANES)
    return pl.pallas_call(
        functools.partial(conv_kernel, taps_n=taps.shape[0]),
        grid_spec=pltpu.PrefetchScalarGridSpec(
            num_scalar_prefetch=1,
            grid=(rows // BLOCK,),
            in_specs=[
                pl.BlockSpec(
                    (pl.Element(BLOCK + 2 * HALO), pl.Element(channels)),
                    lambda i, s: (pl.multiple_of(s[0] + i * BLOCK, HALO), 0),
                ),
                whole(taps.shape),
                whole((1, channels)),
                whole((1, channels)),
                whole((segs, 1)),
                whole((segs, 1)),
            ],
            out_specs=[
                pl.BlockSpec((BLOCK, channels), lambda i, s: (i, 0)),
                whole((segs, channels)),
            ],
            scratch_shapes=[pltpu.VMEM((tiles, BLOCK + 2 * HALO, LANES), F32)],
        ),
        out_shape=[
            jax.ShapeDtypeStruct((rows, channels), BF16),
            jax.ShapeDtypeStruct((segs, channels), F32),
        ],
        compiler_params=params(),
        name="conv",
    )(base, padded, taps, scale, shift, starts, ends)


def run_logits(group_index, frames_pooled, pooled, w_out, w_classes, starts, ends):
    segs, channels = pooled.shape
    width, classes = w_classes.shape
    return pl.pallas_call(
        logits_kernel,
        grid_spec=pltpu.PrefetchScalarGridSpec(
            num_scalar_prefetch=1,
            grid=(1,),
            in_specs=[
                whole((segs, width)),
                whole((segs, channels)),
                pl.BlockSpec((channels, width), lambda i, s: (s[0], 0)),
                whole((width, classes)),
                whole((segs, 1)),
                whole((segs, 1)),
            ],
            out_specs=whole((segs, classes)),
        ),
        out_shape=jax.ShapeDtypeStruct((segs, classes), F32),
        compiler_params=params(),
        name="logits",
    )(group_index, frames_pooled, pooled, w_out, w_classes, starts, ends)


def run_out(scalars, sources, w_out, frames, rows):
    width = frames.shape[1]
    block = BLOCK if rows % BLOCK == 0 else rows
    steps = rows // block
    in_specs, operands = [], []
    for act, place in sources:
        in_specs.append(pl.BlockSpec((block, act.shape[1]), lambda i, s: (i, 0)))
        in_specs.append(
            pl.BlockSpec((act.shape[1], width), functools.partial(lambda p, i, s: (s[p], 0), place))
        )
        operands += [act, w_out]
    in_specs.append(pl.BlockSpec((block, width), lambda i, s: (s[0] * steps + i, 0)))
    return pl.pallas_call(
        out_kernel,
        grid_spec=pltpu.PrefetchScalarGridSpec(
            num_scalar_prefetch=1,
            grid=(steps,),
            in_specs=in_specs,
            out_specs=pl.BlockSpec((block, width), lambda i, s: (i, 0)),
        ),
        out_shape=jax.ShapeDtypeStruct((rows, width), BF16),
        compiler_params=params(),
        name="block_out",
    )(scalars, *operands, frames)


def swap(value, axis, bit):
    count = lax.axis_size(axis)
    return lax.ppermute(value, axis, [(i, i ^ bit) for i in range(count)])


def general_body(
    frames,
    ln_gain,
    w_value,
    w_gate,
    conv_taps,
    bn_scale,
    bn_shift,
    w_out,
    w_classes,
    seg_lengths,
    owners,
    silence,
    tags,
):
    count, width = frames.shape
    channels = w_value.shape[1]
    group_size = lax.axis_size("grp")
    time_size = lax.axis_size("tm")
    group = lax.axis_index("grp")
    time = lax.axis_index("tm")
    own_rows = count // group_size
    lengths = seg_lengths[0]
    segs = lengths.shape[0]
    order = jnp.arange(segs, dtype=jnp.int32)
    ends = jnp.sum(
        jnp.where(order[None, :] <= order[:, None], lengths[None, :], 0), axis=1, keepdims=True
    )
    starts = ends - lengths[:, None]
    group_scalar = group[None].astype(jnp.int32)

    glu, frames_pooled = run_glu(
        group_scalar, own_rows, frames, ln_gain[None, :], w_value, w_gate, starts, ends
    )
    up = [(i, i + 1) for i in range(time_size - 1)]
    down = [(j, i) for i, j in up]
    before = lax.ppermute(glu[count - HALO :], "tm", up)
    after = lax.ppermute(glu[:HALO], "tm", down)
    padded = jnp.concatenate([before, glu, after], axis=0)
    bn = (conv_taps, bn_scale[None, :], bn_shift[None, :], starts, ends)

    if group_size == 2:
        other = 1 - group_scalar
        act_other, pooled_other = run_conv(other * own_rows, own_rows, padded, *bn)
        act_got = swap(act_other, "grp", 1)
        act_own, pooled_own = run_conv(group_scalar * own_rows, own_rows, padded, *bn)
        pooled = pooled_other + pooled_own
        sources = [(act_own, 0), (act_got, 1)]
        scalars = jnp.concatenate([group_scalar, other])
    else:
        act, pooled = run_conv(jnp.zeros((1,), jnp.int32), count, padded, *bn)
        rows = lax.all_to_all(act, "grp", split_axis=0, concat_axis=1, tiled=True)
        sources = [(rows, 1)]
        scalars = jnp.concatenate([group_scalar, jnp.zeros((1,), jnp.int32)])

    logits = run_logits(group_scalar, frames_pooled, pooled, w_out, w_classes, starts, ends)

    scores = tail(logits, owners, silence, tags)

    block_rows = run_out(scalars, sources, w_out, frames, own_rows)
    return (block_rows[None, None], scores)


def in_hbm(value):
    return pltpu.with_memory_space_constraint(value, pltpu.HBM)


def cost(flops, traffic):
    return pl.CostEstimate(flops=flops, bytes_accessed=traffic, transcendentals=0)


VMEM_SPEC = pl.BlockSpec(memory_space=pltpu.VMEM)
SMEM_SPEC = pl.BlockSpec(memory_space=pltpu.SMEM)
ANY_SPEC = pl.BlockSpec(memory_space=pltpu.HBM)
SMALL = pltpu.CompilerParams(vmem_limit_bytes=8 << 20)


def fast_glu_kernel(frames, gain, w_value, w_gate, glu, rows_in, wv, wg, normed, row_sem, col_sem):
    count, width = frames.shape
    channels = wv.shape[1]
    blocks = count // BLOCK
    columns = channels // BLOCK

    def row_copy(b):
        rows = pl.ds(b * BLOCK, BLOCK)
        return pltpu.make_async_copy(frames.at[rows, :], rows_in.at[rows, :], row_sem.at[b])

    def column_copies(c):
        cols = pl.ds(c * BLOCK, BLOCK)
        return (
            pltpu.make_async_copy(w_value.at[:, cols], wv.at[:, cols], col_sem.at[0, c]),
            pltpu.make_async_copy(w_gate.at[:, cols], wg.at[:, cols], col_sem.at[1, c]),
        )

    def normalize(b):
        rows = pl.ds(b * BLOCK, BLOCK)
        x = rows_in[rows, :].astype(F32)
        center = jnp.mean(x, axis=-1, keepdims=True)
        x = x - center
        spread = jnp.mean(x * x, axis=-1, keepdims=True)
        normed[...] = (x * (0.5 * lax.rsqrt(spread + 1e-05)) * gain[...].reshape(1, -1)).astype(BF16)

    def gated(b, c):
        cols = pl.ds(c * BLOCK, BLOCK)
        value = jnp.dot(normed[...], wv[:, cols], preferred_element_type=F32)
        gate = jnp.dot(normed[...], wg[:, cols], preferred_element_type=F32)
        glu[pl.ds(b * BLOCK, BLOCK), cols] = (value * jnp.tanh(gate) + value).astype(BF16)

    row_copy(0).start()
    for c in range(columns):
        for copy in column_copies(c):
            copy.start()
    for b in range(1, blocks):
        row_copy(b).start()
    row_copy(0).wait()
    normalize(0)
    for c in range(columns):
        for copy in column_copies(c):
            copy.wait()
        gated(0, c)

    @pl.loop(1, blocks)
    def _(b):
        row_copy(b).wait()
        normalize(b)
        for c in range(columns):
            gated(b, c)


def run_fast_glu(frames, gain, w_value, w_gate):
    count, width = frames.shape
    channels = w_value.shape[1]
    return pl.pallas_call(
        fast_glu_kernel,
        in_specs=[ANY_SPEC, VMEM_SPEC, ANY_SPEC, ANY_SPEC],
        out_specs=VMEM_SPEC,
        out_shape=jax.ShapeDtypeStruct((count, channels), BF16),
        scratch_shapes=[
            pltpu.VMEM((count, width), BF16),
            pltpu.VMEM((width, channels), BF16),
            pltpu.VMEM((width, channels), BF16),
            pltpu.VMEM((BLOCK, width), BF16),
            pltpu.SemaphoreType.DMA((count // BLOCK,)),
            pltpu.SemaphoreType.DMA((2, channels // BLOCK)),
        ],
        compiler_params=pltpu.CompilerParams(vmem_limit_bytes=14 << 20),
        cost_estimate=cost(4 * count * width * channels, 12 << 20),
        name="glu",
    )(in_hbm(frames), gain, in_hbm(w_value), in_hbm(w_gate))


def segment_bounds(lengths):
    row = lengths[...]
    size = row.shape[1]
    earlier = iota((size, size), 1) <= iota((size, size), 0)
    ends = jnp.sum(jnp.where(earlier, row, 0), axis=1, keepdims=True)
    return ends - as_column(row), ends


def half_places(count, group):
    own = count // 2
    last = count - BLOCK
    return (
        jnp.where(group == 0, BLOCK, own),
        jnp.where(group == 0, 0, last),
        jnp.where(group == 0, BLOCK, 0),
        jnp.where(group == 0, 0, own - BLOCK),
    )


def convolve(glu, halos, taps, scale, shift, xs, plan):
    count, channels = glu.shape
    taps_n = taps.shape[0]
    outer = BLOCK + HALO

    @pl.loop(0, channels // LANES)
    def _(t):
        lanes = pl.ds(pl.multiple_of(t * LANES, LANES), LANES)
        half_scale = 0.5 * scale[lanes].reshape(1, -1)
        half_shift = 0.5 * shift[lanes].reshape(1, -1)
        tap = [
            jnp.broadcast_to((taps[k : k + 1, lanes] * half_scale).astype(BF16), (16, LANES))
            for k in range(taps_n)
        ]
        for inner, source, act, place in plan:
            source = pl.multiple_of(source, BLOCK)
            if inner:
                rows = pl.ds(pl.multiple_of(source - HALO, HALO), BLOCK + 2 * HALO)
                xs[...] = glu[rows, lanes].astype(F32)
            else:
                near, far = halos
                odd = lax.axis_index("tm") % 2 == 1
                inside = jnp.where(odd, source == 0, source != 0)
                halo = jnp.where(inside, near[:, lanes].astype(F32), far[:, lanes].astype(F32))

                @pl.when(source == 0)
                def _():
                    xs[0:HALO, :] = halo
                    xs[HALO:, :] = glu[0:outer, lanes].astype(F32)

                @pl.when(source != 0)
                def _():
                    xs[0:outer, :] = glu[count - outer : count, lanes].astype(F32)
                    xs[outer:, :] = halo

            sums = {}

            def add(block, k, product):
                key = (block, k // 8)
                sums[key] = sums[key] + product if key in sums else product

            for m in range(BLOCK // 16 + 1):
                for r in range(16):
                    if m == BLOCK // 16 and r + 16 >= taps_n:
                        continue
                    shifted = xs[pl.ds(16 * m + r + 1, 16), :].astype(BF16)
                    if m < BLOCK // 16:
                        add(m, r, tap[r] * shifted)
                    if m > 0 and r + 16 < taps_n:
                        add(m - 1, r + 16, tap[r + 16] * shifted)
                if m > 0:
                    total = half_shift
                    for q in range(pl.cdiv(taps_n, 8)):
                        total = total + sums.pop((m - 1, q)).astype(F32)
                    rows = pl.ds(pl.multiple_of(place + 16 * (m - 1), 16), 16)
                    act[rows, lanes] = (total * jnp.tanh(total) + total).astype(BF16)


def pool(plan, starts, ends):
    total = None
    for inner, source, act, place in plan:
        mask = to_bf16(segment_mask(source, BLOCK, starts, ends))
        rows = pl.ds(pl.multiple_of(place, BLOCK), BLOCK)
        part = jnp.dot(mask, act[rows, :], preferred_element_type=F32)
        total = part if total is None else total + part
    return total


def early_kernel(glu, taps, scale, shift, lengths, act, pooled, xs):
    count = glu.shape[0]
    inner = half_places(count, 1 - lax.axis_index("grp"))[0]
    plan = [(True, inner + b, act, b) for b in range(0, act.shape[0], BLOCK)]
    convolve(glu, None, taps, scale, shift, xs, plan)
    starts, ends = segment_bounds(lengths)
    pooled[...] = pool(plan, starts, ends)


def late_kernel(
    glu, before, after, taps, scale, shift, lengths, pooled, frames, w_out, w_classes,
    act_other, act_own, kept, sent, xs, rows_in, w_mine, w_cls, sem,
):
    count, channels = glu.shape
    group = lax.axis_index("grp")
    own_rows = act_own.shape[0]
    own_first = pl.multiple_of(group * own_rows, own_rows)
    copies = [
        pltpu.make_async_copy(
            w_out.at[pl.ds(pl.multiple_of(group * channels, channels), channels), :], w_mine, sem.at[0]
        ),
        pltpu.make_async_copy(frames.at[pl.ds(own_first, own_rows), :], rows_in, sem.at[1]),
        pltpu.make_async_copy(w_classes, w_cls, sem.at[2]),
    ]
    for copy in copies:
        copy.start()
    inner, outer, inner_at, outer_at = half_places(count, group)
    far_inner, far_outer, _, _ = half_places(count, 1 - group)
    rest = act_other.shape[0] - BLOCK
    plan = [(True, far_inner + BLOCK + b, act_other, b) for b in range(0, rest, BLOCK)]
    plan += [(False, far_outer, act_other, rest)]
    plan += [(True, inner + b, act_own, inner_at + b) for b in range(0, own_rows - BLOCK, BLOCK)]
    plan += [(False, outer, act_own, outer_at)]
    convolve(glu, (before, after), taps, scale, shift, xs, plan)
    starts, ends = segment_bounds(lengths)
    total = (pooled[...] + pool(plan, starts, ends)).astype(BF16)
    for copy in copies:
        copy.wait()
    total = jnp.dot(total, w_mine[...], preferred_element_type=F32)
    mask = to_bf16(segment_mask(own_first, own_rows, starts, ends))
    total = total + jnp.dot(mask, rows_in[...], preferred_element_type=F32)
    inverse = 1.0 / (ends - starts).astype(F32)
    logits = jnp.dot((total * inverse).astype(BF16), w_cls[...], preferred_element_type=F32)
    half = logits.shape[1] // 2
    low, high = logits[:, :half], logits[:, half:]
    kept[...] = jnp.where(group == 0, low, high)
    sent[...] = jnp.where(group == 0, high, low).astype(BF16)


def run_early(rows, glu, taps, scale, shift, lengths):
    channels = glu.shape[1]
    return pl.pallas_call(
        early_kernel,
        in_specs=[VMEM_SPEC] * 5,
        out_specs=[VMEM_SPEC, VMEM_SPEC],
        out_shape=[
            jax.ShapeDtypeStruct((rows, channels), BF16),
            jax.ShapeDtypeStruct((lengths.shape[1], channels), F32),
        ],
        scratch_shapes=[pltpu.VMEM((BLOCK + 2 * HALO, LANES), F32)],
        compiler_params=SMALL,
        cost_estimate=cost(1 << 20, 1 << 16),
        name="conv_early",
    )(glu, taps, scale, shift, lengths)


def run_late(glu, before, after, taps, scale, shift, lengths, pooled, frames, w_out, w_classes):
    count, channels = glu.shape
    segs = lengths.shape[1]
    width, classes = w_classes.shape
    own_rows = count // 2
    return pl.pallas_call(
        late_kernel,
        in_specs=[VMEM_SPEC] * 8 + [ANY_SPEC] * 3,
        out_specs=[VMEM_SPEC] * 4,
        out_shape=[
            jax.ShapeDtypeStruct((own_rows - BLOCK, channels), BF16),
            jax.ShapeDtypeStruct((own_rows, channels), BF16),
            jax.ShapeDtypeStruct((segs, classes // 2), F32),
            jax.ShapeDtypeStruct((segs, classes // 2), BF16),
        ],
        scratch_shapes=[
            pltpu.VMEM((BLOCK + 2 * HALO, LANES), F32),
            pltpu.VMEM((own_rows, width), BF16),
            pltpu.VMEM((channels, width), BF16),
            pltpu.VMEM((width, classes), BF16),
            pltpu.SemaphoreType.DMA((3,)),
        ],
        compiler_params=pltpu.CompilerParams(vmem_limit_bytes=14 << 20),
        cost_estimate=cost(1 << 20, 1 << 16),
        name="conv_late",
    )(
        glu, before, after, taps, scale, shift, lengths, pooled,
        in_hbm(frames), in_hbm(w_out), in_hbm(w_classes),
    )


def rest_places(rows, group):
    _, _, inner_at, outer_at = half_places(2 * rows, group)
    blocks = rows // BLOCK - 2
    places = [inner_at + BLOCK * (b + 1) for b in range(blocks)] + [outer_at]
    return inner_at, places


def half_rows(channels, half):
    return pl.ds(pl.multiple_of(half * channels, channels), channels)


def out_first_kernel(frames, own, got, w_out, out, partial, buf, sem, out_sem):
    rows, width = buf.shape
    channels = own.shape[1]
    group = lax.axis_index("grp")
    copy = pltpu.make_async_copy(
        frames.at[pl.ds(pl.multiple_of(group * rows, rows), rows), :], buf, sem
    )
    copy.start()
    first, rest = rest_places(rows, group)
    mine, theirs = half_rows(channels, group), half_rows(channels, 1 - group)
    place = pl.ds(pl.multiple_of(first, BLOCK), BLOCK)
    total = jnp.dot(own[place, :], w_out[mine, :], preferred_element_type=F32) + jnp.dot(
        got[...], w_out[theirs, :], preferred_element_type=F32
    )
    copy.wait()
    buf[place, :] = (total + buf[place, :].astype(F32)).astype(BF16)
    out_copy = pltpu.make_async_copy(buf.at[place, :], out.at[place, :], out_sem)
    out_copy.start()
    for n, at in enumerate(rest):
        place = pl.ds(pl.multiple_of(at, BLOCK), BLOCK)
        total = jnp.dot(own[place, :], w_out[mine, :], preferred_element_type=F32)
        partial[n * BLOCK : (n + 1) * BLOCK, :] = total + buf[place, :].astype(F32)
    out_copy.wait()


def out_rest_kernel(partial, got, w_out, earlier, out, buf, out_sem):
    rest, width = buf.shape
    channels = got.shape[1]
    group = lax.axis_index("grp")
    theirs = half_rows(channels, 1 - group)
    copies = []
    for n, at in enumerate(rest_places(rest + BLOCK, group)[1]):
        rows = pl.ds(n * BLOCK, BLOCK)
        total = jnp.dot(got[rows, :], w_out[theirs, :], preferred_element_type=F32)
        buf[rows, :] = (total + partial[rows, :]).astype(BF16)
        place = pl.ds(pl.multiple_of(at, BLOCK), BLOCK)
        copies.append(pltpu.make_async_copy(buf.at[rows, :], out.at[place, :], out_sem.at[n]))
        copies[-1].start()
    for copy in copies:
        copy.wait()


def run_out_first(frames, own, got, w_out):
    rows, channels = own.shape
    width = frames.shape[1]
    return pl.pallas_call(
        out_first_kernel,
        in_specs=[ANY_SPEC] + [VMEM_SPEC] * 3,
        out_specs=[ANY_SPEC, VMEM_SPEC],
        out_shape=[
            jax.ShapeDtypeStruct((rows, width), BF16),
            jax.ShapeDtypeStruct((rows - BLOCK, width), F32),
        ],
        scratch_shapes=[
            pltpu.VMEM((rows, width), BF16),
            pltpu.SemaphoreType.DMA(()),
            pltpu.SemaphoreType.DMA(()),
        ],
        compiler_params=SMALL,
        cost_estimate=cost(1 << 24, 1 << 20),
        name="out_first",
    )(in_hbm(frames), own, got, w_out)


def run_out_rest(partial, got, w_out, earlier):
    rows, channels = got.shape
    width = w_out.shape[1]
    return pl.pallas_call(
        out_rest_kernel,
        in_specs=[VMEM_SPEC] * 3 + [ANY_SPEC],
        out_specs=ANY_SPEC,
        out_shape=jax.ShapeDtypeStruct(earlier.shape, BF16),
        input_output_aliases={3: 0},
        scratch_shapes=[
            pltpu.VMEM((rows, width), BF16),
            pltpu.SemaphoreType.DMA((rows // BLOCK,)),
        ],
        compiler_params=SMALL,
        cost_estimate=cost(1 << 24, 1 << 20),
        name="out_rest",
    )(partial, got, w_out, earlier)


def tail(logits, owners, silence, tags):
    group_size = lax.axis_size("grp")
    time_size = lax.axis_size("tm")
    group = lax.axis_index("grp")
    time = lax.axis_index("tm")
    segs = logits.shape[0]
    order = jnp.arange(segs, dtype=jnp.int32)

    bit = group_size // 2
    while bit:
        half = logits.shape[1] // 2
        upper = (group // bit) % 2
        kept = lax.dynamic_slice_in_dim(logits, upper * half, half, 1)
        sent = lax.dynamic_slice_in_dim(logits, (1 - upper) * half, half, 1)
        logits = kept + swap(sent.astype(BF16), "grp", bit).astype(F32)
        bit //= 2
    classes = logits.shape[1]

    owner_ids = owners[:, 0]
    earlier = order[None, :] < order[:, None]
    slot = jnp.sum(((owner_ids[:, None] == owner_ids[None, :]) & earlier).astype(jnp.int32), axis=1)
    dest = owner_ids * CAP + slot
    slots = time_size * CAP
    placing = (dest[None, :] == jnp.arange(slots, dtype=jnp.int32)[:, None]).astype(BF16)
    rounded = logits.astype(BF16)
    tag_numbers = (tags[0] + 1).astype(BF16)
    pad = jnp.zeros((segs, LANES - 1), BF16)
    labelled = jnp.concatenate([rounded, tag_numbers[:, None], pad], axis=1)
    send = jnp.dot(placing, labelled, preferred_element_type=F32).astype(BF16)
    got = lax.all_to_all(send, "tm", split_axis=0, concat_axis=0, tiled=True)

    tag_ids = jnp.arange(TAGS, dtype=jnp.int32)
    weighted = (tag_ids[:, None] == tags) & (silence > 0)
    sums = jnp.dot(weighted.astype(BF16), rounded, preferred_element_type=F32)
    counts = jnp.sum(weighted.astype(F32), axis=1, keepdims=True)
    counts = jnp.broadcast_to(counts, (TAGS, LANES))

    def exchanged(values, numbers, bit):
        high = jnp.floor(numbers * (1 / 128)) * 128
        lane = lax.broadcasted_iota(jnp.int32, numbers.shape, 1)
        coded = jnp.where(lane == 0, high, numbers - high)
        message = jnp.concatenate([values, coded], axis=1).astype(BF16)
        arrived = swap(message, "tm", bit).astype(F32)
        return arrived[:, :classes], arrived[:, classes : classes + 1] + arrived[:, classes + 1 : classes + 2]

    core = time % 2
    half = TAGS // 2
    sent_sums = lax.dynamic_slice_in_dim(sums, (1 - core) * half, half, 0)
    sent_counts = lax.dynamic_slice_in_dim(counts, (1 - core) * half, half, 0)
    sums = lax.dynamic_slice_in_dim(sums, core * half, half, 0)
    counts = lax.dynamic_slice_in_dim(counts, core * half, half, 0)
    more_sums, more_counts = exchanged(sent_sums, sent_counts, 1)
    sums, counts = sums + more_sums, counts + more_counts
    bit = 2
    while bit < time_size:
        more_sums, more_counts = exchanged(sums, counts, bit)
        sums, counts = sums + more_sums, counts + more_counts
        bit *= 2
    mine = (sums / (counts[:, :1] + 1.0)).astype(BF16)
    theirs = swap(mine, "tm", 1)
    shard_tags = got[:, classes : classes + 1].astype(jnp.int32)
    onehot_mine = (shard_tags == (tag_ids[:half] + core * half + 1)[None, :]).astype(BF16)
    onehot_theirs = (shard_tags == (tag_ids[:half] + (1 - core) * half + 1)[None, :]).astype(BF16)
    calibration = jnp.dot(onehot_mine, mine, preferred_element_type=F32) + jnp.dot(
        onehot_theirs, theirs, preferred_element_type=F32
    )
    scores = got[:, :classes].astype(F32) - calibration
    return scores

SUM_ROWS = TAGS // 2
AUX_ROWS = 16
MESSAGE = SUM_ROWS + AUX_ROWS + 64
SEGS = 128


def as_column(row):
    size = row.shape[1]
    eye = lax.broadcasted_iota(jnp.int32, (size, size), 0) == lax.broadcasted_iota(
        jnp.int32, (size, size), 1
    )
    return jnp.sum(jnp.where(eye, row, jnp.zeros_like(row)), axis=1, keepdims=True)


def iota(shape, dim):
    return lax.broadcasted_iota(jnp.int32, shape, dim)


def to_bf16(mask):
    return mask.astype(F32).astype(BF16)


def labels_kernel(after, owners, silence, tags, placing, weighted, aux):
    owner = owners[...]
    square = (SEGS, SEGS)
    same = as_column(owner) == owner
    slot_row = jnp.sum(jnp.where(same & (iota(square, 0) < iota(square, 1)), 1, 0), axis=0, keepdims=True)
    slot_column = jnp.sum(jnp.where(same & (iota(square, 1) < iota(square, 0)), 1, 0), axis=1, keepdims=True)
    placing[...] = to_bf16(iota(square, 0) == owner * CAP + slot_row)
    chosen = (iota((TAGS, SEGS), 0) == tags[...]) & (silence[...] > 0)
    weighted[...] = to_bf16(chosen)
    named = jnp.where(iota((AUX_ROWS, SEGS), 0) == owner, tags[...] + 1, 0).astype(F32).astype(BF16)
    lane = to_bf16(iota(square, 1) == slot_column + lax.axis_index("tm") * CAP)
    aux[:, 0:SEGS] = jnp.dot(named, lane, preferred_element_type=F32)
    silent = jnp.where(silence[...] > 0, 1.0, 0.0)
    ones = jnp.broadcast_to(silent, (8, SEGS)).astype(BF16)
    columns = as_column(tags[...])
    aux[:, SEGS:] = jnp.zeros((AUX_ROWS, SEGS), F32)
    for h in range(2):
        match = to_bf16(columns == iota((SEGS, SUM_ROWS), 1) + h * SUM_ROWS)
        count = jnp.dot(ones, match, preferred_element_type=F32)
        aux[2 + h : 3 + h, SEGS:] = count[0:1, :]


def picked(have, bit):
    rows, columns = iota((64, SEGS), 0), iota((64, SEGS), 1)
    chosen = columns == (rows // 8) * 16 + bit * 8 + rows % 8
    return jnp.dot(to_bf16(chosen), have, preferred_element_type=F32).astype(BF16)


def send_parts(message, keep, aux, sums, totals, have, bit):
    counts = aux[0:2, SEGS:] + aux[2:4, SEGS:]
    high = jnp.floor(counts * (1 / 128)) * 128
    totals[...] = aux
    totals[0:2, SEGS:] = high
    totals[2:4, SEGS:] = counts - high
    message[0:SUM_ROWS, :] = sums.astype(BF16)
    message[SUM_ROWS : SUM_ROWS + AUX_ROWS, :] = totals[...].astype(BF16)
    message[SUM_ROWS + AUX_ROWS :, :] = picked(have, 1 - bit)
    keep[...] = picked(have, bit)


def time_bit(b):
    return lax.div(lax.axis_index("tm"), 1 << b) % 2


def first_kernel(mine, got, placing, weighted, aux, message, sums, totals, keep):
    core = time_bit(0)
    rounded = (mine[...] + got[...].astype(F32)).astype(BF16)
    have = jnp.dot(placing[...], rounded, preferred_element_type=F32).astype(BF16)
    kept = weighted[pl.ds(pl.multiple_of(core * SUM_ROWS, SUM_ROWS), SUM_ROWS), :]
    sent = weighted[pl.ds(pl.multiple_of((1 - core) * SUM_ROWS, SUM_ROWS), SUM_ROWS), :]
    sums[...] = jnp.dot(kept, rounded, preferred_element_type=F32)
    sent = jnp.dot(sent, rounded, preferred_element_type=F32)
    send_parts(message, keep, aux[...], sent, totals, have, core)


def merged(bit, arrived, sums, totals, keep, have):
    have[pl.ds(pl.multiple_of(bit * 64, 64), 64), :] = keep[...]
    have[pl.ds(pl.multiple_of((1 - bit) * 64, 64), 64), :] = arrived[SUM_ROWS + AUX_ROWS :, :]
    total = sums[...] + arrived[0:SUM_ROWS, :].astype(F32)
    aux = totals[...] + arrived[SUM_ROWS : SUM_ROWS + AUX_ROWS, :].astype(F32)
    return total, aux


def middle_kernel(
    after, arrived, sums, totals, keep, message, sums_out, totals_out, keep_out, have, *, hop
):
    total, aux = merged(time_bit(hop), arrived, sums, totals, keep, have)
    sums_out[...] = total
    send_parts(message, keep_out, aux, total, totals_out, have[...], time_bit(hop + 1))


def last_kernel(after, arrived, sums, totals, keep, calibration, table, have):
    total, aux = merged(time_bit(3), arrived, sums, totals, keep, have)
    table[...] = aux
    both = aux[0:2, SEGS:] + aux[2:4, SEGS:]
    counts = jnp.where(time_bit(0) == 0, both[0:1, :], both[1:2, :])
    calibration[...] = (total / (as_column(counts) + 1.0)).astype(BF16)


def scores_kernel(mine, theirs, table, have, scores):
    named = jnp.where(iota((AUX_ROWS, SEGS), 0) == lax.axis_index("tm"), table[:, 0:SEGS], 0.0)
    row = jnp.sum(named, axis=0, keepdims=True).astype(jnp.int32)
    column = as_column(row)
    ids = iota((SEGS, SUM_ROWS), 1) + 1
    core = time_bit(0)
    near = to_bf16(column == ids + core * SUM_ROWS)
    far = to_bf16(column == ids + (1 - core) * SUM_ROWS)
    scores[...] = (
        have[...].astype(F32)
        - jnp.dot(near, mine[...], preferred_element_type=F32)
        - jnp.dot(far, theirs[...], preferred_element_type=F32)
    )


def small_call(kernel, name, operands, outs, scratch=(), hbm=0):
    return pl.pallas_call(
        kernel,
        in_specs=[ANY_SPEC] * hbm + [VMEM_SPEC] * (len(operands) - hbm),
        out_specs=[VMEM_SPEC] * len(outs),
        out_shape=[jax.ShapeDtypeStruct(*o) for o in outs],
        scratch_shapes=list(scratch),
        compiler_params=SMALL,
        cost_estimate=cost(1 << 24, 1 << 20),
        name=name,
    )(*operands)


def fast_tail(mine, got, act_rest, owners, silence, tags, block_out):
    classes = mine.shape[1]
    sums = ((SUM_ROWS, classes), F32)
    aux = ((AUX_ROWS, 2 * SEGS), F32)
    keep = ((64, classes), BF16)
    message = ((MESSAGE, classes), BF16)
    have = (pltpu.VMEM((SEGS, classes), BF16),)
    placing, weighted, labels = small_call(
        labels_kernel,
        "labels",
        [mine, owners[:, 0][None, :], silence, tags],
        [((SEGS, SEGS), BF16), ((TAGS, SEGS), BF16), aux],
    )
    act_rest, got = lax.optimization_barrier((act_rest, got))
    got_rest = swap(act_rest, "grp", 1)
    state = small_call(
        first_kernel, "first", [mine, got, placing, weighted, labels], [message, sums, aux, keep]
    )
    for b in range(3):
        arrived = swap(state[0], "tm", 1 << b)
        if b == 1:
            token, finish = block_out()
        state = small_call(
            functools.partial(middle_kernel, hop=b),
            "middle",
            [token if b == 1 else arrived, arrived, *state[1:]],
            [message, sums, aux, keep],
            have,
        )
    arrived = swap(state[0], "tm", 8)
    block_rows = finish(got_rest)
    calibration, table, ready = small_call(
        last_kernel,
        "last",
        [in_hbm(block_rows), arrived, *state[1:]],
        [((SUM_ROWS, classes), BF16), aux, ((SEGS, classes), BF16)],
        hbm=1,
    )
    theirs = swap(calibration, "tm", 1)
    [scores] = small_call(
        scores_kernel, "scores", [calibration, theirs, table, ready], [((SEGS, classes), F32)]
    )
    return block_rows, scores


def fast_body(
    frames,
    ln_gain,
    w_value,
    w_gate,
    conv_taps,
    bn_scale,
    bn_shift,
    w_out,
    w_classes,
    seg_lengths,
    owners,
    silence,
    tags,
):
    count = frames.shape[0]
    time_size = lax.axis_size("tm")
    own_rows = count // 2
    glu = run_fast_glu(frames, ln_gain, w_value, w_gate)
    odd = lax.axis_index("tm") % 2 == 1
    first, last = glu[:HALO], glu[count - HALO :]
    across = [(i, i + 1) for i in range(1, time_size - 1, 2)]
    across += [(j, i) for i, j in across]
    near = swap(jnp.where(odd, first, last), "tm", 1)
    far = lax.ppermute(jnp.where(odd, last, first), "tm", across)
    bn = (conv_taps, bn_scale, bn_shift, seg_lengths)
    act_first, pooled = run_early(BLOCK, glu, *bn)
    got_first = swap(act_first, "grp", 1)
    act_rest, act_own, mine, sent = run_late(
        glu, near, far, *bn, pooled, frames, w_out, w_classes
    )
    sent, got_first = lax.optimization_barrier((sent, got_first))
    got = swap(sent, "grp", 1)

    def block_out():
        rows, partial = run_out_first(frames, act_own, got_first, w_out)
        return partial, lambda got_rest: run_out_rest(partial, got_rest, w_out, rows)

    block_rows, scores = fast_tail(mine, got, act_rest, owners, silence, tags, block_out)
    return (block_rows[None, None], scores)


def body(*args):
    rows = args[0].shape[0] // lax.axis_size("grp")
    channels = args[2].shape[1]
    fits = rows % BLOCK == 0 and rows > BLOCK and channels % BLOCK == 0
    fits = fits and lax.axis_size("grp") == 2 and lax.axis_size("tm") == 16
    fits = fits and args[4].shape[0] == 31 and args[8].shape[1] == 512 and args[9].shape[1] == SEGS
    return (fast_body if fits else general_body)(*args)


def solution(mesh):
    in_specs = (
        P("tm", None),
        P(),
        P(None, "grp"),
        P(None, "grp"),
        P(None, "grp"),
        P("grp"),
        P("grp"),
        P(),
        P(),
        P("tm", None),
        P("tm", None),
        P("tm", None),
        P("tm", None),
    )
    out_specs = (P("tm", "grp", None, None), P("tm", "grp"))
    return jax.shard_map(body, mesh=mesh, in_specs=in_specs, out_specs=out_specs, check_vma=False)
```

```python
import functools

import jax
import jax.numpy as jnp
from jax import lax
from jax.experimental import pallas as pl
from jax.experimental.pallas import tpu as pltpu
from jax.sharding import PartitionSpec as P

TAGS = 256
CAP = 8
HALO = 16
BLOCK = 256
LANES = 128
VMEM_LIMIT = 48 << 20
F32, BF16 = jnp.float32, jnp.bfloat16


def sigmoid(v):
    return 0.5 * jnp.tanh(0.5 * v) + 0.5


def params():
    return pltpu.CompilerParams(
        dimension_semantics=("arbitrary",), vmem_limit_bytes=VMEM_LIMIT
    )


def whole(shape):
    return pl.BlockSpec(shape, lambda i, s: (0,) * len(shape))


def segment_mask(first, count, starts, ends):
    rows = first + lax.broadcasted_iota(jnp.int32, (starts.shape[0], count), 1)
    return (rows >= starts) & (rows < ends)


def glu_kernel(s, frames, gain, w_value, w_gate, starts, ends, glu, pooled, *, own_rows):
    step = pl.program_id(0)
    block = frames.shape[0]
    own_first = s[0] * own_rows

    @pl.when(step == 0)
    def _():
        pooled[...] = jnp.zeros_like(pooled)

    first = step * block

    @pl.when((first < own_first + own_rows) & (first + block > own_first))
    def _():
        rows = first + lax.broadcasted_iota(jnp.int32, (starts.shape[0], block), 1)
        low = jnp.maximum(starts[...], own_first)
        high = jnp.minimum(ends[...], own_first + own_rows)
        mask = ((rows >= low) & (rows < high)).astype(F32).astype(BF16)
        pooled[...] += jnp.dot(mask, frames[...], preferred_element_type=F32)

    half = block // 2
    for part in range(2):
        rows = pl.ds(part * half, half)
        x = frames[rows, :].astype(F32)
        center = jnp.mean(x, axis=-1, keepdims=True)
        x = x - center
        spread = jnp.mean(x * x, axis=-1, keepdims=True)
        normed = (x * lax.rsqrt(spread + 1e-05) * gain[...]).astype(BF16)
        value = jnp.dot(normed, w_value[...], preferred_element_type=F32)
        gate = jnp.dot(normed, w_gate[...], preferred_element_type=F32)
        glu[rows, :] = (value * sigmoid(gate)).astype(BF16)


def conv_kernel(s, window, taps, scale, shift, starts, ends, act, pooled, xs, *, taps_n):
    step = pl.program_id(0)
    block, channels = act.shape
    tiles = [(c, min(LANES, channels - c)) for c in range(0, channels, LANES)]
    for t, (c, w) in enumerate(tiles):
        xs[t, :, 0:w] = window[:, c : c + w].astype(F32)

    def tile(t, c, w):
        lanes = pl.ds(c, w)
        for r in range(0, block, 64):
            total = jnp.zeros((64, w), F32)
            for k in range(taps_n):
                total = total + taps[k : k + 1, lanes] * xs[t, pl.ds(r + 1 + k, 64), 0:w]
            v = total * scale[:, lanes] + shift[:, lanes]
            act[pl.ds(r, 64), lanes] = (v * sigmoid(v)).astype(BF16)

    if channels % LANES == 0:

        @pl.loop(0, channels // LANES)
        def _(t):
            tile(t, pl.multiple_of(t * LANES, LANES), LANES)
    else:
        for t, (c, w) in enumerate(tiles):
            tile(t, c, w)

    first = s[0] + step * block
    mask = segment_mask(first, block, starts[...], ends[...]).astype(F32).astype(BF16)
    part = jnp.dot(mask, act[...], preferred_element_type=F32)

    @pl.when(step == 0)
    def _():
        pooled[...] = part

    @pl.when(step > 0)
    def _():
        pooled[...] += part


def logits_kernel(s, frames_pooled, pooled, w_out, w_classes, starts, ends, out):
    mixed = jnp.dot(pooled[...].astype(BF16), w_out[...], preferred_element_type=F32)
    inverse = 1.0 / (ends[...] - starts[...]).astype(F32)
    mean = ((frames_pooled[...] + mixed) * inverse).astype(BF16)
    out[...] = jnp.dot(mean, w_classes[...], preferred_element_type=F32)


def out_kernel(s, *refs):
    *pairs, frames, out = refs
    total = frames[...].astype(F32)
    for act, w_out in zip(pairs[0::2], pairs[1::2]):
        total = total + jnp.dot(act[...], w_out[...], preferred_element_type=F32)
    out[...] = total.astype(BF16)


def run_glu(group_index, own_rows, frames, gain, w_value, w_gate, starts, ends):
    count, width = frames.shape
    channels = w_value.shape[1]
    segs = starts.shape[0]
    return pl.pallas_call(
        functools.partial(glu_kernel, own_rows=own_rows),
        grid_spec=pltpu.PrefetchScalarGridSpec(
            num_scalar_prefetch=1,
            grid=(count // BLOCK,),
            in_specs=[
                pl.BlockSpec((BLOCK, width), lambda i, s: (i, 0)),
                whole((1, width)),
                whole((width, channels)),
                whole((width, channels)),
                whole((segs, 1)),
                whole((segs, 1)),
            ],
            out_specs=[
                pl.BlockSpec((BLOCK, channels), lambda i, s: (i, 0)),
                whole((segs, width)),
            ],
        ),
        out_shape=[
            jax.ShapeDtypeStruct((count, channels), BF16),
            jax.ShapeDtypeStruct((segs, width), F32),
        ],
        compiler_params=params(),
        name="glu",
    )(group_index, frames, gain, w_value, w_gate, starts, ends)


def run_conv(base, rows, padded, taps, scale, shift, starts, ends):
    channels = padded.shape[1]
    segs = starts.shape[0]
    tiles = pl.cdiv(channels, LANES)
    return pl.pallas_call(
        functools.partial(conv_kernel, taps_n=taps.shape[0]),
        grid_spec=pltpu.PrefetchScalarGridSpec(
            num_scalar_prefetch=1,
            grid=(rows // BLOCK,),
            in_specs=[
                pl.BlockSpec(
                    (pl.Element(BLOCK + 2 * HALO), pl.Element(channels)),
                    lambda i, s: (pl.multiple_of(s[0] + i * BLOCK, HALO), 0),
                ),
                whole(taps.shape),
                whole((1, channels)),
                whole((1, channels)),
                whole((segs, 1)),
                whole((segs, 1)),
            ],
            out_specs=[
                pl.BlockSpec((BLOCK, channels), lambda i, s: (i, 0)),
                whole((segs, channels)),
            ],
            scratch_shapes=[pltpu.VMEM((tiles, BLOCK + 2 * HALO, LANES), F32)],
        ),
        out_shape=[
            jax.ShapeDtypeStruct((rows, channels), BF16),
            jax.ShapeDtypeStruct((segs, channels), F32),
        ],
        compiler_params=params(),
        name="conv",
    )(base, padded, taps, scale, shift, starts, ends)


def run_logits(group_index, frames_pooled, pooled, w_out, w_classes, starts, ends):
    segs, channels = pooled.shape
    width, classes = w_classes.shape
    return pl.pallas_call(
        logits_kernel,
        grid_spec=pltpu.PrefetchScalarGridSpec(
            num_scalar_prefetch=1,
            grid=(1,),
            in_specs=[
                whole((segs, width)),
                whole((segs, channels)),
                pl.BlockSpec((channels, width), lambda i, s: (s[0], 0)),
                whole((width, classes)),
                whole((segs, 1)),
                whole((segs, 1)),
            ],
            out_specs=whole((segs, classes)),
        ),
        out_shape=jax.ShapeDtypeStruct((segs, classes), F32),
        compiler_params=params(),
        name="logits",
    )(group_index, frames_pooled, pooled, w_out, w_classes, starts, ends)


def run_out(scalars, sources, w_out, frames, rows):
    width = frames.shape[1]
    block = BLOCK if rows % BLOCK == 0 else rows
    steps = rows // block
    in_specs, operands = [], []
    for act, place in sources:
        in_specs.append(pl.BlockSpec((block, act.shape[1]), lambda i, s: (i, 0)))
        in_specs.append(
            pl.BlockSpec((act.shape[1], width), functools.partial(lambda p, i, s: (s[p], 0), place))
        )
        operands += [act, w_out]
    in_specs.append(pl.BlockSpec((block, width), lambda i, s: (s[0] * steps + i, 0)))
    return pl.pallas_call(
        out_kernel,
        grid_spec=pltpu.PrefetchScalarGridSpec(
            num_scalar_prefetch=1,
            grid=(steps,),
            in_specs=in_specs,
            out_specs=pl.BlockSpec((block, width), lambda i, s: (i, 0)),
        ),
        out_shape=jax.ShapeDtypeStruct((rows, width), BF16),
        compiler_params=params(),
        name="block_out",
    )(scalars, *operands, frames)


def swap(value, axis, bit):
    count = lax.axis_size(axis)
    return lax.ppermute(value, axis, [(i, i ^ bit) for i in range(count)])


def general_body(
    frames,
    ln_gain,
    w_value,
    w_gate,
    conv_taps,
    bn_scale,
    bn_shift,
    w_out,
    w_classes,
    seg_lengths,
    owners,
    silence,
    tags,
):
    count, width = frames.shape
    channels = w_value.shape[1]
    group_size = lax.axis_size("grp")
    time_size = lax.axis_size("tm")
    group = lax.axis_index("grp")
    time = lax.axis_index("tm")
    own_rows = count // group_size
    lengths = seg_lengths[0]
    segs = lengths.shape[0]
    order = jnp.arange(segs, dtype=jnp.int32)
    ends = jnp.sum(
        jnp.where(order[None, :] <= order[:, None], lengths[None, :], 0), axis=1, keepdims=True
    )
    starts = ends - lengths[:, None]
    group_scalar = group[None].astype(jnp.int32)

    glu, frames_pooled = run_glu(
        group_scalar, own_rows, frames, ln_gain[None, :], w_value, w_gate, starts, ends
    )
    up = [(i, i + 1) for i in range(time_size - 1)]
    down = [(j, i) for i, j in up]
    before = lax.ppermute(glu[count - HALO :], "tm", up)
    after = lax.ppermute(glu[:HALO], "tm", down)
    padded = jnp.concatenate([before, glu, after], axis=0)
    bn = (conv_taps, bn_scale[None, :], bn_shift[None, :], starts, ends)

    if group_size == 2:
        other = 1 - group_scalar
        act_other, pooled_other = run_conv(other * own_rows, own_rows, padded, *bn)
        act_got = swap(act_other, "grp", 1)
        act_own, pooled_own = run_conv(group_scalar * own_rows, own_rows, padded, *bn)
        pooled = pooled_other + pooled_own
        sources = [(act_own, 0), (act_got, 1)]
        scalars = jnp.concatenate([group_scalar, other])
    else:
        act, pooled = run_conv(jnp.zeros((1,), jnp.int32), count, padded, *bn)
        rows = lax.all_to_all(act, "grp", split_axis=0, concat_axis=1, tiled=True)
        sources = [(rows, 1)]
        scalars = jnp.concatenate([group_scalar, jnp.zeros((1,), jnp.int32)])

    logits = run_logits(group_scalar, frames_pooled, pooled, w_out, w_classes, starts, ends)

    scores = tail(logits, owners, silence, tags)

    block_rows = run_out(scalars, sources, w_out, frames, own_rows)
    return (block_rows[None, None], scores)


def in_hbm(value):
    return pltpu.with_memory_space_constraint(value, pltpu.HBM)


def cost(flops, traffic):
    return pl.CostEstimate(flops=flops, bytes_accessed=traffic, transcendentals=0)


VMEM_SPEC = pl.BlockSpec(memory_space=pltpu.VMEM)
SMEM_SPEC = pl.BlockSpec(memory_space=pltpu.SMEM)
ANY_SPEC = pl.BlockSpec(memory_space=pltpu.HBM)
SMALL = pltpu.CompilerParams(vmem_limit_bytes=8 << 20)


GLU_LEAD = 3
HALF = BLOCK // 2
FIRST = BLOCK + HALF


def fast_glu_kernel(
    frames, gain_in, w_value, w_gate, glu, rows_in, wv, wg, gain, normed, row_sem, col_sem
):
    count, width = frames.shape
    channels = wv.shape[1]
    blocks = count // BLOCK
    columns = channels // BLOCK

    def row_copy(b):
        rows = pl.ds(b * BLOCK, BLOCK)
        return pltpu.make_async_copy(frames.at[rows, :], rows_in.at[rows, :], row_sem.at[b])

    def column_copies(c):
        cols = pl.ds(c * BLOCK, BLOCK)
        return (
            pltpu.make_async_copy(w_value.at[:, cols], wv.at[:, cols], col_sem.at[0, c]),
            pltpu.make_async_copy(w_gate.at[:, cols], wg.at[:, cols], col_sem.at[1, c]),
        )

    def normalize(b):
        row_copy(b).wait()
        x = rows_in[pl.ds(b * BLOCK, BLOCK), :].astype(F32)
        center = jnp.mean(x, axis=-1, keepdims=True)
        x = x - center
        spread = jnp.mean(x * x, axis=-1, keepdims=True)
        factor = 0.5 * lax.rsqrt(spread + 1e-05)
        normed[b % GLU_LEAD] = (x * factor * gain[...].reshape(1, -1)).astype(BF16)

    def gated(b, c):
        cols = pl.ds(c * BLOCK, BLOCK)
        rows = normed[b % GLU_LEAD]
        value = jnp.dot(rows, wv[:, cols], preferred_element_type=F32)
        gate = jnp.dot(rows, wg[:, cols], preferred_element_type=F32)
        glu[pl.ds(b * BLOCK, BLOCK), cols] = (value * jnp.tanh(gate) + value).astype(BF16)

    gain_copy = pltpu.make_async_copy(gain_in, gain, row_sem.at[blocks])
    gain_copy.start()
    for b in range(GLU_LEAD):
        row_copy(b).start()
    for c in range(columns):
        for copy in column_copies(c):
            copy.start()
    for b in range(GLU_LEAD, blocks):
        row_copy(b).start()
    gain_copy.wait()
    for b in range(GLU_LEAD):
        normalize(b)
    for c in range(columns):
        for copy in column_copies(c):
            copy.wait()
        for b in range(GLU_LEAD):
            gated(b, c)
    for b in range(GLU_LEAD, blocks):
        normalize(b)
        for c in range(columns):
            gated(b, c)


def run_fast_glu(frames, gain, w_value, w_gate):
    count, width = frames.shape
    channels = w_value.shape[1]
    return pl.pallas_call(
        fast_glu_kernel,
        in_specs=[ANY_SPEC] * 4,
        out_specs=VMEM_SPEC,
        out_shape=jax.ShapeDtypeStruct((count, channels), BF16),
        scratch_shapes=[
            pltpu.VMEM((count, width), BF16),
            pltpu.VMEM((width, channels), BF16),
            pltpu.VMEM((width, channels), BF16),
            pltpu.VMEM((width,), F32),
            pltpu.VMEM((GLU_LEAD, BLOCK, width), BF16),
            pltpu.SemaphoreType.DMA((count // BLOCK + 1,)),
            pltpu.SemaphoreType.DMA((2, channels // BLOCK)),
        ],
        compiler_params=pltpu.CompilerParams(vmem_limit_bytes=14 << 20),
        cost_estimate=cost(4 * count * width * channels, 12 << 20),
        name="glu",
    )(in_hbm(frames), in_hbm(gain), in_hbm(w_value), in_hbm(w_gate))


def segment_bounds(lengths):
    row = lengths[...]
    size = row.shape[1]
    earlier = iota((size, size), 1) <= iota((size, size), 0)
    ends = jnp.sum(jnp.where(earlier, row, 0), axis=1, keepdims=True)
    return ends - as_column(row), ends


def half_places(count, group):
    own = count // 2
    last = count - BLOCK
    return (
        jnp.where(group == 0, BLOCK, own),
        jnp.where(group == 0, 0, last),
        jnp.where(group == 0, BLOCK, 0),
        jnp.where(group == 0, 0, own - BLOCK),
    )


def convolve(glu, halos, taps, scale, shift, xs, plan):
    count, channels = glu.shape
    taps_n = taps.shape[0]
    outer = BLOCK + HALO

    @pl.loop(0, channels // LANES)
    def _(t):
        lanes = pl.ds(pl.multiple_of(t * LANES, LANES), LANES)
        half_scale = 0.5 * scale[lanes].reshape(1, -1)
        half_shift = 0.5 * shift[lanes].reshape(1, -1)
        tap = [
            jnp.broadcast_to((taps[k : k + 1, lanes] * half_scale).astype(BF16), (16, LANES))
            for k in range(taps_n)
        ]
        for rows_n, source, act, place in plan:
            source = pl.multiple_of(source, HALF)
            if rows_n:
                rows = pl.ds(pl.multiple_of(source - HALO, HALO), rows_n + 2 * HALO)
                xs[0 : rows_n + 2 * HALO, :] = glu[rows, lanes].astype(F32)
            else:
                near, far = halos
                odd = lax.axis_index("tm") % 2 == 1
                inside = jnp.where(odd, source == 0, source != 0)
                halo = jnp.where(inside, near[:, lanes].astype(F32), far[:, lanes].astype(F32))

                @pl.when(source == 0)
                def _():
                    xs[0:HALO, :] = halo
                    xs[HALO:, :] = glu[0:outer, lanes].astype(F32)

                @pl.when(source != 0)
                def _():
                    xs[0:outer, :] = glu[count - outer : count, lanes].astype(F32)
                    xs[outer:, :] = halo

            sums = {}

            def add(block, k, product):
                key = (block, k // 8)
                sums[key] = sums[key] + product if key in sums else product

            rows_n = rows_n or BLOCK
            for m in range(rows_n // 16 + 1):
                for r in range(16):
                    if m == rows_n // 16 and r + 16 >= taps_n:
                        continue
                    shifted = xs[pl.ds(16 * m + r + 1, 16), :].astype(BF16)
                    if m < rows_n // 16:
                        add(m, r, tap[r] * shifted)
                    if m > 0 and r + 16 < taps_n:
                        add(m - 1, r + 16, tap[r + 16] * shifted)
                if m > 0:
                    total = half_shift
                    for q in range(pl.cdiv(taps_n, 8)):
                        total = total + sums.pop((m - 1, q)).astype(F32)
                    rows = pl.ds(pl.multiple_of(place + 16 * (m - 1), 16), 16)
                    act[rows, lanes] = (total * jnp.tanh(total) + total).astype(BF16)


def pool(plan, starts, ends):
    total = None
    for rows_n, source, act, place in plan:
        rows_n = rows_n or BLOCK
        mask = to_bf16(segment_mask(source, rows_n, starts, ends))
        rows = pl.ds(pl.multiple_of(place, HALF), rows_n)
        part = jnp.dot(mask, act[rows, :], preferred_element_type=F32)
        total = part if total is None else total + part
    return total


def early_kernel(glu, taps, scale, shift, lengths, act, pooled, xs):
    count = glu.shape[0]
    inner = half_places(count, 1 - lax.axis_index("grp"))[0]
    plan = [(BLOCK, inner, act, 0), (HALF, inner + BLOCK, act, BLOCK)]
    convolve(glu, None, taps, scale, shift, xs, plan)
    starts, ends = segment_bounds(lengths)
    pooled[...] = pool(plan, starts, ends)


def late_kernel(
    glu, before, after, taps, scale, shift, lengths, pooled, frames, w_out, w_classes,
    act_other, act_own, kept, sent, xs, rows_in, w_mine, w_cls, sem,
):
    count, channels = glu.shape
    group = lax.axis_index("grp")
    own_rows = act_own.shape[0]
    own_first = pl.multiple_of(group * own_rows, own_rows)
    copies = [
        pltpu.make_async_copy(
            w_out.at[pl.ds(pl.multiple_of(group * channels, channels), channels), :], w_mine, sem.at[0]
        ),
        pltpu.make_async_copy(frames.at[pl.ds(own_first, own_rows), :], rows_in, sem.at[1]),
        pltpu.make_async_copy(w_classes, w_cls, sem.at[2]),
    ]
    for copy in copies:
        copy.start()
    inner, outer, inner_at, outer_at = half_places(count, group)
    far_inner, far_outer, _, _ = half_places(count, 1 - group)
    plan = [(HALF, far_inner + FIRST, act_other, 0), (0, far_outer, act_other, HALF)]
    plan += [(BLOCK, inner + b, act_own, inner_at + b) for b in (0, BLOCK)]
    plan += [(0, outer, act_own, outer_at)]
    convolve(glu, (before, after), taps, scale, shift, xs, plan)
    starts, ends = segment_bounds(lengths)
    total = (pooled[...] + pool(plan, starts, ends)).astype(BF16)
    for copy in copies:
        copy.wait()
    total = jnp.dot(total, w_mine[...], preferred_element_type=F32)
    mask = to_bf16(segment_mask(own_first, own_rows, starts, ends))
    total = total + jnp.dot(mask, rows_in[...], preferred_element_type=F32)
    inverse = 1.0 / (ends - starts).astype(F32)
    logits = jnp.dot((total * inverse).astype(BF16), w_cls[...], preferred_element_type=F32)
    half = logits.shape[1] // 2
    low, high = logits[:, :half], logits[:, half:]
    kept[...] = jnp.where(group == 0, low, high)
    sent[...] = jnp.where(group == 0, high, low).astype(BF16)


def run_early(rows, glu, taps, scale, shift, lengths):
    channels = glu.shape[1]
    return pl.pallas_call(
        early_kernel,
        in_specs=[VMEM_SPEC] * 5,
        out_specs=[VMEM_SPEC, VMEM_SPEC],
        out_shape=[
            jax.ShapeDtypeStruct((rows, channels), BF16),
            jax.ShapeDtypeStruct((lengths.shape[1], channels), F32),
        ],
        scratch_shapes=[pltpu.VMEM((BLOCK + 2 * HALO, LANES), F32)],
        compiler_params=SMALL,
        cost_estimate=cost(1 << 20, 1 << 16),
        name="conv_early",
    )(glu, taps, scale, shift, lengths)


def run_late(glu, before, after, taps, scale, shift, lengths, pooled, frames, w_out, w_classes):
    count, channels = glu.shape
    segs = lengths.shape[1]
    width, classes = w_classes.shape
    own_rows = count // 2
    return pl.pallas_call(
        late_kernel,
        in_specs=[VMEM_SPEC] * 8 + [ANY_SPEC] * 3,
        out_specs=[VMEM_SPEC] * 4,
        out_shape=[
            jax.ShapeDtypeStruct((own_rows - FIRST, channels), BF16),
            jax.ShapeDtypeStruct((own_rows, channels), BF16),
            jax.ShapeDtypeStruct((segs, classes // 2), F32),
            jax.ShapeDtypeStruct((segs, classes // 2), BF16),
        ],
        scratch_shapes=[
            pltpu.VMEM((BLOCK + 2 * HALO, LANES), F32),
            pltpu.VMEM((own_rows, width), BF16),
            pltpu.VMEM((channels, width), BF16),
            pltpu.VMEM((width, classes), BF16),
            pltpu.SemaphoreType.DMA((3,)),
        ],
        compiler_params=pltpu.CompilerParams(vmem_limit_bytes=14 << 20),
        cost_estimate=cost(1 << 20, 1 << 16),
        name="conv_late",
    )(
        glu, before, after, taps, scale, shift, lengths, pooled,
        in_hbm(frames), in_hbm(w_out), in_hbm(w_classes),
    )


def rest_places(rows, group):
    _, _, inner_at, outer_at = half_places(2 * rows, group)
    return inner_at, [(0, HALF, inner_at + FIRST), (HALF, BLOCK, outer_at)]


def half_block(at, rows):
    return pl.ds(pl.multiple_of(at, HALF), rows)


def half_rows(channels, half):
    return pl.ds(pl.multiple_of(half * channels, channels), channels)


def own_row_copy(frames, buf, sem, at, own_rows):
    first = lax.axis_index("grp") * own_rows + at
    return pltpu.make_async_copy(frames.at[half_block(first, buf.shape[0]), :], buf, sem)


def out_first_kernel(frames, own, got, w_out, out, buf, sem):
    rows, channels = own.shape
    group = lax.axis_index("grp")
    first = rest_places(rows, group)[0]
    copy = own_row_copy(frames, buf, sem, first, rows)
    copy.start()
    mine, theirs = half_rows(channels, group), half_rows(channels, 1 - group)
    place = half_block(first, FIRST)
    total = jnp.dot(own[place, :], w_out[mine, :], preferred_element_type=F32) + jnp.dot(
        got[...], w_out[theirs, :], preferred_element_type=F32
    )
    copy.wait()
    buf[...] = (total + buf[...].astype(F32)).astype(BF16)
    out_copy = pltpu.make_async_copy(buf, out.at[place, :], sem)
    out_copy.start()
    out_copy.wait()


def out_partial_kernel(after, frames, own, w_out, partial, buf, sem):
    rows, channels = own.shape
    group = lax.axis_index("grp")
    rest = rest_places(rows, group)[1]
    copies = [
        own_row_copy(frames, buf.at[pl.ds(n, r), :], sem.at[i], at, rows)
        for i, (n, r, at) in enumerate(rest)
    ]
    for copy in copies:
        copy.start()
    mine = half_rows(channels, group)
    for copy, (n, r, at) in zip(copies, rest):
        total = jnp.dot(own[half_block(at, r), :], w_out[mine, :], preferred_element_type=F32)
        copy.wait()
        partial[n : n + r, :] = total + buf[n : n + r, :].astype(F32)


def out_rest_kernel(partial, got, w_out, earlier, out, buf, out_sem):
    rest, channels = got.shape
    group = lax.axis_index("grp")
    theirs = half_rows(channels, 1 - group)
    copies = []
    for i, (n, r, at) in enumerate(rest_places(rest + FIRST, group)[1]):
        total = jnp.dot(got[n : n + r, :], w_out[theirs, :], preferred_element_type=F32)
        buf[n : n + r, :] = (total + partial[n : n + r, :]).astype(BF16)
        copies.append(
            pltpu.make_async_copy(buf.at[pl.ds(n, r), :], out.at[half_block(at, r), :], out_sem.at[i])
        )
        copies[-1].start()
    for copy in copies:
        copy.wait()


def run_out_first(frames, own, got, w_out):
    width = frames.shape[1]
    return pl.pallas_call(
        out_first_kernel,
        in_specs=[ANY_SPEC] + [VMEM_SPEC] * 3,
        out_specs=ANY_SPEC,
        out_shape=jax.ShapeDtypeStruct((own.shape[0], width), BF16),
        scratch_shapes=[pltpu.VMEM((FIRST, width), BF16), pltpu.SemaphoreType.DMA(())],
        compiler_params=SMALL,
        cost_estimate=cost(1 << 24, 1 << 20),
        name="out_first",
    )(in_hbm(frames), own, got, w_out)


def run_out_partial(after, frames, own, w_out):
    rows = own.shape[0] - FIRST
    width = frames.shape[1]
    return pl.pallas_call(
        out_partial_kernel,
        in_specs=[VMEM_SPEC, ANY_SPEC, VMEM_SPEC, VMEM_SPEC],
        out_specs=VMEM_SPEC,
        out_shape=jax.ShapeDtypeStruct((rows, width), F32),
        scratch_shapes=[
            pltpu.VMEM((rows, width), BF16),
            pltpu.SemaphoreType.DMA((2,)),
        ],
        compiler_params=SMALL,
        cost_estimate=cost(1 << 24, 1 << 20),
        name="out_partial",
    )(after, in_hbm(frames), own, w_out)


def run_out_rest(partial, got, w_out, earlier):
    rows, channels = got.shape
    width = w_out.shape[1]
    return pl.pallas_call(
        out_rest_kernel,
        in_specs=[VMEM_SPEC] * 3 + [ANY_SPEC],
        out_specs=ANY_SPEC,
        out_shape=jax.ShapeDtypeStruct(earlier.shape, BF16),
        input_output_aliases={3: 0},
        scratch_shapes=[
            pltpu.VMEM((rows, width), BF16),
            pltpu.SemaphoreType.DMA((2,)),
        ],
        compiler_params=SMALL,
        cost_estimate=cost(1 << 24, 1 << 20),
        name="out_rest",
    )(partial, got, w_out, earlier)


def tail(logits, owners, silence, tags):
    group_size = lax.axis_size("grp")
    time_size = lax.axis_size("tm")
    group = lax.axis_index("grp")
    time = lax.axis_index("tm")
    segs = logits.shape[0]
    order = jnp.arange(segs, dtype=jnp.int32)

    bit = group_size // 2
    while bit:
        half = logits.shape[1] // 2
        upper = (group // bit) % 2
        kept = lax.dynamic_slice_in_dim(logits, upper * half, half, 1)
        sent = lax.dynamic_slice_in_dim(logits, (1 - upper) * half, half, 1)
        logits = kept + swap(sent.astype(BF16), "grp", bit).astype(F32)
        bit //= 2
    classes = logits.shape[1]

    owner_ids = owners[:, 0]
    earlier = order[None, :] < order[:, None]
    slot = jnp.sum(((owner_ids[:, None] == owner_ids[None, :]) & earlier).astype(jnp.int32), axis=1)
    dest = owner_ids * CAP + slot
    slots = time_size * CAP
    placing = (dest[None, :] == jnp.arange(slots, dtype=jnp.int32)[:, None]).astype(BF16)
    rounded = logits.astype(BF16)
    tag_numbers = (tags[0] + 1).astype(BF16)
    pad = jnp.zeros((segs, LANES - 1), BF16)
    labelled = jnp.concatenate([rounded, tag_numbers[:, None], pad], axis=1)
    send = jnp.dot(placing, labelled, preferred_element_type=F32).astype(BF16)
    got = lax.all_to_all(send, "tm", split_axis=0, concat_axis=0, tiled=True)

    tag_ids = jnp.arange(TAGS, dtype=jnp.int32)
    weighted = (tag_ids[:, None] == tags) & (silence > 0)
    sums = jnp.dot(weighted.astype(BF16), rounded, preferred_element_type=F32)
    counts = jnp.sum(weighted.astype(F32), axis=1, keepdims=True)
    counts = jnp.broadcast_to(counts, (TAGS, LANES))

    def exchanged(values, numbers, bit):
        high = jnp.floor(numbers * (1 / 128)) * 128
        lane = lax.broadcasted_iota(jnp.int32, numbers.shape, 1)
        coded = jnp.where(lane == 0, high, numbers - high)
        message = jnp.concatenate([values, coded], axis=1).astype(BF16)
        arrived = swap(message, "tm", bit).astype(F32)
        return arrived[:, :classes], arrived[:, classes : classes + 1] + arrived[:, classes + 1 : classes + 2]

    core = time % 2
    half = TAGS // 2
    sent_sums = lax.dynamic_slice_in_dim(sums, (1 - core) * half, half, 0)
    sent_counts = lax.dynamic_slice_in_dim(counts, (1 - core) * half, half, 0)
    sums = lax.dynamic_slice_in_dim(sums, core * half, half, 0)
    counts = lax.dynamic_slice_in_dim(counts, core * half, half, 0)
    more_sums, more_counts = exchanged(sent_sums, sent_counts, 1)
    sums, counts = sums + more_sums, counts + more_counts
    bit = 2
    while bit < time_size:
        more_sums, more_counts = exchanged(sums, counts, bit)
        sums, counts = sums + more_sums, counts + more_counts
        bit *= 2
    mine = (sums / (counts[:, :1] + 1.0)).astype(BF16)
    theirs = swap(mine, "tm", 1)
    shard_tags = got[:, classes : classes + 1].astype(jnp.int32)
    onehot_mine = (shard_tags == (tag_ids[:half] + core * half + 1)[None, :]).astype(BF16)
    onehot_theirs = (shard_tags == (tag_ids[:half] + (1 - core) * half + 1)[None, :]).astype(BF16)
    calibration = jnp.dot(onehot_mine, mine, preferred_element_type=F32) + jnp.dot(
        onehot_theirs, theirs, preferred_element_type=F32
    )
    scores = got[:, :classes].astype(F32) - calibration
    return scores

SUM_ROWS = TAGS // 2
AUX_ROWS = 16
MESSAGE = SUM_ROWS + AUX_ROWS + 64
SEGS = 128


def as_column(row):
    size = row.shape[1]
    eye = lax.broadcasted_iota(jnp.int32, (size, size), 0) == lax.broadcasted_iota(
        jnp.int32, (size, size), 1
    )
    return jnp.sum(jnp.where(eye, row, jnp.zeros_like(row)), axis=1, keepdims=True)


def iota(shape, dim):
    return lax.broadcasted_iota(jnp.int32, shape, dim)


def to_bf16(mask):
    return mask.astype(F32).astype(BF16)


def labels_kernel(after, owners, silence, tags, placing, weighted, aux):
    owner = owners[...]
    square = (SEGS, SEGS)
    same = as_column(owner) == owner
    slot_row = jnp.sum(jnp.where(same & (iota(square, 0) < iota(square, 1)), 1, 0), axis=0, keepdims=True)
    slot_column = jnp.sum(jnp.where(same & (iota(square, 1) < iota(square, 0)), 1, 0), axis=1, keepdims=True)
    placing[...] = to_bf16(iota(square, 0) == owner * CAP + slot_row)
    chosen = (iota((TAGS, SEGS), 0) == tags[...]) & (silence[...] > 0)
    weighted[...] = to_bf16(chosen)
    named = jnp.where(iota((AUX_ROWS, SEGS), 0) == owner, tags[...] + 1, 0).astype(F32).astype(BF16)
    lane = to_bf16(iota(square, 1) == slot_column + lax.axis_index("tm") * CAP)
    aux[:, 0:SEGS] = jnp.dot(named, lane, preferred_element_type=F32)
    silent = jnp.where(silence[...] > 0, 1.0, 0.0)
    ones = jnp.broadcast_to(silent, (8, SEGS)).astype(BF16)
    columns = as_column(tags[...])
    aux[:, SEGS:] = jnp.zeros((AUX_ROWS, SEGS), F32)
    for h in range(2):
        match = to_bf16(columns == iota((SEGS, SUM_ROWS), 1) + h * SUM_ROWS)
        count = jnp.dot(ones, match, preferred_element_type=F32)
        aux[2 + h : 3 + h, SEGS:] = count[0:1, :]


def picked(have, bit):
    rows, columns = iota((64, SEGS), 0), iota((64, SEGS), 1)
    chosen = columns == (rows // 8) * 16 + bit * 8 + rows % 8
    return jnp.dot(to_bf16(chosen), have, preferred_element_type=F32).astype(BF16)


def split_counts(aux, totals):
    counts = aux[0:2, SEGS:] + aux[2:4, SEGS:]
    high = jnp.floor(counts * (1 / 128)) * 128
    totals[...] = aux
    totals[0:2, SEGS:] = high
    totals[2:4, SEGS:] = counts - high


def send_parts(message, keep, aux, sums, totals, have, bit):
    split_counts(aux, totals)
    message[0:SUM_ROWS, :] = sums.astype(BF16)
    message[SUM_ROWS : SUM_ROWS + AUX_ROWS, :] = totals[...].astype(BF16)
    message[SUM_ROWS + AUX_ROWS :, :] = picked(have, 1 - bit)
    keep[...] = picked(have, bit)


def time_bit(b):
    return lax.div(lax.axis_index("tm"), 1 << b) % 2


def first_kernel(mine, got, placing, weighted, aux, message, sums, totals, keep):
    core = time_bit(0)
    rounded = (mine[...] + got[...].astype(F32)).astype(BF16)
    have = jnp.dot(placing[...], rounded, preferred_element_type=F32).astype(BF16)
    kept = weighted[pl.ds(pl.multiple_of(core * SUM_ROWS, SUM_ROWS), SUM_ROWS), :]
    sent = weighted[pl.ds(pl.multiple_of((1 - core) * SUM_ROWS, SUM_ROWS), SUM_ROWS), :]
    sums[...] = jnp.dot(kept, rounded, preferred_element_type=F32)
    sent = jnp.dot(sent, rounded, preferred_element_type=F32)
    send_parts(message, keep, aux[...], sent, totals, have, core)


def merged(bit, arrived, sums, totals, keep, have):
    have[pl.ds(pl.multiple_of(bit * 64, 64), 64), :] = keep[...]
    have[pl.ds(pl.multiple_of((1 - bit) * 64, 64), 64), :] = arrived[SUM_ROWS + AUX_ROWS :, :]
    total = sums[...] + arrived[0:SUM_ROWS, :].astype(F32)
    aux = totals[...] + arrived[SUM_ROWS : SUM_ROWS + AUX_ROWS, :].astype(F32)
    return total, aux


QUARTER = SUM_ROWS + AUX_ROWS + 32


def time_pair():
    return lax.div(lax.axis_index("tm"), 2) % 4


def picked_quarter(have, value):
    rows, columns = iota((32, SEGS), 0), iota((32, SEGS), 1)
    chosen = columns == (rows // 8) * 32 + value * 8 + rows % 8
    return jnp.dot(to_bf16(chosen), have, preferred_element_type=F32).astype(BF16)


def spread_kernel(arrived, sums, totals, keep, *rest):
    *messages, sums_out, totals_out, keep_out, have = rest
    total, aux = merged(time_bit(0), arrived, sums, totals, keep, have)
    sums_out[...] = total
    split_counts(aux, totals_out)
    total = total.astype(BF16)
    aux = totals_out[...].astype(BF16)
    pair = time_pair()
    held = have[...]
    for n, message in enumerate(messages):
        message[0:SUM_ROWS, :] = total
        message[SUM_ROWS : SUM_ROWS + AUX_ROWS, :] = aux
        message[SUM_ROWS + AUX_ROWS :, :] = picked_quarter(held, pair ^ (n + 1))
    keep_out[...] = picked_quarter(held, pair)


def gather_kernel(after, *rest):
    *arrived, sums, totals, keep, message, sums_out, totals_out, keep_out, have = rest
    pair = time_pair()
    have[pl.ds(pl.multiple_of(pair * 32, 32), 32), :] = keep[...]
    total, aux = sums[...], totals[...]
    for n, part in enumerate(arrived):
        place = pl.ds(pl.multiple_of((pair ^ (n + 1)) * 32, 32), 32)
        have[place, :] = part[SUM_ROWS + AUX_ROWS :, :]
        total = total + part[0:SUM_ROWS, :].astype(F32)
        aux = aux + part[SUM_ROWS : SUM_ROWS + AUX_ROWS, :].astype(F32)
    sums_out[...] = total
    send_parts(message, keep_out, aux, total, totals_out, have[...], time_bit(3))


def last_kernel(after, arrived, sums, totals, keep, calibration, table, have):
    total, aux = merged(time_bit(3), arrived, sums, totals, keep, have)
    table[...] = aux
    both = aux[0:2, SEGS:] + aux[2:4, SEGS:]
    counts = jnp.where(time_bit(0) == 0, both[0:1, :], both[1:2, :])
    calibration[...] = (total / (as_column(counts) + 1.0)).astype(BF16)


def scores_kernel(mine, theirs, table, have, scores):
    named = jnp.where(iota((AUX_ROWS, SEGS), 0) == lax.axis_index("tm"), table[:, 0:SEGS], 0.0)
    row = jnp.sum(named, axis=0, keepdims=True).astype(jnp.int32)
    column = as_column(row)
    ids = iota((SEGS, SUM_ROWS), 1) + 1
    core = time_bit(0)
    near = to_bf16(column == ids + core * SUM_ROWS)
    far = to_bf16(column == ids + (1 - core) * SUM_ROWS)
    scores[...] = (
        have[...].astype(F32)
        - jnp.dot(near, mine[...], preferred_element_type=F32)
        - jnp.dot(far, theirs[...], preferred_element_type=F32)
    )


def small_call(kernel, name, operands, outs, scratch=(), hbm=0):
    return pl.pallas_call(
        kernel,
        in_specs=[ANY_SPEC] * hbm + [VMEM_SPEC] * (len(operands) - hbm),
        out_specs=[VMEM_SPEC] * len(outs),
        out_shape=[jax.ShapeDtypeStruct(*o) for o in outs],
        scratch_shapes=list(scratch),
        compiler_params=SMALL,
        cost_estimate=cost(1 << 24, 1 << 20),
        name=name,
    )(*operands)


def fast_tail(mine, got, act_rest, owners, silence, tags, block_out):
    classes = mine.shape[1]
    sums = ((SUM_ROWS, classes), F32)
    aux = ((AUX_ROWS, 2 * SEGS), F32)
    keep = ((64, classes), BF16)
    message = ((MESSAGE, classes), BF16)
    have = (pltpu.VMEM((SEGS, classes), BF16),)
    placing, weighted, labels = small_call(
        labels_kernel,
        "labels",
        [mine, owners[:, 0][None, :], silence, tags],
        [((SEGS, SEGS), BF16), ((TAGS, SEGS), BF16), aux],
    )
    act_rest, got, placing = lax.optimization_barrier((act_rest, got, placing))
    got_rest = swap(act_rest, "grp", 1)
    state = small_call(
        first_kernel, "first", [mine, got, placing, weighted, labels], [message, sums, aux, keep]
    )
    arrived = swap(state[0], "tm", 1)
    quarter = ((QUARTER, classes), BF16)
    *spread, part_sums, part_totals, part_keep = small_call(
        spread_kernel,
        "spread",
        [arrived, *state[1:]],
        [quarter, quarter, quarter, sums, aux, ((32, classes), BF16)],
        have,
    )
    arrived = [swap(part, "tm", 2 * (n + 1)) for n, part in enumerate(spread)]
    rows = block_out.first()
    state = small_call(
        gather_kernel,
        "gather",
        [in_hbm(rows), *arrived, part_sums, part_totals, part_keep],
        [message, sums, aux, keep],
        have,
        hbm=1,
    )
    partial = block_out.partial(state[1])
    arrived = swap(state[0], "tm", 8)
    block_rows = block_out.rest(partial, got_rest, rows)
    calibration, table, ready = small_call(
        last_kernel,
        "last",
        [in_hbm(block_rows), arrived, *state[1:]],
        [((SUM_ROWS, classes), BF16), aux, ((SEGS, classes), BF16)],
        hbm=1,
    )
    theirs = swap(calibration, "tm", 1)
    [scores] = small_call(
        scores_kernel, "scores", [calibration, theirs, table, ready], [((SEGS, classes), F32)]
    )
    return block_rows, scores


def fast_body(
    frames,
    ln_gain,
    w_value,
    w_gate,
    conv_taps,
    bn_scale,
    bn_shift,
    w_out,
    w_classes,
    seg_lengths,
    owners,
    silence,
    tags,
):
    count = frames.shape[0]
    time_size = lax.axis_size("tm")
    own_rows = count // 2
    glu = run_fast_glu(frames, ln_gain, w_value, w_gate)
    odd = lax.axis_index("tm") % 2 == 1
    first, last = glu[:HALO], glu[count - HALO :]
    across = [(i, i + 1) for i in range(1, time_size - 1, 2)]
    across += [(j, i) for i, j in across]
    near = swap(jnp.where(odd, first, last), "tm", 1)
    far = lax.ppermute(jnp.where(odd, last, first), "tm", across)
    bn = (conv_taps, bn_scale, bn_shift, seg_lengths)
    act_first, pooled = run_early(FIRST, glu, *bn)
    got_first = swap(act_first, "grp", 1)
    act_rest, act_own, mine, sent = run_late(
        glu, near, far, *bn, pooled, frames, w_out, w_classes
    )
    sent, got_first = lax.optimization_barrier((sent, got_first))
    got = swap(sent, "grp", 1)

    class block_out:
        def first():
            return run_out_first(frames, act_own, got_first, w_out)

        def partial(after):
            return run_out_partial(after, frames, act_own, w_out)

        def rest(partial, got_rest, rows):
            return run_out_rest(partial, got_rest, w_out, rows)

    block_rows, scores = fast_tail(mine, got, act_rest, owners, silence, tags, block_out)
    return (block_rows[None, None], scores)


def body(*args):
    rows = args[0].shape[0] // lax.axis_size("grp")
    channels = args[2].shape[1]
    fits = rows == 3 * BLOCK and channels % BLOCK == 0
    fits = fits and lax.axis_size("grp") == 2 and lax.axis_size("tm") == 16
    fits = fits and args[4].shape[0] == 31 and args[8].shape[1] == 512 and args[9].shape[1] == SEGS
    return (fast_body if fits else general_body)(*args)


def solution(mesh):
    in_specs = (
        P("tm", None),
        P(),
        P(None, "grp"),
        P(None, "grp"),
        P(None, "grp"),
        P("grp"),
        P("grp"),
        P(),
        P(),
        P("tm", None),
        P("tm", None),
        P("tm", None),
        P("tm", None),
    )
    out_specs = (P("tm", "grp", None, None), P("tm", "grp"))
    return jax.shard_map(body, mesh=mesh, in_specs=in_specs, out_specs=out_specs, check_vma=False)
```

```python
import functools

import jax
import jax.numpy as jnp
from jax import lax
from jax.experimental import pallas as pl
from jax.experimental.pallas import tpu as pltpu
from jax.sharding import PartitionSpec as P

TAGS = 256
CAP = 8
HALO = 16
BLOCK = 256
LANES = 128
VMEM_LIMIT = 48 << 20
F32, BF16 = jnp.float32, jnp.bfloat16


def sigmoid(v):
    return 0.5 * jnp.tanh(0.5 * v) + 0.5


def params():
    return pltpu.CompilerParams(
        dimension_semantics=("arbitrary",), vmem_limit_bytes=VMEM_LIMIT
    )


def whole(shape):
    return pl.BlockSpec(shape, lambda i, s: (0,) * len(shape))


def segment_mask(first, count, starts, ends):
    rows = first + lax.broadcasted_iota(jnp.int32, (starts.shape[0], count), 1)
    return (rows >= starts) & (rows < ends)


def glu_kernel(s, frames, gain, w_value, w_gate, starts, ends, glu, pooled, *, own_rows):
    step = pl.program_id(0)
    block = frames.shape[0]
    own_first = s[0] * own_rows

    @pl.when(step == 0)
    def _():
        pooled[...] = jnp.zeros_like(pooled)

    first = step * block

    @pl.when((first < own_first + own_rows) & (first + block > own_first))
    def _():
        rows = first + lax.broadcasted_iota(jnp.int32, (starts.shape[0], block), 1)
        low = jnp.maximum(starts[...], own_first)
        high = jnp.minimum(ends[...], own_first + own_rows)
        mask = ((rows >= low) & (rows < high)).astype(F32).astype(BF16)
        pooled[...] += jnp.dot(mask, frames[...], preferred_element_type=F32)

    half = block // 2
    for part in range(2):
        rows = pl.ds(part * half, half)
        x = frames[rows, :].astype(F32)
        center = jnp.mean(x, axis=-1, keepdims=True)
        x = x - center
        spread = jnp.mean(x * x, axis=-1, keepdims=True)
        normed = (x * lax.rsqrt(spread + 1e-05) * gain[...]).astype(BF16)
        value = jnp.dot(normed, w_value[...], preferred_element_type=F32)
        gate = jnp.dot(normed, w_gate[...], preferred_element_type=F32)
        glu[rows, :] = (value * sigmoid(gate)).astype(BF16)


def conv_kernel(s, window, taps, scale, shift, starts, ends, act, pooled, xs, *, taps_n):
    step = pl.program_id(0)
    block, channels = act.shape
    tiles = [(c, min(LANES, channels - c)) for c in range(0, channels, LANES)]
    for t, (c, w) in enumerate(tiles):
        xs[t, :, 0:w] = window[:, c : c + w].astype(F32)

    def tile(t, c, w):
        lanes = pl.ds(c, w)
        for r in range(0, block, 64):
            total = jnp.zeros((64, w), F32)
            for k in range(taps_n):
                total = total + taps[k : k + 1, lanes] * xs[t, pl.ds(r + 1 + k, 64), 0:w]
            v = total * scale[:, lanes] + shift[:, lanes]
            act[pl.ds(r, 64), lanes] = (v * sigmoid(v)).astype(BF16)

    if channels % LANES == 0:

        @pl.loop(0, channels // LANES)
        def _(t):
            tile(t, pl.multiple_of(t * LANES, LANES), LANES)
    else:
        for t, (c, w) in enumerate(tiles):
            tile(t, c, w)

    first = s[0] + step * block
    mask = segment_mask(first, block, starts[...], ends[...]).astype(F32).astype(BF16)
    part = jnp.dot(mask, act[...], preferred_element_type=F32)

    @pl.when(step == 0)
    def _():
        pooled[...] = part

    @pl.when(step > 0)
    def _():
        pooled[...] += part


def logits_kernel(s, frames_pooled, pooled, w_out, w_classes, starts, ends, out):
    mixed = jnp.dot(pooled[...].astype(BF16), w_out[...], preferred_element_type=F32)
    inverse = 1.0 / (ends[...] - starts[...]).astype(F32)
    mean = ((frames_pooled[...] + mixed) * inverse).astype(BF16)
    out[...] = jnp.dot(mean, w_classes[...], preferred_element_type=F32)


def out_kernel(s, *refs):
    *pairs, frames, out = refs
    total = frames[...].astype(F32)
    for act, w_out in zip(pairs[0::2], pairs[1::2]):
        total = total + jnp.dot(act[...], w_out[...], preferred_element_type=F32)
    out[...] = total.astype(BF16)


def run_glu(group_index, own_rows, frames, gain, w_value, w_gate, starts, ends):
    count, width = frames.shape
    channels = w_value.shape[1]
    segs = starts.shape[0]
    return pl.pallas_call(
        functools.partial(glu_kernel, own_rows=own_rows),
        grid_spec=pltpu.PrefetchScalarGridSpec(
            num_scalar_prefetch=1,
            grid=(count // BLOCK,),
            in_specs=[
                pl.BlockSpec((BLOCK, width), lambda i, s: (i, 0)),
                whole((1, width)),
                whole((width, channels)),
                whole((width, channels)),
                whole((segs, 1)),
                whole((segs, 1)),
            ],
            out_specs=[
                pl.BlockSpec((BLOCK, channels), lambda i, s: (i, 0)),
                whole((segs, width)),
            ],
        ),
        out_shape=[
            jax.ShapeDtypeStruct((count, channels), BF16),
            jax.ShapeDtypeStruct((segs, width), F32),
        ],
        compiler_params=params(),
        name="glu",
    )(group_index, frames, gain, w_value, w_gate, starts, ends)


def run_conv(base, rows, padded, taps, scale, shift, starts, ends):
    channels = padded.shape[1]
    segs = starts.shape[0]
    tiles = pl.cdiv(channels, LANES)
    return pl.pallas_call(
        functools.partial(conv_kernel, taps_n=taps.shape[0]),
        grid_spec=pltpu.PrefetchScalarGridSpec(
            num_scalar_prefetch=1,
            grid=(rows // BLOCK,),
            in_specs=[
                pl.BlockSpec(
                    (pl.Element(BLOCK + 2 * HALO), pl.Element(channels)),
                    lambda i, s: (pl.multiple_of(s[0] + i * BLOCK, HALO), 0),
                ),
                whole(taps.shape),
                whole((1, channels)),
                whole((1, channels)),
                whole((segs, 1)),
                whole((segs, 1)),
            ],
            out_specs=[
                pl.BlockSpec((BLOCK, channels), lambda i, s: (i, 0)),
                whole((segs, channels)),
            ],
            scratch_shapes=[pltpu.VMEM((tiles, BLOCK + 2 * HALO, LANES), F32)],
        ),
        out_shape=[
            jax.ShapeDtypeStruct((rows, channels), BF16),
            jax.ShapeDtypeStruct((segs, channels), F32),
        ],
        compiler_params=params(),
        name="conv",
    )(base, padded, taps, scale, shift, starts, ends)


def run_logits(group_index, frames_pooled, pooled, w_out, w_classes, starts, ends):
    segs, channels = pooled.shape
    width, classes = w_classes.shape
    return pl.pallas_call(
        logits_kernel,
        grid_spec=pltpu.PrefetchScalarGridSpec(
            num_scalar_prefetch=1,
            grid=(1,),
            in_specs=[
                whole((segs, width)),
                whole((segs, channels)),
                pl.BlockSpec((channels, width), lambda i, s: (s[0], 0)),
                whole((width, classes)),
                whole((segs, 1)),
                whole((segs, 1)),
            ],
            out_specs=whole((segs, classes)),
        ),
        out_shape=jax.ShapeDtypeStruct((segs, classes), F32),
        compiler_params=params(),
        name="logits",
    )(group_index, frames_pooled, pooled, w_out, w_classes, starts, ends)


def run_out(scalars, sources, w_out, frames, rows):
    width = frames.shape[1]
    block = BLOCK if rows % BLOCK == 0 else rows
    steps = rows // block
    in_specs, operands = [], []
    for act, place in sources:
        in_specs.append(pl.BlockSpec((block, act.shape[1]), lambda i, s: (i, 0)))
        in_specs.append(
            pl.BlockSpec((act.shape[1], width), functools.partial(lambda p, i, s: (s[p], 0), place))
        )
        operands += [act, w_out]
    in_specs.append(pl.BlockSpec((block, width), lambda i, s: (s[0] * steps + i, 0)))
    return pl.pallas_call(
        out_kernel,
        grid_spec=pltpu.PrefetchScalarGridSpec(
            num_scalar_prefetch=1,
            grid=(steps,),
            in_specs=in_specs,
            out_specs=pl.BlockSpec((block, width), lambda i, s: (i, 0)),
        ),
        out_shape=jax.ShapeDtypeStruct((rows, width), BF16),
        compiler_params=params(),
        name="block_out",
    )(scalars, *operands, frames)


def swap(value, axis, bit):
    count = lax.axis_size(axis)
    return lax.ppermute(value, axis, [(i, i ^ bit) for i in range(count)])


def general_body(
    frames,
    ln_gain,
    w_value,
    w_gate,
    conv_taps,
    bn_scale,
    bn_shift,
    w_out,
    w_classes,
    seg_lengths,
    owners,
    silence,
    tags,
):
    count, width = frames.shape
    channels = w_value.shape[1]
    group_size = lax.axis_size("grp")
    time_size = lax.axis_size("tm")
    group = lax.axis_index("grp")
    time = lax.axis_index("tm")
    own_rows = count // group_size
    lengths = seg_lengths[0]
    segs = lengths.shape[0]
    order = jnp.arange(segs, dtype=jnp.int32)
    ends = jnp.sum(
        jnp.where(order[None, :] <= order[:, None], lengths[None, :], 0), axis=1, keepdims=True
    )
    starts = ends - lengths[:, None]
    group_scalar = group[None].astype(jnp.int32)

    glu, frames_pooled = run_glu(
        group_scalar, own_rows, frames, ln_gain[None, :], w_value, w_gate, starts, ends
    )
    up = [(i, i + 1) for i in range(time_size - 1)]
    down = [(j, i) for i, j in up]
    before = lax.ppermute(glu[count - HALO :], "tm", up)
    after = lax.ppermute(glu[:HALO], "tm", down)
    padded = jnp.concatenate([before, glu, after], axis=0)
    bn = (conv_taps, bn_scale[None, :], bn_shift[None, :], starts, ends)

    if group_size == 2:
        other = 1 - group_scalar
        act_other, pooled_other = run_conv(other * own_rows, own_rows, padded, *bn)
        act_got = swap(act_other, "grp", 1)
        act_own, pooled_own = run_conv(group_scalar * own_rows, own_rows, padded, *bn)
        pooled = pooled_other + pooled_own
        sources = [(act_own, 0), (act_got, 1)]
        scalars = jnp.concatenate([group_scalar, other])
    else:
        act, pooled = run_conv(jnp.zeros((1,), jnp.int32), count, padded, *bn)
        rows = lax.all_to_all(act, "grp", split_axis=0, concat_axis=1, tiled=True)
        sources = [(rows, 1)]
        scalars = jnp.concatenate([group_scalar, jnp.zeros((1,), jnp.int32)])

    logits = run_logits(group_scalar, frames_pooled, pooled, w_out, w_classes, starts, ends)

    scores = tail(logits, owners, silence, tags)

    block_rows = run_out(scalars, sources, w_out, frames, own_rows)
    return (block_rows[None, None], scores)


def in_hbm(value):
    return pltpu.with_memory_space_constraint(value, pltpu.HBM)


def cost(flops, traffic):
    return pl.CostEstimate(flops=flops, bytes_accessed=traffic, transcendentals=0)


VMEM_SPEC = pl.BlockSpec(memory_space=pltpu.VMEM)
SMEM_SPEC = pl.BlockSpec(memory_space=pltpu.SMEM)
ANY_SPEC = pl.BlockSpec(memory_space=pltpu.HBM)
SMALL = pltpu.CompilerParams(vmem_limit_bytes=8 << 20)


GLU_LEAD = 3
HALF = 64
REST = BLOCK - HALF
FIRST = BLOCK + HALF


def fast_glu_kernel(
    frames, gain_in, w_value, w_gate, glu, rows_in, wv, wg, gain, normed, row_sem, col_sem
):
    count, width = frames.shape
    channels = wv.shape[1]
    blocks = count // BLOCK
    columns = channels // BLOCK

    def row_copy(b):
        rows = pl.ds(b * BLOCK, BLOCK)
        return pltpu.make_async_copy(frames.at[rows, :], rows_in.at[rows, :], row_sem.at[b])

    def column_copies(c):
        cols = pl.ds(c * BLOCK, BLOCK)
        return (
            pltpu.make_async_copy(w_value.at[:, cols], wv.at[:, cols], col_sem.at[0, c]),
            pltpu.make_async_copy(w_gate.at[:, cols], wg.at[:, cols], col_sem.at[1, c]),
        )

    def normalize(b):
        row_copy(b).wait()
        x = rows_in[pl.ds(b * BLOCK, BLOCK), :].astype(F32)
        center = jnp.mean(x, axis=-1, keepdims=True)
        x = x - center
        spread = jnp.mean(x * x, axis=-1, keepdims=True)
        factor = 0.5 * lax.rsqrt(spread + 1e-05)
        normed[b % GLU_LEAD] = (x * factor * gain[...].reshape(1, -1)).astype(BF16)

    def gated(b, c):
        cols = pl.ds(c * BLOCK, BLOCK)
        rows = normed[b % GLU_LEAD]
        value = jnp.dot(rows, wv[:, cols], preferred_element_type=F32)
        gate = jnp.dot(rows, wg[:, cols], preferred_element_type=F32)
        glu[pl.ds(b * BLOCK, BLOCK), cols] = (value * jnp.tanh(gate) + value).astype(BF16)

    gain_copy = pltpu.make_async_copy(gain_in, gain, row_sem.at[blocks])
    gain_copy.start()
    for b in range(GLU_LEAD):
        row_copy(b).start()
    for c in range(columns):
        for copy in column_copies(c):
            copy.start()
    for b in range(GLU_LEAD, blocks):
        row_copy(b).start()
    gain_copy.wait()
    for b in range(GLU_LEAD):
        normalize(b)
    for c in range(columns):
        for copy in column_copies(c):
            copy.wait()
        for b in range(GLU_LEAD):
            gated(b, c)
    for b in range(GLU_LEAD, blocks):
        normalize(b)
        for c in range(columns):
            gated(b, c)


def run_fast_glu(frames, gain, w_value, w_gate):
    count, width = frames.shape
    channels = w_value.shape[1]
    return pl.pallas_call(
        fast_glu_kernel,
        in_specs=[ANY_SPEC] * 4,
        out_specs=VMEM_SPEC,
        out_shape=jax.ShapeDtypeStruct((count, channels), BF16),
        scratch_shapes=[
            pltpu.VMEM((count, width), BF16),
            pltpu.VMEM((width, channels), BF16),
            pltpu.VMEM((width, channels), BF16),
            pltpu.VMEM((width,), F32),
            pltpu.VMEM((GLU_LEAD, BLOCK, width), BF16),
            pltpu.SemaphoreType.DMA((count // BLOCK + 1,)),
            pltpu.SemaphoreType.DMA((2, channels // BLOCK)),
        ],
        compiler_params=pltpu.CompilerParams(vmem_limit_bytes=14 << 20),
        cost_estimate=cost(4 * count * width * channels, 12 << 20),
        name="glu",
    )(in_hbm(frames), in_hbm(gain), in_hbm(w_value), in_hbm(w_gate))


def segment_bounds(lengths):
    row = lengths[...]
    size = row.shape[1]
    earlier = iota((size, size), 1) <= iota((size, size), 0)
    ends = jnp.sum(jnp.where(earlier, row, 0), axis=1, keepdims=True)
    return ends - as_column(row), ends


def half_places(count, group):
    own = count // 2
    last = count - BLOCK
    return (
        jnp.where(group == 0, BLOCK, own),
        jnp.where(group == 0, 0, last),
        jnp.where(group == 0, BLOCK, 0),
        jnp.where(group == 0, 0, own - BLOCK),
    )


def convolve(glu, halos, taps, scale, shift, xs, plan):
    count, channels = glu.shape
    taps_n = taps.shape[0]
    outer = BLOCK + HALO

    @pl.loop(0, channels // LANES)
    def _(t):
        lanes = pl.ds(pl.multiple_of(t * LANES, LANES), LANES)
        half_scale = 0.5 * scale[lanes].reshape(1, -1)
        half_shift = 0.5 * shift[lanes].reshape(1, -1)
        tap = [
            jnp.broadcast_to((taps[k : k + 1, lanes] * half_scale).astype(BF16), (16, LANES))
            for k in range(taps_n)
        ]
        for rows_n, source, act, place in plan:
            source = pl.multiple_of(source, HALF)
            if rows_n:
                rows = pl.ds(pl.multiple_of(source - HALO, HALO), rows_n + 2 * HALO)
                xs[0 : rows_n + 2 * HALO, :] = glu[rows, lanes].astype(F32)
            else:
                near, far = halos
                odd = lax.axis_index("tm") % 2 == 1
                inside = jnp.where(odd, source == 0, source != 0)
                halo = jnp.where(inside, near[:, lanes].astype(F32), far[:, lanes].astype(F32))

                @pl.when(source == 0)
                def _():
                    xs[0:HALO, :] = halo
                    xs[HALO:, :] = glu[0:outer, lanes].astype(F32)

                @pl.when(source != 0)
                def _():
                    xs[0:outer, :] = glu[count - outer : count, lanes].astype(F32)
                    xs[outer:, :] = halo

            sums = {}

            def add(block, value):
                stack, level = sums.setdefault(block, []), 0
                while stack and stack[-1][0] == level:
                    value, level = stack.pop()[1] + value, level + 1
                stack.append((level, value))

            def finished(block):
                (_, value), *stack = reversed(sums.pop(block))
                for _, earlier in stack:
                    value = value + earlier
                return value.astype(F32)

            rows_n = rows_n or BLOCK
            for m in range(rows_n // 16 + 1):
                for r in range(16):
                    if m == rows_n // 16 and r + 16 >= taps_n:
                        continue
                    shifted = xs[pl.ds(16 * m + r + 1, 16), :].astype(BF16)
                    if m < rows_n // 16:
                        add(m, tap[r] * shifted)
                    if m > 0 and r + 16 < taps_n:
                        add(m - 1, tap[r + 16] * shifted)
                if m > 0:
                    total = half_shift + finished(m - 1)
                    rows = pl.ds(pl.multiple_of(place + 16 * (m - 1), 16), 16)
                    act[rows, lanes] = (total * jnp.tanh(total) + total).astype(BF16)


def pool(plan, starts, ends):
    total = None
    for rows_n, source, act, place in plan:
        rows_n = rows_n or BLOCK
        mask = to_bf16(segment_mask(source, rows_n, starts, ends))
        rows = pl.ds(pl.multiple_of(place, HALF), rows_n)
        part = jnp.dot(mask, act[rows, :], preferred_element_type=F32)
        total = part if total is None else total + part
    return total


def early_kernel(glu, taps, scale, shift, lengths, act, pooled, xs):
    count = glu.shape[0]
    inner = half_places(count, 1 - lax.axis_index("grp"))[0]
    plan = [(BLOCK, inner, act, 0), (HALF, inner + BLOCK, act, BLOCK)]
    convolve(glu, None, taps, scale, shift, xs, plan)
    starts, ends = segment_bounds(lengths)
    pooled[...] = pool(plan, starts, ends)


def late_kernel(
    glu, before, after, taps, scale, shift, lengths, pooled, frames, w_out, w_classes,
    act_other, act_own, kept, sent, xs, rows_in, w_mine, w_cls, sem,
):
    count, channels = glu.shape
    group = lax.axis_index("grp")
    own_rows = act_own.shape[0]
    own_first = pl.multiple_of(group * own_rows, own_rows)
    copies = [
        pltpu.make_async_copy(
            w_out.at[pl.ds(pl.multiple_of(group * channels, channels), channels), :], w_mine, sem.at[0]
        ),
        pltpu.make_async_copy(frames.at[pl.ds(own_first, own_rows), :], rows_in, sem.at[1]),
        pltpu.make_async_copy(w_classes, w_cls, sem.at[2]),
    ]
    for copy in copies:
        copy.start()
    inner, outer, inner_at, outer_at = half_places(count, group)
    far_inner, far_outer, _, _ = half_places(count, 1 - group)
    plan = [(REST, far_inner + FIRST, act_other, 0), (0, far_outer, act_other, REST)]
    plan += [(BLOCK, inner + b, act_own, inner_at + b) for b in (0, BLOCK)]
    plan += [(0, outer, act_own, outer_at)]
    convolve(glu, (before, after), taps, scale, shift, xs, plan)
    starts, ends = segment_bounds(lengths)
    total = (pooled[...] + pool(plan, starts, ends)).astype(BF16)
    for copy in copies:
        copy.wait()
    total = jnp.dot(total, w_mine[...], preferred_element_type=F32)
    mask = to_bf16(segment_mask(own_first, own_rows, starts, ends))
    total = total + jnp.dot(mask, rows_in[...], preferred_element_type=F32)
    inverse = 1.0 / (ends - starts).astype(F32)
    logits = jnp.dot((total * inverse).astype(BF16), w_cls[...], preferred_element_type=F32)
    half = logits.shape[1] // 2
    low, high = logits[:, :half], logits[:, half:]
    kept[...] = jnp.where(group == 0, low, high)
    sent[...] = jnp.where(group == 0, high, low).astype(BF16)


def run_early(rows, glu, taps, scale, shift, lengths):
    channels = glu.shape[1]
    return pl.pallas_call(
        early_kernel,
        in_specs=[VMEM_SPEC] * 5,
        out_specs=[VMEM_SPEC, VMEM_SPEC],
        out_shape=[
            jax.ShapeDtypeStruct((rows, channels), BF16),
            jax.ShapeDtypeStruct((lengths.shape[1], channels), F32),
        ],
        scratch_shapes=[pltpu.VMEM((BLOCK + 2 * HALO, LANES), F32)],
        compiler_params=SMALL,
        cost_estimate=cost(1 << 20, 1 << 16),
        name="conv_early",
    )(glu, taps, scale, shift, lengths)


def run_late(glu, before, after, taps, scale, shift, lengths, pooled, frames, w_out, w_classes):
    count, channels = glu.shape
    segs = lengths.shape[1]
    width, classes = w_classes.shape
    own_rows = count // 2
    return pl.pallas_call(
        late_kernel,
        in_specs=[VMEM_SPEC] * 8 + [ANY_SPEC] * 3,
        out_specs=[VMEM_SPEC] * 4,
        out_shape=[
            jax.ShapeDtypeStruct((own_rows - FIRST, channels), BF16),
            jax.ShapeDtypeStruct((own_rows, channels), BF16),
            jax.ShapeDtypeStruct((segs, classes // 2), F32),
            jax.ShapeDtypeStruct((segs, classes // 2), BF16),
        ],
        scratch_shapes=[
            pltpu.VMEM((BLOCK + 2 * HALO, LANES), F32),
            pltpu.VMEM((own_rows, width), BF16),
            pltpu.VMEM((channels, width), BF16),
            pltpu.VMEM((width, classes), BF16),
            pltpu.SemaphoreType.DMA((3,)),
        ],
        compiler_params=pltpu.CompilerParams(vmem_limit_bytes=14 << 20),
        cost_estimate=cost(1 << 20, 1 << 16),
        name="conv_late",
    )(
        glu, before, after, taps, scale, shift, lengths, pooled,
        in_hbm(frames), in_hbm(w_out), in_hbm(w_classes),
    )


def rest_places(rows, group):
    _, _, inner_at, outer_at = half_places(2 * rows, group)
    return inner_at, [(0, REST, inner_at + FIRST), (REST, BLOCK, outer_at)]


def half_block(at, rows):
    return pl.ds(pl.multiple_of(at, HALF), rows)


def half_rows(channels, half):
    return pl.ds(pl.multiple_of(half * channels, channels), channels)


def own_row_copy(frames, buf, sem, at, own_rows):
    first = lax.axis_index("grp") * own_rows + at
    return pltpu.make_async_copy(frames.at[half_block(first, buf.shape[0]), :], buf, sem)


def out_first_kernel(frames, own, got, w_out, out, buf, sem):
    rows, channels = own.shape
    group = lax.axis_index("grp")
    first = rest_places(rows, group)[0]
    copy = own_row_copy(frames, buf, sem, first, rows)
    copy.start()
    mine, theirs = half_rows(channels, group), half_rows(channels, 1 - group)
    place = half_block(first, FIRST)
    total = jnp.dot(own[place, :], w_out[mine, :], preferred_element_type=F32) + jnp.dot(
        got[...], w_out[theirs, :], preferred_element_type=F32
    )
    copy.wait()
    buf[...] = (total + buf[...].astype(F32)).astype(BF16)
    out_copy = pltpu.make_async_copy(buf, out.at[place, :], sem)
    out_copy.start()
    out_copy.wait()


def out_partial_kernel(after, frames, own, w_out, partial, buf, sem):
    rows, channels = own.shape
    group = lax.axis_index("grp")
    rest = rest_places(rows, group)[1]
    copies = [
        own_row_copy(frames, buf.at[pl.ds(n, r), :], sem.at[i], at, rows)
        for i, (n, r, at) in enumerate(rest)
    ]
    for copy in copies:
        copy.start()
    mine = half_rows(channels, group)
    for copy, (n, r, at) in zip(copies, rest):
        total = jnp.dot(own[half_block(at, r), :], w_out[mine, :], preferred_element_type=F32)
        copy.wait()
        partial[n : n + r, :] = total + buf[n : n + r, :].astype(F32)


def out_rest_kernel(partial, got, w_out, earlier, out, buf, out_sem):
    rest, channels = got.shape
    group = lax.axis_index("grp")
    theirs = half_rows(channels, 1 - group)
    copies = []
    for i, (n, r, at) in enumerate(rest_places(rest + FIRST, group)[1]):
        total = jnp.dot(got[n : n + r, :], w_out[theirs, :], preferred_element_type=F32)
        buf[n : n + r, :] = (total + partial[n : n + r, :]).astype(BF16)
        copies.append(
            pltpu.make_async_copy(buf.at[pl.ds(n, r), :], out.at[half_block(at, r), :], out_sem.at[i])
        )
        copies[-1].start()
    for copy in copies:
        copy.wait()


def run_out_first(frames, own, got, w_out):
    width = frames.shape[1]
    return pl.pallas_call(
        out_first_kernel,
        in_specs=[ANY_SPEC] + [VMEM_SPEC] * 3,
        out_specs=ANY_SPEC,
        out_shape=jax.ShapeDtypeStruct((own.shape[0], width), BF16),
        scratch_shapes=[pltpu.VMEM((FIRST, width), BF16), pltpu.SemaphoreType.DMA(())],
        compiler_params=SMALL,
        cost_estimate=cost(1 << 24, 1 << 20),
        name="out_first",
    )(in_hbm(frames), own, got, w_out)


def run_out_partial(after, frames, own, w_out):
    rows = own.shape[0] - FIRST
    width = frames.shape[1]
    return pl.pallas_call(
        out_partial_kernel,
        in_specs=[VMEM_SPEC, ANY_SPEC, VMEM_SPEC, VMEM_SPEC],
        out_specs=VMEM_SPEC,
        out_shape=jax.ShapeDtypeStruct((rows, width), F32),
        scratch_shapes=[
            pltpu.VMEM((rows, width), BF16),
            pltpu.SemaphoreType.DMA((2,)),
        ],
        compiler_params=SMALL,
        cost_estimate=cost(1 << 24, 1 << 20),
        name="out_partial",
    )(after, in_hbm(frames), own, w_out)


def run_out_rest(partial, got, w_out, earlier):
    rows, channels = got.shape
    width = w_out.shape[1]
    return pl.pallas_call(
        out_rest_kernel,
        in_specs=[VMEM_SPEC] * 3 + [ANY_SPEC],
        out_specs=ANY_SPEC,
        out_shape=jax.ShapeDtypeStruct(earlier.shape, BF16),
        input_output_aliases={3: 0},
        scratch_shapes=[
            pltpu.VMEM((rows, width), BF16),
            pltpu.SemaphoreType.DMA((2,)),
        ],
        compiler_params=SMALL,
        cost_estimate=cost(1 << 24, 1 << 20),
        name="out_rest",
    )(partial, got, w_out, earlier)


def tail(logits, owners, silence, tags):
    group_size = lax.axis_size("grp")
    time_size = lax.axis_size("tm")
    group = lax.axis_index("grp")
    time = lax.axis_index("tm")
    segs = logits.shape[0]
    order = jnp.arange(segs, dtype=jnp.int32)

    bit = group_size // 2
    while bit:
        half = logits.shape[1] // 2
        upper = (group // bit) % 2
        kept = lax.dynamic_slice_in_dim(logits, upper * half, half, 1)
        sent = lax.dynamic_slice_in_dim(logits, (1 - upper) * half, half, 1)
        logits = kept + swap(sent.astype(BF16), "grp", bit).astype(F32)
        bit //= 2
    classes = logits.shape[1]

    owner_ids = owners[:, 0]
    earlier = order[None, :] < order[:, None]
    slot = jnp.sum(((owner_ids[:, None] == owner_ids[None, :]) & earlier).astype(jnp.int32), axis=1)
    dest = owner_ids * CAP + slot
    slots = time_size * CAP
    placing = (dest[None, :] == jnp.arange(slots, dtype=jnp.int32)[:, None]).astype(BF16)
    rounded = logits.astype(BF16)
    tag_numbers = (tags[0] + 1).astype(BF16)
    pad = jnp.zeros((segs, LANES - 1), BF16)
    labelled = jnp.concatenate([rounded, tag_numbers[:, None], pad], axis=1)
    send = jnp.dot(placing, labelled, preferred_element_type=F32).astype(BF16)
    got = lax.all_to_all(send, "tm", split_axis=0, concat_axis=0, tiled=True)

    tag_ids = jnp.arange(TAGS, dtype=jnp.int32)
    weighted = (tag_ids[:, None] == tags) & (silence > 0)
    sums = jnp.dot(weighted.astype(BF16), rounded, preferred_element_type=F32)
    counts = jnp.sum(weighted.astype(F32), axis=1, keepdims=True)
    counts = jnp.broadcast_to(counts, (TAGS, LANES))

    def exchanged(values, numbers, bit):
        high = jnp.floor(numbers * (1 / 128)) * 128
        lane = lax.broadcasted_iota(jnp.int32, numbers.shape, 1)
        coded = jnp.where(lane == 0, high, numbers - high)
        message = jnp.concatenate([values, coded], axis=1).astype(BF16)
        arrived = swap(message, "tm", bit).astype(F32)
        return arrived[:, :classes], arrived[:, classes : classes + 1] + arrived[:, classes + 1 : classes + 2]

    core = time % 2
    half = TAGS // 2
    sent_sums = lax.dynamic_slice_in_dim(sums, (1 - core) * half, half, 0)
    sent_counts = lax.dynamic_slice_in_dim(counts, (1 - core) * half, half, 0)
    sums = lax.dynamic_slice_in_dim(sums, core * half, half, 0)
    counts = lax.dynamic_slice_in_dim(counts, core * half, half, 0)
    more_sums, more_counts = exchanged(sent_sums, sent_counts, 1)
    sums, counts = sums + more_sums, counts + more_counts
    bit = 2
    while bit < time_size:
        more_sums, more_counts = exchanged(sums, counts, bit)
        sums, counts = sums + more_sums, counts + more_counts
        bit *= 2
    mine = (sums / (counts[:, :1] + 1.0)).astype(BF16)
    theirs = swap(mine, "tm", 1)
    shard_tags = got[:, classes : classes + 1].astype(jnp.int32)
    onehot_mine = (shard_tags == (tag_ids[:half] + core * half + 1)[None, :]).astype(BF16)
    onehot_theirs = (shard_tags == (tag_ids[:half] + (1 - core) * half + 1)[None, :]).astype(BF16)
    calibration = jnp.dot(onehot_mine, mine, preferred_element_type=F32) + jnp.dot(
        onehot_theirs, theirs, preferred_element_type=F32
    )
    scores = got[:, :classes].astype(F32) - calibration
    return scores

SUM_ROWS = TAGS // 2
AUX_ROWS = 16
MESSAGE = SUM_ROWS + AUX_ROWS + 64
SEGS = 128


def as_column(row):
    size = row.shape[1]
    eye = lax.broadcasted_iota(jnp.int32, (size, size), 0) == lax.broadcasted_iota(
        jnp.int32, (size, size), 1
    )
    return jnp.sum(jnp.where(eye, row, jnp.zeros_like(row)), axis=1, keepdims=True)


def iota(shape, dim):
    return lax.broadcasted_iota(jnp.int32, shape, dim)


def to_bf16(mask):
    return mask.astype(F32).astype(BF16)


def labels_kernel(after, owners, silence, tags, placing, weighted, aux):
    owner = owners[...]
    square = (SEGS, SEGS)
    same = as_column(owner) == owner
    slot_row = jnp.sum(jnp.where(same & (iota(square, 0) < iota(square, 1)), 1, 0), axis=0, keepdims=True)
    slot_column = jnp.sum(jnp.where(same & (iota(square, 1) < iota(square, 0)), 1, 0), axis=1, keepdims=True)
    placing[...] = to_bf16(iota(square, 0) == owner * CAP + slot_row)
    chosen = (iota((TAGS, SEGS), 0) == tags[...]) & (silence[...] > 0)
    weighted[...] = to_bf16(chosen)
    named = jnp.where(iota((AUX_ROWS, SEGS), 0) == owner, tags[...] + 1, 0).astype(F32).astype(BF16)
    lane = to_bf16(iota(square, 1) == slot_column + lax.axis_index("tm") * CAP)
    aux[:, 0:SEGS] = jnp.dot(named, lane, preferred_element_type=F32)
    silent = jnp.where(silence[...] > 0, 1.0, 0.0)
    ones = jnp.broadcast_to(silent, (8, SEGS)).astype(BF16)
    columns = as_column(tags[...])
    aux[:, SEGS:] = jnp.zeros((AUX_ROWS, SEGS), F32)
    for h in range(2):
        match = to_bf16(columns == iota((SEGS, SUM_ROWS), 1) + h * SUM_ROWS)
        count = jnp.dot(ones, match, preferred_element_type=F32)
        aux[2 + h : 3 + h, SEGS:] = count[0:1, :]


def picked(have, bit):
    rows, columns = iota((64, SEGS), 0), iota((64, SEGS), 1)
    chosen = columns == (rows // 8) * 16 + bit * 8 + rows % 8
    return jnp.dot(to_bf16(chosen), have, preferred_element_type=F32).astype(BF16)


def split_counts(aux, totals):
    counts = aux[0:2, SEGS:] + aux[2:4, SEGS:]
    high = jnp.floor(counts * (1 / 128)) * 128
    totals[...] = aux
    totals[0:2, SEGS:] = high
    totals[2:4, SEGS:] = counts - high


def send_parts(message, keep, aux, sums, totals, have, bit):
    split_counts(aux, totals)
    message[0:SUM_ROWS, :] = sums.astype(BF16)
    message[SUM_ROWS : SUM_ROWS + AUX_ROWS, :] = totals[...].astype(BF16)
    message[SUM_ROWS + AUX_ROWS :, :] = picked(have, 1 - bit)
    keep[...] = picked(have, bit)


def time_bit(b):
    return lax.div(lax.axis_index("tm"), 1 << b) % 2


def first_kernel(mine, got, placing, weighted, aux, message, sums, totals, keep):
    core = time_bit(0)
    rounded = (mine[...] + got[...].astype(F32)).astype(BF16)
    have = jnp.dot(placing[...], rounded, preferred_element_type=F32).astype(BF16)
    kept = weighted[pl.ds(pl.multiple_of(core * SUM_ROWS, SUM_ROWS), SUM_ROWS), :]
    sent = weighted[pl.ds(pl.multiple_of((1 - core) * SUM_ROWS, SUM_ROWS), SUM_ROWS), :]
    sums[...] = jnp.dot(kept, rounded, preferred_element_type=F32)
    sent = jnp.dot(sent, rounded, preferred_element_type=F32)
    send_parts(message, keep, aux[...], sent, totals, have, core)


def merged(bit, arrived, sums, totals, keep, have):
    have[pl.ds(pl.multiple_of(bit * 64, 64), 64), :] = keep[...]
    have[pl.ds(pl.multiple_of((1 - bit) * 64, 64), 64), :] = arrived[SUM_ROWS + AUX_ROWS :, :]
    total = sums[...] + arrived[0:SUM_ROWS, :].astype(F32)
    aux = totals[...] + arrived[SUM_ROWS : SUM_ROWS + AUX_ROWS, :].astype(F32)
    return total, aux


QUARTER = SUM_ROWS + AUX_ROWS + 32


def time_pair():
    return lax.div(lax.axis_index("tm"), 2) % 4


def picked_quarter(have, value):
    rows, columns = iota((32, SEGS), 0), iota((32, SEGS), 1)
    chosen = columns == (rows // 8) * 32 + value * 8 + rows % 8
    return jnp.dot(to_bf16(chosen), have, preferred_element_type=F32).astype(BF16)


def spread_kernel(arrived, sums, totals, keep, *rest):
    *messages, sums_out, totals_out, keep_out, have = rest
    total, aux = merged(time_bit(0), arrived, sums, totals, keep, have)
    sums_out[...] = total
    split_counts(aux, totals_out)
    total = total.astype(BF16)
    aux = totals_out[...].astype(BF16)
    pair = time_pair()
    held = have[...]
    for n, message in enumerate(messages):
        message[0:SUM_ROWS, :] = total
        message[SUM_ROWS : SUM_ROWS + AUX_ROWS, :] = aux
        message[SUM_ROWS + AUX_ROWS :, :] = picked_quarter(held, pair ^ (n + 1))
    keep_out[...] = picked_quarter(held, pair)


def gather_kernel(after, *rest):
    *arrived, sums, totals, keep, message, sums_out, totals_out, keep_out, have = rest
    pair = time_pair()
    have[pl.ds(pl.multiple_of(pair * 32, 32), 32), :] = keep[...]
    total, aux = sums[...], totals[...]
    for n, part in enumerate(arrived):
        place = pl.ds(pl.multiple_of((pair ^ (n + 1)) * 32, 32), 32)
        have[place, :] = part[SUM_ROWS + AUX_ROWS :, :]
        total = total + part[0:SUM_ROWS, :].astype(F32)
        aux = aux + part[SUM_ROWS : SUM_ROWS + AUX_ROWS, :].astype(F32)
    sums_out[...] = total
    send_parts(message, keep_out, aux, total, totals_out, have[...], time_bit(3))


def last_kernel(after, arrived, sums, totals, keep, calibration, table, have):
    total, aux = merged(time_bit(3), arrived, sums, totals, keep, have)
    table[...] = aux
    both = aux[0:2, SEGS:] + aux[2:4, SEGS:]
    counts = jnp.where(time_bit(0) == 0, both[0:1, :], both[1:2, :])
    calibration[...] = (total / (as_column(counts) + 1.0)).astype(BF16)


def scores_kernel(mine, theirs, table, have, scores):
    named = jnp.where(iota((AUX_ROWS, SEGS), 0) == lax.axis_index("tm"), table[:, 0:SEGS], 0.0)
    row = jnp.sum(named, axis=0, keepdims=True).astype(jnp.int32)
    column = as_column(row)
    ids = iota((SEGS, SUM_ROWS), 1) + 1
    core = time_bit(0)
    near = to_bf16(column == ids + core * SUM_ROWS)
    far = to_bf16(column == ids + (1 - core) * SUM_ROWS)
    scores[...] = (
        have[...].astype(F32)
        - jnp.dot(near, mine[...], preferred_element_type=F32)
        - jnp.dot(far, theirs[...], preferred_element_type=F32)
    )


def small_call(kernel, name, operands, outs, scratch=(), hbm=0):
    return pl.pallas_call(
        kernel,
        in_specs=[ANY_SPEC] * hbm + [VMEM_SPEC] * (len(operands) - hbm),
        out_specs=[VMEM_SPEC] * len(outs),
        out_shape=[jax.ShapeDtypeStruct(*o) for o in outs],
        scratch_shapes=list(scratch),
        compiler_params=SMALL,
        cost_estimate=cost(1 << 24, 1 << 20),
        name=name,
    )(*operands)


def fast_tail(mine, got, act_rest, owners, silence, tags, block_out):
    classes = mine.shape[1]
    sums = ((SUM_ROWS, classes), F32)
    aux = ((AUX_ROWS, 2 * SEGS), F32)
    keep = ((64, classes), BF16)
    message = ((MESSAGE, classes), BF16)
    have = (pltpu.VMEM((SEGS, classes), BF16),)
    placing, weighted, labels = small_call(
        labels_kernel,
        "labels",
        [mine, owners[:, 0][None, :], silence, tags],
        [((SEGS, SEGS), BF16), ((TAGS, SEGS), BF16), aux],
    )
    act_rest, got, placing = lax.optimization_barrier((act_rest, got, placing))
    got_rest = swap(act_rest, "grp", 1)
    state = small_call(
        first_kernel, "first", [mine, got, placing, weighted, labels], [message, sums, aux, keep]
    )
    arrived = swap(state[0], "tm", 1)
    quarter = ((QUARTER, classes), BF16)
    *spread, part_sums, part_totals, part_keep = small_call(
        spread_kernel,
        "spread",
        [arrived, *state[1:]],
        [quarter, quarter, quarter, sums, aux, ((32, classes), BF16)],
        have,
    )
    arrived = [swap(part, "tm", 2 * (n + 1)) for n, part in enumerate(spread)]
    rows = block_out.first()
    state = small_call(
        gather_kernel,
        "gather",
        [in_hbm(rows), *arrived, part_sums, part_totals, part_keep],
        [message, sums, aux, keep],
        have,
        hbm=1,
    )
    partial = block_out.partial(state[1])
    arrived = swap(state[0], "tm", 8)
    block_rows = block_out.rest(partial, got_rest, rows)
    calibration, table, ready = small_call(
        last_kernel,
        "last",
        [in_hbm(block_rows), arrived, *state[1:]],
        [((SUM_ROWS, classes), BF16), aux, ((SEGS, classes), BF16)],
        hbm=1,
    )
    theirs = swap(calibration, "tm", 1)
    [scores] = small_call(
        scores_kernel, "scores", [calibration, theirs, table, ready], [((SEGS, classes), F32)]
    )
    return block_rows, scores


def fast_body(
    frames,
    ln_gain,
    w_value,
    w_gate,
    conv_taps,
    bn_scale,
    bn_shift,
    w_out,
    w_classes,
    seg_lengths,
    owners,
    silence,
    tags,
):
    count = frames.shape[0]
    time_size = lax.axis_size("tm")
    own_rows = count // 2
    glu = run_fast_glu(frames, ln_gain, w_value, w_gate)
    odd = lax.axis_index("tm") % 2 == 1
    first, last = glu[:HALO], glu[count - HALO :]
    across = [(i, i + 1) for i in range(1, time_size - 1, 2)]
    across += [(j, i) for i, j in across]
    near = swap(jnp.where(odd, first, last), "tm", 1)
    far = lax.ppermute(jnp.where(odd, last, first), "tm", across)
    bn = (conv_taps, bn_scale, bn_shift, seg_lengths)
    act_first, pooled = run_early(FIRST, glu, *bn)
    got_first = swap(act_first, "grp", 1)
    act_rest, act_own, mine, sent = run_late(
        glu, near, far, *bn, pooled, frames, w_out, w_classes
    )
    sent, got_first = lax.optimization_barrier((sent, got_first))
    got = swap(sent, "grp", 1)

    class block_out:
        def first():
            return run_out_first(frames, act_own, got_first, w_out)

        def partial(after):
            return run_out_partial(after, frames, act_own, w_out)

        def rest(partial, got_rest, rows):
            return run_out_rest(partial, got_rest, w_out, rows)

    block_rows, scores = fast_tail(mine, got, act_rest, owners, silence, tags, block_out)
    return (block_rows[None, None], scores)


def body(*args):
    rows = args[0].shape[0] // lax.axis_size("grp")
    channels = args[2].shape[1]
    fits = rows == 3 * BLOCK and channels % BLOCK == 0
    fits = fits and lax.axis_size("grp") == 2 and lax.axis_size("tm") == 16
    fits = fits and args[4].shape[0] == 31 and args[8].shape[1] == 512 and args[9].shape[1] == SEGS
    return (fast_body if fits else general_body)(*args)


def solution(mesh):
    in_specs = (
        P("tm", None),
        P(),
        P(None, "grp"),
        P(None, "grp"),
        P(None, "grp"),
        P("grp"),
        P("grp"),
        P(),
        P(),
        P("tm", None),
        P("tm", None),
        P("tm", None),
        P("tm", None),
    )
    out_specs = (P("tm", "grp", None, None), P("tm", "grp"))
    return jax.shard_map(body, mesh=mesh, in_specs=in_specs, out_specs=out_specs, check_vma=False)
```

```python
import functools

import jax
import jax.numpy as jnp
from jax import lax
from jax.experimental import pallas as pl
from jax.experimental.pallas import tpu as pltpu
from jax.sharding import PartitionSpec as P

TAGS = 256
CAP = 8
HALO = 16
BLOCK = 256
LANES = 128
VMEM_LIMIT = 48 << 20
F32, BF16 = jnp.float32, jnp.bfloat16


def sigmoid(v):
    return 0.5 * jnp.tanh(0.5 * v) + 0.5


def params():
    return pltpu.CompilerParams(
        dimension_semantics=("arbitrary",), vmem_limit_bytes=VMEM_LIMIT
    )


def whole(shape):
    return pl.BlockSpec(shape, lambda i, s: (0,) * len(shape))


def segment_mask(first, count, starts, ends):
    rows = first + lax.broadcasted_iota(jnp.int32, (starts.shape[0], count), 1)
    return (rows >= starts) & (rows < ends)


def glu_kernel(s, frames, gain, w_value, w_gate, starts, ends, glu, pooled, *, own_rows):
    step = pl.program_id(0)
    block = frames.shape[0]
    own_first = s[0] * own_rows

    @pl.when(step == 0)
    def _():
        pooled[...] = jnp.zeros_like(pooled)

    first = step * block

    @pl.when((first < own_first + own_rows) & (first + block > own_first))
    def _():
        rows = first + lax.broadcasted_iota(jnp.int32, (starts.shape[0], block), 1)
        low = jnp.maximum(starts[...], own_first)
        high = jnp.minimum(ends[...], own_first + own_rows)
        mask = ((rows >= low) & (rows < high)).astype(F32).astype(BF16)
        pooled[...] += jnp.dot(mask, frames[...], preferred_element_type=F32)

    half = block // 2
    for part in range(2):
        rows = pl.ds(part * half, half)
        x = frames[rows, :].astype(F32)
        center = jnp.mean(x, axis=-1, keepdims=True)
        x = x - center
        spread = jnp.mean(x * x, axis=-1, keepdims=True)
        normed = (x * lax.rsqrt(spread + 1e-05) * gain[...]).astype(BF16)
        value = jnp.dot(normed, w_value[...], preferred_element_type=F32)
        gate = jnp.dot(normed, w_gate[...], preferred_element_type=F32)
        glu[rows, :] = (value * sigmoid(gate)).astype(BF16)


def conv_kernel(s, window, taps, scale, shift, starts, ends, act, pooled, xs, *, taps_n):
    step = pl.program_id(0)
    block, channels = act.shape
    tiles = [(c, min(LANES, channels - c)) for c in range(0, channels, LANES)]
    for t, (c, w) in enumerate(tiles):
        xs[t, :, 0:w] = window[:, c : c + w].astype(F32)

    def tile(t, c, w):
        lanes = pl.ds(c, w)
        for r in range(0, block, 64):
            total = jnp.zeros((64, w), F32)
            for k in range(taps_n):
                total = total + taps[k : k + 1, lanes] * xs[t, pl.ds(r + 1 + k, 64), 0:w]
            v = total * scale[:, lanes] + shift[:, lanes]
            act[pl.ds(r, 64), lanes] = (v * sigmoid(v)).astype(BF16)

    if channels % LANES == 0:

        @pl.loop(0, channels // LANES)
        def _(t):
            tile(t, pl.multiple_of(t * LANES, LANES), LANES)
    else:
        for t, (c, w) in enumerate(tiles):
            tile(t, c, w)

    first = s[0] + step * block
    mask = segment_mask(first, block, starts[...], ends[...]).astype(F32).astype(BF16)
    part = jnp.dot(mask, act[...], preferred_element_type=F32)

    @pl.when(step == 0)
    def _():
        pooled[...] = part

    @pl.when(step > 0)
    def _():
        pooled[...] += part


def logits_kernel(s, frames_pooled, pooled, w_out, w_classes, starts, ends, out):
    mixed = jnp.dot(pooled[...].astype(BF16), w_out[...], preferred_element_type=F32)
    inverse = 1.0 / (ends[...] - starts[...]).astype(F32)
    mean = ((frames_pooled[...] + mixed) * inverse).astype(BF16)
    out[...] = jnp.dot(mean, w_classes[...], preferred_element_type=F32)


def out_kernel(s, *refs):
    *pairs, frames, out = refs
    total = frames[...].astype(F32)
    for act, w_out in zip(pairs[0::2], pairs[1::2]):
        total = total + jnp.dot(act[...], w_out[...], preferred_element_type=F32)
    out[...] = total.astype(BF16)


def run_glu(group_index, own_rows, frames, gain, w_value, w_gate, starts, ends):
    count, width = frames.shape
    channels = w_value.shape[1]
    segs = starts.shape[0]
    return pl.pallas_call(
        functools.partial(glu_kernel, own_rows=own_rows),
        grid_spec=pltpu.PrefetchScalarGridSpec(
            num_scalar_prefetch=1,
            grid=(count // BLOCK,),
            in_specs=[
                pl.BlockSpec((BLOCK, width), lambda i, s: (i, 0)),
                whole((1, width)),
                whole((width, channels)),
                whole((width, channels)),
                whole((segs, 1)),
                whole((segs, 1)),
            ],
            out_specs=[
                pl.BlockSpec((BLOCK, channels), lambda i, s: (i, 0)),
                whole((segs, width)),
            ],
        ),
        out_shape=[
            jax.ShapeDtypeStruct((count, channels), BF16),
            jax.ShapeDtypeStruct((segs, width), F32),
        ],
        compiler_params=params(),
        name="glu",
    )(group_index, frames, gain, w_value, w_gate, starts, ends)


def run_conv(base, rows, padded, taps, scale, shift, starts, ends):
    channels = padded.shape[1]
    segs = starts.shape[0]
    tiles = pl.cdiv(channels, LANES)
    return pl.pallas_call(
        functools.partial(conv_kernel, taps_n=taps.shape[0]),
        grid_spec=pltpu.PrefetchScalarGridSpec(
            num_scalar_prefetch=1,
            grid=(rows // BLOCK,),
            in_specs=[
                pl.BlockSpec(
                    (pl.Element(BLOCK + 2 * HALO), pl.Element(channels)),
                    lambda i, s: (pl.multiple_of(s[0] + i * BLOCK, HALO), 0),
                ),
                whole(taps.shape),
                whole((1, channels)),
                whole((1, channels)),
                whole((segs, 1)),
                whole((segs, 1)),
            ],
            out_specs=[
                pl.BlockSpec((BLOCK, channels), lambda i, s: (i, 0)),
                whole((segs, channels)),
            ],
            scratch_shapes=[pltpu.VMEM((tiles, BLOCK + 2 * HALO, LANES), F32)],
        ),
        out_shape=[
            jax.ShapeDtypeStruct((rows, channels), BF16),
            jax.ShapeDtypeStruct((segs, channels), F32),
        ],
        compiler_params=params(),
        name="conv",
    )(base, padded, taps, scale, shift, starts, ends)


def run_logits(group_index, frames_pooled, pooled, w_out, w_classes, starts, ends):
    segs, channels = pooled.shape
    width, classes = w_classes.shape
    return pl.pallas_call(
        logits_kernel,
        grid_spec=pltpu.PrefetchScalarGridSpec(
            num_scalar_prefetch=1,
            grid=(1,),
            in_specs=[
                whole((segs, width)),
                whole((segs, channels)),
                pl.BlockSpec((channels, width), lambda i, s: (s[0], 0)),
                whole((width, classes)),
                whole((segs, 1)),
                whole((segs, 1)),
            ],
            out_specs=whole((segs, classes)),
        ),
        out_shape=jax.ShapeDtypeStruct((segs, classes), F32),
        compiler_params=params(),
        name="logits",
    )(group_index, frames_pooled, pooled, w_out, w_classes, starts, ends)


def run_out(scalars, sources, w_out, frames, rows):
    width = frames.shape[1]
    block = BLOCK if rows % BLOCK == 0 else rows
    steps = rows // block
    in_specs, operands = [], []
    for act, place in sources:
        in_specs.append(pl.BlockSpec((block, act.shape[1]), lambda i, s: (i, 0)))
        in_specs.append(
            pl.BlockSpec((act.shape[1], width), functools.partial(lambda p, i, s: (s[p], 0), place))
        )
        operands += [act, w_out]
    in_specs.append(pl.BlockSpec((block, width), lambda i, s: (s[0] * steps + i, 0)))
    return pl.pallas_call(
        out_kernel,
        grid_spec=pltpu.PrefetchScalarGridSpec(
            num_scalar_prefetch=1,
            grid=(steps,),
            in_specs=in_specs,
            out_specs=pl.BlockSpec((block, width), lambda i, s: (i, 0)),
        ),
        out_shape=jax.ShapeDtypeStruct((rows, width), BF16),
        compiler_params=params(),
        name="block_out",
    )(scalars, *operands, frames)


def swap(value, axis, bit):
    count = lax.axis_size(axis)
    return lax.ppermute(value, axis, [(i, i ^ bit) for i in range(count)])


def general_body(
    frames,
    ln_gain,
    w_value,
    w_gate,
    conv_taps,
    bn_scale,
    bn_shift,
    w_out,
    w_classes,
    seg_lengths,
    owners,
    silence,
    tags,
):
    count, width = frames.shape
    channels = w_value.shape[1]
    group_size = lax.axis_size("grp")
    time_size = lax.axis_size("tm")
    group = lax.axis_index("grp")
    time = lax.axis_index("tm")
    own_rows = count // group_size
    lengths = seg_lengths[0]
    segs = lengths.shape[0]
    order = jnp.arange(segs, dtype=jnp.int32)
    ends = jnp.sum(
        jnp.where(order[None, :] <= order[:, None], lengths[None, :], 0), axis=1, keepdims=True
    )
    starts = ends - lengths[:, None]
    group_scalar = group[None].astype(jnp.int32)

    glu, frames_pooled = run_glu(
        group_scalar, own_rows, frames, ln_gain[None, :], w_value, w_gate, starts, ends
    )
    up = [(i, i + 1) for i in range(time_size - 1)]
    down = [(j, i) for i, j in up]
    before = lax.ppermute(glu[count - HALO :], "tm", up)
    after = lax.ppermute(glu[:HALO], "tm", down)
    padded = jnp.concatenate([before, glu, after], axis=0)
    bn = (conv_taps, bn_scale[None, :], bn_shift[None, :], starts, ends)

    if group_size == 2:
        other = 1 - group_scalar
        act_other, pooled_other = run_conv(other * own_rows, own_rows, padded, *bn)
        act_got = swap(act_other, "grp", 1)
        act_own, pooled_own = run_conv(group_scalar * own_rows, own_rows, padded, *bn)
        pooled = pooled_other + pooled_own
        sources = [(act_own, 0), (act_got, 1)]
        scalars = jnp.concatenate([group_scalar, other])
    else:
        act, pooled = run_conv(jnp.zeros((1,), jnp.int32), count, padded, *bn)
        rows = lax.all_to_all(act, "grp", split_axis=0, concat_axis=1, tiled=True)
        sources = [(rows, 1)]
        scalars = jnp.concatenate([group_scalar, jnp.zeros((1,), jnp.int32)])

    logits = run_logits(group_scalar, frames_pooled, pooled, w_out, w_classes, starts, ends)

    scores = tail(logits, owners, silence, tags)

    block_rows = run_out(scalars, sources, w_out, frames, own_rows)
    return (block_rows[None, None], scores)


def in_hbm(value):
    return pltpu.with_memory_space_constraint(value, pltpu.HBM)


def cost(flops, traffic):
    return pl.CostEstimate(flops=flops, bytes_accessed=traffic, transcendentals=0)


VMEM_SPEC = pl.BlockSpec(memory_space=pltpu.VMEM)
SMEM_SPEC = pl.BlockSpec(memory_space=pltpu.SMEM)
ANY_SPEC = pl.BlockSpec(memory_space=pltpu.HBM)
SMALL = pltpu.CompilerParams(vmem_limit_bytes=8 << 20)


GLU_LEAD = 3
HALF = 96
REST = BLOCK - HALF
FIRST = BLOCK + HALF


def fast_glu_kernel(
    frames, gain_in, w_value, w_gate, glu, rows_in, wv, wg, gain, normed, row_sem, col_sem
):
    count, width = frames.shape
    channels = wv.shape[1]
    blocks = count // BLOCK
    columns = channels // BLOCK

    def row_copy(b):
        rows = pl.ds(b * BLOCK, BLOCK)
        return pltpu.make_async_copy(frames.at[rows, :], rows_in.at[rows, :], row_sem.at[b])

    def column_copies(c):
        cols = pl.ds(c * BLOCK, BLOCK)
        return (
            pltpu.make_async_copy(w_value.at[:, cols], wv.at[:, cols], col_sem.at[0, c]),
            pltpu.make_async_copy(w_gate.at[:, cols], wg.at[:, cols], col_sem.at[1, c]),
        )

    def normalize(b):
        row_copy(b).wait()
        x = rows_in[pl.ds(b * BLOCK, BLOCK), :].astype(F32)
        center = jnp.mean(x, axis=-1, keepdims=True)
        x = x - center
        spread = jnp.mean(x * x, axis=-1, keepdims=True)
        factor = 0.5 * lax.rsqrt(spread + 1e-05)
        normed[b % GLU_LEAD] = (x * factor * gain[...].reshape(1, -1)).astype(BF16)

    def gated(b, c):
        cols = pl.ds(c * BLOCK, BLOCK)
        rows = normed[b % GLU_LEAD]
        value = jnp.dot(rows, wv[:, cols], preferred_element_type=F32)
        gate = jnp.dot(rows, wg[:, cols], preferred_element_type=F32)
        glu[pl.ds(b * BLOCK, BLOCK), cols] = (value * jnp.tanh(gate) + value).astype(BF16)

    gain_copy = pltpu.make_async_copy(gain_in, gain, row_sem.at[blocks])
    gain_copy.start()
    for b in range(GLU_LEAD):
        row_copy(b).start()
    for c in range(columns):
        for copy in column_copies(c):
            copy.start()
    for b in range(GLU_LEAD, blocks):
        row_copy(b).start()
    gain_copy.wait()
    for b in range(GLU_LEAD):
        normalize(b)
    for c in range(columns):
        for copy in column_copies(c):
            copy.wait()
        for b in range(GLU_LEAD):
            gated(b, c)
    for b in range(GLU_LEAD, blocks):
        normalize(b)
        for c in range(columns):
            gated(b, c)


def run_fast_glu(frames, gain, w_value, w_gate):
    count, width = frames.shape
    channels = w_value.shape[1]
    return pl.pallas_call(
        fast_glu_kernel,
        in_specs=[ANY_SPEC] * 4,
        out_specs=VMEM_SPEC,
        out_shape=jax.ShapeDtypeStruct((count, channels), BF16),
        scratch_shapes=[
            pltpu.VMEM((count, width), BF16),
            pltpu.VMEM((width, channels), BF16),
            pltpu.VMEM((width, channels), BF16),
            pltpu.VMEM((width,), F32),
            pltpu.VMEM((GLU_LEAD, BLOCK, width), BF16),
            pltpu.SemaphoreType.DMA((count // BLOCK + 1,)),
            pltpu.SemaphoreType.DMA((2, channels // BLOCK)),
        ],
        compiler_params=pltpu.CompilerParams(vmem_limit_bytes=14 << 20),
        cost_estimate=cost(4 * count * width * channels, 12 << 20),
        name="glu",
    )(in_hbm(frames), in_hbm(gain), in_hbm(w_value), in_hbm(w_gate))


def segment_bounds(lengths):
    row = lengths[...]
    size = row.shape[1]
    earlier = iota((size, size), 1) <= iota((size, size), 0)
    ends = jnp.sum(jnp.where(earlier, row, 0), axis=1, keepdims=True)
    return ends - as_column(row), ends


def half_places(count, group):
    own = count // 2
    last = count - BLOCK
    return (
        jnp.where(group == 0, BLOCK, own),
        jnp.where(group == 0, 0, last),
        jnp.where(group == 0, BLOCK, 0),
        jnp.where(group == 0, 0, own - BLOCK),
    )


def convolve(glu, halos, taps, scale, shift, xs, plan):
    count, channels = glu.shape
    taps_n = taps.shape[0]
    outer = BLOCK + HALO

    @pl.loop(0, channels // LANES)
    def _(t):
        lanes = pl.ds(pl.multiple_of(t * LANES, LANES), LANES)
        half_scale = 0.5 * scale[lanes].reshape(1, -1)
        half_shift = 0.5 * shift[lanes].reshape(1, -1)
        tap = [
            jnp.broadcast_to((taps[k : k + 1, lanes] * half_scale).astype(BF16), (16, LANES))
            for k in range(taps_n)
        ]
        for rows_n, source, act, place in plan:
            source = pl.multiple_of(source, 32)
            if rows_n:
                rows = pl.ds(pl.multiple_of(source - HALO, HALO), rows_n + 2 * HALO)
                xs[0 : rows_n + 2 * HALO, :] = glu[rows, lanes].astype(F32)
            else:
                near, far = halos
                odd = lax.axis_index("tm") % 2 == 1
                inside = jnp.where(odd, source == 0, source != 0)
                halo = jnp.where(inside, near[:, lanes].astype(F32), far[:, lanes].astype(F32))

                @pl.when(source == 0)
                def _():
                    xs[0:HALO, :] = halo
                    xs[HALO:, :] = glu[0:outer, lanes].astype(F32)

                @pl.when(source != 0)
                def _():
                    xs[0:outer, :] = glu[count - outer : count, lanes].astype(F32)
                    xs[outer:, :] = halo

            sums = {}

            def add(block, value):
                stack, level = sums.setdefault(block, []), 0
                while stack and stack[-1][0] == level:
                    value, level = stack.pop()[1] + value, level + 1
                stack.append((level, value))

            def finished(block):
                (_, value), *stack = reversed(sums.pop(block))
                for _, earlier in stack:
                    value = value + earlier
                return value.astype(F32)

            rows_n = rows_n or BLOCK
            for m in range(rows_n // 16 + 1):
                for r in range(16):
                    if m == rows_n // 16 and r + 16 >= taps_n:
                        continue
                    shifted = xs[pl.ds(16 * m + r + 1, 16), :].astype(BF16)
                    if m < rows_n // 16:
                        add(m, tap[r] * shifted)
                    if m > 0 and r + 16 < taps_n:
                        add(m - 1, tap[r + 16] * shifted)
                if m > 0:
                    total = half_shift + finished(m - 1)
                    rows = pl.ds(pl.multiple_of(place + 16 * (m - 1), 16), 16)
                    act[rows, lanes] = (total * jnp.tanh(total) + total).astype(BF16)


def pool(plan, starts, ends):
    total = None
    for rows_n, source, act, place in plan:
        rows_n = rows_n or BLOCK
        mask = to_bf16(segment_mask(source, rows_n, starts, ends))
        rows = pl.ds(pl.multiple_of(place, 32), rows_n)
        part = jnp.dot(mask, act[rows, :], preferred_element_type=F32)
        total = part if total is None else total + part
    return total


def early_kernel(glu, taps, scale, shift, lengths, act, pooled, xs):
    count = glu.shape[0]
    inner = half_places(count, 1 - lax.axis_index("grp"))[0]
    plan = [(BLOCK, inner, act, 0), (HALF, inner + BLOCK, act, BLOCK)]
    convolve(glu, None, taps, scale, shift, xs, plan)
    starts, ends = segment_bounds(lengths)
    pooled[...] = pool(plan, starts, ends)


def late_kernel(
    glu, before, after, taps, scale, shift, lengths, pooled, frames, w_out, w_classes,
    act_other, act_own, kept, sent, xs, rows_in, w_mine, w_cls, sem,
):
    count, channels = glu.shape
    group = lax.axis_index("grp")
    own_rows = act_own.shape[0]
    own_first = pl.multiple_of(group * own_rows, own_rows)
    copies = [
        pltpu.make_async_copy(
            w_out.at[pl.ds(pl.multiple_of(group * channels, channels), channels), :], w_mine, sem.at[0]
        ),
        pltpu.make_async_copy(frames.at[pl.ds(own_first, own_rows), :], rows_in, sem.at[1]),
        pltpu.make_async_copy(w_classes, w_cls, sem.at[2]),
    ]
    for copy in copies:
        copy.start()
    inner, outer, inner_at, outer_at = half_places(count, group)
    far_inner, far_outer, _, _ = half_places(count, 1 - group)
    plan = [(REST, far_inner + FIRST, act_other, 0), (0, far_outer, act_other, REST)]
    plan += [(BLOCK, inner + b, act_own, inner_at + b) for b in (0, BLOCK)]
    plan += [(0, outer, act_own, outer_at)]
    convolve(glu, (before, after), taps, scale, shift, xs, plan)
    starts, ends = segment_bounds(lengths)
    total = (pooled[...] + pool(plan, starts, ends)).astype(BF16)
    for copy in copies:
        copy.wait()
    total = jnp.dot(total, w_mine[...], preferred_element_type=F32)
    mask = to_bf16(segment_mask(own_first, own_rows, starts, ends))
    total = total + jnp.dot(mask, rows_in[...], preferred_element_type=F32)
    inverse = 1.0 / (ends - starts).astype(F32)
    logits = jnp.dot((total * inverse).astype(BF16), w_cls[...], preferred_element_type=F32)
    half = logits.shape[1] // 2
    low, high = logits[:, :half], logits[:, half:]
    kept[...] = jnp.where(group == 0, low, high)
    sent[...] = jnp.where(group == 0, high, low).astype(BF16)


def run_early(rows, glu, taps, scale, shift, lengths):
    channels = glu.shape[1]
    return pl.pallas_call(
        early_kernel,
        in_specs=[VMEM_SPEC] * 5,
        out_specs=[VMEM_SPEC, VMEM_SPEC],
        out_shape=[
            jax.ShapeDtypeStruct((rows, channels), BF16),
            jax.ShapeDtypeStruct((lengths.shape[1], channels), F32),
        ],
        scratch_shapes=[pltpu.VMEM((BLOCK + 2 * HALO, LANES), F32)],
        compiler_params=SMALL,
        cost_estimate=cost(1 << 20, 1 << 16),
        name="conv_early",
    )(glu, taps, scale, shift, lengths)


def run_late(glu, before, after, taps, scale, shift, lengths, pooled, frames, w_out, w_classes):
    count, channels = glu.shape
    segs = lengths.shape[1]
    width, classes = w_classes.shape
    own_rows = count // 2
    return pl.pallas_call(
        late_kernel,
        in_specs=[VMEM_SPEC] * 8 + [ANY_SPEC] * 3,
        out_specs=[VMEM_SPEC] * 4,
        out_shape=[
            jax.ShapeDtypeStruct((own_rows - FIRST, channels), BF16),
            jax.ShapeDtypeStruct((own_rows, channels), BF16),
            jax.ShapeDtypeStruct((segs, classes // 2), F32),
            jax.ShapeDtypeStruct((segs, classes // 2), BF16),
        ],
        scratch_shapes=[
            pltpu.VMEM((BLOCK + 2 * HALO, LANES), F32),
            pltpu.VMEM((own_rows, width), BF16),
            pltpu.VMEM((channels, width), BF16),
            pltpu.VMEM((width, classes), BF16),
            pltpu.SemaphoreType.DMA((3,)),
        ],
        compiler_params=pltpu.CompilerParams(vmem_limit_bytes=14 << 20),
        cost_estimate=cost(1 << 20, 1 << 16),
        name="conv_late",
    )(
        glu, before, after, taps, scale, shift, lengths, pooled,
        in_hbm(frames), in_hbm(w_out), in_hbm(w_classes),
    )


def rest_places(rows, group):
    _, _, inner_at, outer_at = half_places(2 * rows, group)
    return inner_at, [(0, REST, inner_at + FIRST), (REST, BLOCK, outer_at)]


def half_block(at, rows):
    return pl.ds(pl.multiple_of(at, 32), rows)


def half_rows(channels, half):
    return pl.ds(pl.multiple_of(half * channels, channels), channels)


def own_row_copy(frames, buf, sem, at, own_rows):
    first = lax.axis_index("grp") * own_rows + at
    return pltpu.make_async_copy(frames.at[half_block(first, buf.shape[0]), :], buf, sem)


def out_first_kernel(frames, own, got, w_out, out, buf, sem):
    rows, channels = own.shape
    group = lax.axis_index("grp")
    first = rest_places(rows, group)[0]
    copy = own_row_copy(frames, buf, sem, first, rows)
    copy.start()
    mine, theirs = half_rows(channels, group), half_rows(channels, 1 - group)
    place = half_block(first, FIRST)
    total = jnp.dot(own[place, :], w_out[mine, :], preferred_element_type=F32) + jnp.dot(
        got[...], w_out[theirs, :], preferred_element_type=F32
    )
    copy.wait()
    buf[...] = (total + buf[...].astype(F32)).astype(BF16)
    out_copy = pltpu.make_async_copy(buf, out.at[place, :], sem)
    out_copy.start()
    out_copy.wait()


def out_partial_kernel(after, frames, own, w_out, partial, buf, sem):
    rows, channels = own.shape
    group = lax.axis_index("grp")
    rest = rest_places(rows, group)[1]
    copies = [
        own_row_copy(frames, buf.at[pl.ds(n, r), :], sem.at[i], at, rows)
        for i, (n, r, at) in enumerate(rest)
    ]
    for copy in copies:
        copy.start()
    mine = half_rows(channels, group)
    for copy, (n, r, at) in zip(copies, rest):
        total = jnp.dot(own[half_block(at, r), :], w_out[mine, :], preferred_element_type=F32)
        copy.wait()
        partial[n : n + r, :] = total + buf[n : n + r, :].astype(F32)


def out_rest_kernel(partial, got, w_out, earlier, out, buf, out_sem):
    rest, channels = got.shape
    group = lax.axis_index("grp")
    theirs = half_rows(channels, 1 - group)
    copies = []
    for i, (n, r, at) in enumerate(rest_places(rest + FIRST, group)[1]):
        total = jnp.dot(got[n : n + r, :], w_out[theirs, :], preferred_element_type=F32)
        buf[n : n + r, :] = (total + partial[n : n + r, :]).astype(BF16)
        copies.append(
            pltpu.make_async_copy(buf.at[pl.ds(n, r), :], out.at[half_block(at, r), :], out_sem.at[i])
        )
        copies[-1].start()
    for copy in copies:
        copy.wait()


def run_out_first(frames, own, got, w_out):
    width = frames.shape[1]
    return pl.pallas_call(
        out_first_kernel,
        in_specs=[ANY_SPEC] + [VMEM_SPEC] * 3,
        out_specs=ANY_SPEC,
        out_shape=jax.ShapeDtypeStruct((own.shape[0], width), BF16),
        scratch_shapes=[pltpu.VMEM((FIRST, width), BF16), pltpu.SemaphoreType.DMA(())],
        compiler_params=SMALL,
        cost_estimate=cost(1 << 24, 1 << 20),
        name="out_first",
    )(in_hbm(frames), own, got, w_out)


def run_out_partial(after, frames, own, w_out):
    rows = own.shape[0] - FIRST
    width = frames.shape[1]
    return pl.pallas_call(
        out_partial_kernel,
        in_specs=[VMEM_SPEC, ANY_SPEC, VMEM_SPEC, VMEM_SPEC],
        out_specs=VMEM_SPEC,
        out_shape=jax.ShapeDtypeStruct((rows, width), F32),
        scratch_shapes=[
            pltpu.VMEM((rows, width), BF16),
            pltpu.SemaphoreType.DMA((2,)),
        ],
        compiler_params=SMALL,
        cost_estimate=cost(1 << 24, 1 << 20),
        name="out_partial",
    )(after, in_hbm(frames), own, w_out)


def run_out_rest(partial, got, w_out, earlier):
    rows, channels = got.shape
    width = w_out.shape[1]
    return pl.pallas_call(
        out_rest_kernel,
        in_specs=[VMEM_SPEC] * 3 + [ANY_SPEC],
        out_specs=ANY_SPEC,
        out_shape=jax.ShapeDtypeStruct(earlier.shape, BF16),
        input_output_aliases={3: 0},
        scratch_shapes=[
            pltpu.VMEM((rows, width), BF16),
            pltpu.SemaphoreType.DMA((2,)),
        ],
        compiler_params=SMALL,
        cost_estimate=cost(1 << 24, 1 << 20),
        name="out_rest",
    )(partial, got, w_out, earlier)


def tail(logits, owners, silence, tags):
    group_size = lax.axis_size("grp")
    time_size = lax.axis_size("tm")
    group = lax.axis_index("grp")
    time = lax.axis_index("tm")
    segs = logits.shape[0]
    order = jnp.arange(segs, dtype=jnp.int32)

    bit = group_size // 2
    while bit:
        half = logits.shape[1] // 2
        upper = (group // bit) % 2
        kept = lax.dynamic_slice_in_dim(logits, upper * half, half, 1)
        sent = lax.dynamic_slice_in_dim(logits, (1 - upper) * half, half, 1)
        logits = kept + swap(sent.astype(BF16), "grp", bit).astype(F32)
        bit //= 2
    classes = logits.shape[1]

    owner_ids = owners[:, 0]
    earlier = order[None, :] < order[:, None]
    slot = jnp.sum(((owner_ids[:, None] == owner_ids[None, :]) & earlier).astype(jnp.int32), axis=1)
    dest = owner_ids * CAP + slot
    slots = time_size * CAP
    placing = (dest[None, :] == jnp.arange(slots, dtype=jnp.int32)[:, None]).astype(BF16)
    rounded = logits.astype(BF16)
    tag_numbers = (tags[0] + 1).astype(BF16)
    pad = jnp.zeros((segs, LANES - 1), BF16)
    labelled = jnp.concatenate([rounded, tag_numbers[:, None], pad], axis=1)
    send = jnp.dot(placing, labelled, preferred_element_type=F32).astype(BF16)
    got = lax.all_to_all(send, "tm", split_axis=0, concat_axis=0, tiled=True)

    tag_ids = jnp.arange(TAGS, dtype=jnp.int32)
    weighted = (tag_ids[:, None] == tags) & (silence > 0)
    sums = jnp.dot(weighted.astype(BF16), rounded, preferred_element_type=F32)
    counts = jnp.sum(weighted.astype(F32), axis=1, keepdims=True)
    counts = jnp.broadcast_to(counts, (TAGS, LANES))

    def exchanged(values, numbers, bit):
        high = jnp.floor(numbers * (1 / 128)) * 128
        lane = lax.broadcasted_iota(jnp.int32, numbers.shape, 1)
        coded = jnp.where(lane == 0, high, numbers - high)
        message = jnp.concatenate([values, coded], axis=1).astype(BF16)
        arrived = swap(message, "tm", bit).astype(F32)
        return arrived[:, :classes], arrived[:, classes : classes + 1] + arrived[:, classes + 1 : classes + 2]

    core = time % 2
    half = TAGS // 2
    sent_sums = lax.dynamic_slice_in_dim(sums, (1 - core) * half, half, 0)
    sent_counts = lax.dynamic_slice_in_dim(counts, (1 - core) * half, half, 0)
    sums = lax.dynamic_slice_in_dim(sums, core * half, half, 0)
    counts = lax.dynamic_slice_in_dim(counts, core * half, half, 0)
    more_sums, more_counts = exchanged(sent_sums, sent_counts, 1)
    sums, counts = sums + more_sums, counts + more_counts
    bit = 2
    while bit < time_size:
        more_sums, more_counts = exchanged(sums, counts, bit)
        sums, counts = sums + more_sums, counts + more_counts
        bit *= 2
    mine = (sums / (counts[:, :1] + 1.0)).astype(BF16)
    theirs = swap(mine, "tm", 1)
    shard_tags = got[:, classes : classes + 1].astype(jnp.int32)
    onehot_mine = (shard_tags == (tag_ids[:half] + core * half + 1)[None, :]).astype(BF16)
    onehot_theirs = (shard_tags == (tag_ids[:half] + (1 - core) * half + 1)[None, :]).astype(BF16)
    calibration = jnp.dot(onehot_mine, mine, preferred_element_type=F32) + jnp.dot(
        onehot_theirs, theirs, preferred_element_type=F32
    )
    scores = got[:, :classes].astype(F32) - calibration
    return scores

SUM_ROWS = TAGS // 2
AUX_ROWS = 16
MESSAGE = SUM_ROWS + AUX_ROWS + 64
SEGS = 128


def as_column(row):
    size = row.shape[1]
    eye = lax.broadcasted_iota(jnp.int32, (size, size), 0) == lax.broadcasted_iota(
        jnp.int32, (size, size), 1
    )
    return jnp.sum(jnp.where(eye, row, jnp.zeros_like(row)), axis=1, keepdims=True)


def iota(shape, dim):
    return lax.broadcasted_iota(jnp.int32, shape, dim)


def to_bf16(mask):
    return mask.astype(F32).astype(BF16)


def labels_kernel(after, owners, silence, tags, placing, weighted, aux):
    owner = owners[...]
    square = (SEGS, SEGS)
    same = as_column(owner) == owner
    slot_row = jnp.sum(jnp.where(same & (iota(square, 0) < iota(square, 1)), 1, 0), axis=0, keepdims=True)
    slot_column = jnp.sum(jnp.where(same & (iota(square, 1) < iota(square, 0)), 1, 0), axis=1, keepdims=True)
    placing[...] = to_bf16(iota(square, 0) == owner * CAP + slot_row)
    chosen = (iota((TAGS, SEGS), 0) == tags[...]) & (silence[...] > 0)
    weighted[...] = to_bf16(chosen)
    named = jnp.where(iota((AUX_ROWS, SEGS), 0) == owner, tags[...] + 1, 0).astype(F32).astype(BF16)
    lane = to_bf16(iota(square, 1) == slot_column + lax.axis_index("tm") * CAP)
    aux[:, 0:SEGS] = jnp.dot(named, lane, preferred_element_type=F32)
    silent = jnp.where(silence[...] > 0, 1.0, 0.0)
    ones = jnp.broadcast_to(silent, (8, SEGS)).astype(BF16)
    columns = as_column(tags[...])
    aux[:, SEGS:] = jnp.zeros((AUX_ROWS, SEGS), F32)
    for h in range(2):
        match = to_bf16(columns == iota((SEGS, SUM_ROWS), 1) + h * SUM_ROWS)
        count = jnp.dot(ones, match, preferred_element_type=F32)
        aux[2 + h : 3 + h, SEGS:] = count[0:1, :]


def picked(have, bit):
    rows, columns = iota((64, SEGS), 0), iota((64, SEGS), 1)
    chosen = columns == (rows // 8) * 16 + bit * 8 + rows % 8
    return jnp.dot(to_bf16(chosen), have, preferred_element_type=F32).astype(BF16)


def split_counts(aux, totals):
    counts = aux[0:2, SEGS:] + aux[2:4, SEGS:]
    high = jnp.floor(counts * (1 / 128)) * 128
    totals[...] = aux
    totals[0:2, SEGS:] = high
    totals[2:4, SEGS:] = counts - high


def send_parts(message, keep, aux, sums, totals, have, bit):
    split_counts(aux, totals)
    message[0:SUM_ROWS, :] = sums.astype(BF16)
    message[SUM_ROWS : SUM_ROWS + AUX_ROWS, :] = totals[...].astype(BF16)
    message[SUM_ROWS + AUX_ROWS :, :] = picked(have, 1 - bit)
    keep[...] = picked(have, bit)


def time_bit(b):
    return lax.div(lax.axis_index("tm"), 1 << b) % 2


def first_kernel(mine, got, placing, weighted, aux, message, sums, totals, keep):
    core = time_bit(0)
    rounded = (mine[...] + got[...].astype(F32)).astype(BF16)
    have = jnp.dot(placing[...], rounded, preferred_element_type=F32).astype(BF16)
    kept = weighted[pl.ds(pl.multiple_of(core * SUM_ROWS, SUM_ROWS), SUM_ROWS), :]
    sent = weighted[pl.ds(pl.multiple_of((1 - core) * SUM_ROWS, SUM_ROWS), SUM_ROWS), :]
    sums[...] = jnp.dot(kept, rounded, preferred_element_type=F32)
    sent = jnp.dot(sent, rounded, preferred_element_type=F32)
    send_parts(message, keep, aux[...], sent, totals, have, core)


def merged(bit, arrived, sums, totals, keep, have):
    have[pl.ds(pl.multiple_of(bit * 64, 64), 64), :] = keep[...]
    have[pl.ds(pl.multiple_of((1 - bit) * 64, 64), 64), :] = arrived[SUM_ROWS + AUX_ROWS :, :]
    total = sums[...] + arrived[0:SUM_ROWS, :].astype(F32)
    aux = totals[...] + arrived[SUM_ROWS : SUM_ROWS + AUX_ROWS, :].astype(F32)
    return total, aux


QUARTER = SUM_ROWS + AUX_ROWS + 32


def time_pair():
    return lax.div(lax.axis_index("tm"), 2) % 4


def picked_quarter(have, value):
    rows, columns = iota((32, SEGS), 0), iota((32, SEGS), 1)
    chosen = columns == (rows // 8) * 32 + value * 8 + rows % 8
    return jnp.dot(to_bf16(chosen), have, preferred_element_type=F32).astype(BF16)


def spread_kernel(arrived, sums, totals, keep, *rest):
    *messages, sums_out, totals_out, keep_out, have = rest
    total, aux = merged(time_bit(0), arrived, sums, totals, keep, have)
    sums_out[...] = total
    split_counts(aux, totals_out)
    total = total.astype(BF16)
    aux = totals_out[...].astype(BF16)
    pair = time_pair()
    held = have[...]
    for n, message in enumerate(messages):
        message[0:SUM_ROWS, :] = total
        message[SUM_ROWS : SUM_ROWS + AUX_ROWS, :] = aux
        message[SUM_ROWS + AUX_ROWS :, :] = picked_quarter(held, pair ^ (n + 1))
    keep_out[...] = picked_quarter(held, pair)


def gather_kernel(after, *rest):
    *arrived, sums, totals, keep, message, sums_out, totals_out, keep_out, have = rest
    pair = time_pair()
    have[pl.ds(pl.multiple_of(pair * 32, 32), 32), :] = keep[...]
    total, aux = sums[...], totals[...]
    for n, part in enumerate(arrived):
        place = pl.ds(pl.multiple_of((pair ^ (n + 1)) * 32, 32), 32)
        have[place, :] = part[SUM_ROWS + AUX_ROWS :, :]
        total = total + part[0:SUM_ROWS, :].astype(F32)
        aux = aux + part[SUM_ROWS : SUM_ROWS + AUX_ROWS, :].astype(F32)
    sums_out[...] = total
    send_parts(message, keep_out, aux, total, totals_out, have[...], time_bit(3))


def last_kernel(after, arrived, sums, totals, keep, calibration, table, have):
    total, aux = merged(time_bit(3), arrived, sums, totals, keep, have)
    table[...] = aux
    both = aux[0:2, SEGS:] + aux[2:4, SEGS:]
    counts = jnp.where(time_bit(0) == 0, both[0:1, :], both[1:2, :])
    calibration[...] = (total / (as_column(counts) + 1.0)).astype(BF16)


def near_kernel(mine, table, have, near_scores, far):
    named = jnp.where(iota((AUX_ROWS, SEGS), 0) == lax.axis_index("tm"), table[:, 0:SEGS], 0.0)
    row = jnp.sum(named, axis=0, keepdims=True).astype(jnp.int32)
    column = as_column(row)
    ids = iota((SEGS, SUM_ROWS), 1) + 1
    core = time_bit(0)
    near = to_bf16(column == ids + core * SUM_ROWS)
    far[...] = to_bf16(column == ids + (1 - core) * SUM_ROWS)
    near_scores[...] = have[...].astype(F32) - jnp.dot(near, mine[...], preferred_element_type=F32)


def scores_kernel(theirs, near_scores, far, scores):
    scores[...] = near_scores[...] - jnp.dot(far[...], theirs[...], preferred_element_type=F32)


def small_call(kernel, name, operands, outs, scratch=(), hbm=0):
    return pl.pallas_call(
        kernel,
        in_specs=[ANY_SPEC] * hbm + [VMEM_SPEC] * (len(operands) - hbm),
        out_specs=[VMEM_SPEC] * len(outs),
        out_shape=[jax.ShapeDtypeStruct(*o) for o in outs],
        scratch_shapes=list(scratch),
        compiler_params=SMALL,
        cost_estimate=cost(1 << 24, 1 << 20),
        name=name,
    )(*operands)


def fast_tail(mine, got, act_rest, owners, silence, tags, block_out):
    classes = mine.shape[1]
    sums = ((SUM_ROWS, classes), F32)
    aux = ((AUX_ROWS, 2 * SEGS), F32)
    keep = ((64, classes), BF16)
    message = ((MESSAGE, classes), BF16)
    have = (pltpu.VMEM((SEGS, classes), BF16),)
    placing, weighted, labels = small_call(
        labels_kernel,
        "labels",
        [mine, owners[:, 0][None, :], silence, tags],
        [((SEGS, SEGS), BF16), ((TAGS, SEGS), BF16), aux],
    )
    act_rest, got, placing = lax.optimization_barrier((act_rest, got, placing))
    got_rest = swap(act_rest, "grp", 1)
    state = small_call(
        first_kernel, "first", [mine, got, placing, weighted, labels], [message, sums, aux, keep]
    )
    arrived = swap(state[0], "tm", 1)
    quarter = ((QUARTER, classes), BF16)
    *spread, part_sums, part_totals, part_keep = small_call(
        spread_kernel,
        "spread",
        [arrived, *state[1:]],
        [quarter, quarter, quarter, sums, aux, ((32, classes), BF16)],
        have,
    )
    arrived = [swap(part, "tm", 2 * (n + 1)) for n, part in enumerate(spread)]
    rows = block_out.first()
    state = small_call(
        gather_kernel,
        "gather",
        [in_hbm(rows), *arrived, part_sums, part_totals, part_keep],
        [message, sums, aux, keep],
        have,
        hbm=1,
    )
    partial = block_out.partial(state[1])
    arrived = swap(state[0], "tm", 8)
    block_rows = block_out.rest(partial, got_rest, rows)
    calibration, table, ready = small_call(
        last_kernel,
        "last",
        [in_hbm(block_rows), arrived, *state[1:]],
        [((SUM_ROWS, classes), BF16), aux, ((SEGS, classes), BF16)],
        hbm=1,
    )
    theirs = swap(calibration, "tm", 1)
    near_scores, far = small_call(
        near_kernel,
        "near",
        [calibration, table, ready],
        [((SEGS, classes), F32), ((SEGS, SUM_ROWS), BF16)],
    )
    [scores] = small_call(
        scores_kernel, "scores", [theirs, near_scores, far], [((SEGS, classes), F32)]
    )
    return block_rows, scores


def fast_body(
    frames,
    ln_gain,
    w_value,
    w_gate,
    conv_taps,
    bn_scale,
    bn_shift,
    w_out,
    w_classes,
    seg_lengths,
    owners,
    silence,
    tags,
):
    count = frames.shape[0]
    time_size = lax.axis_size("tm")
    own_rows = count // 2
    glu = run_fast_glu(frames, ln_gain, w_value, w_gate)
    odd = lax.axis_index("tm") % 2 == 1
    first, last = glu[:HALO], glu[count - HALO :]
    across = [(i, i + 1) for i in range(1, time_size - 1, 2)]
    across += [(j, i) for i, j in across]
    near = swap(jnp.where(odd, first, last), "tm", 1)
    far = lax.ppermute(jnp.where(odd, last, first), "tm", across)
    bn = (conv_taps, bn_scale, bn_shift, seg_lengths)
    act_first, pooled = run_early(FIRST, glu, *bn)
    got_first = swap(act_first, "grp", 1)
    act_rest, act_own, mine, sent = run_late(
        glu, near, far, *bn, pooled, frames, w_out, w_classes
    )
    sent, got_first = lax.optimization_barrier((sent, got_first))
    got = swap(sent, "grp", 1)

    class block_out:
        def first():
            return run_out_first(frames, act_own, got_first, w_out)

        def partial(after):
            return run_out_partial(after, frames, act_own, w_out)

        def rest(partial, got_rest, rows):
            return run_out_rest(partial, got_rest, w_out, rows)

    block_rows, scores = fast_tail(mine, got, act_rest, owners, silence, tags, block_out)
    return (block_rows[None, None], scores)


def body(*args):
    rows = args[0].shape[0] // lax.axis_size("grp")
    channels = args[2].shape[1]
    fits = rows == 3 * BLOCK and channels % BLOCK == 0
    fits = fits and lax.axis_size("grp") == 2 and lax.axis_size("tm") == 16
    fits = fits and args[4].shape[0] == 31 and args[8].shape[1] == 512 and args[9].shape[1] == SEGS
    return (fast_body if fits else general_body)(*args)


def solution(mesh):
    in_specs = (
        P("tm", None),
        P(),
        P(None, "grp"),
        P(None, "grp"),
        P(None, "grp"),
        P("grp"),
        P("grp"),
        P(),
        P(),
        P("tm", None),
        P("tm", None),
        P("tm", None),
        P("tm", None),
    )
    out_specs = (P("tm", "grp", None, None), P("tm", "grp"))
    return jax.shard_map(body, mesh=mesh, in_specs=in_specs, out_specs=out_specs, check_vma=False)
```
